32 devices in a mesh: dp: 8 (over z, y), tensor: 4 (over x, core).
Axes of the slice: x: 2, y: 2, z: 4, core: 2. Of those that a mesh axis runs over, the one named last changes fastest.
Arguments:
- tokens: bfloat16 [8192, 2048], P(('dp', 'tensor')), may hold values from -6 to 6
- prefix: int32 [8], P('dp'), may hold values from 102 to 512
- query_weight: bfloat16 [2048, 2048], P('dp', 'tensor'), may hold values from -0.125 to 0.125
- key_weight: bfloat16 [2048, 2048], P('dp', 'tensor'), may hold values from -0.25 to 0.25
- value_weight: bfloat16 [2048, 2048], P('dp', 'tensor'), may hold values from -0.125 to 0.125
- out_weight: bfloat16 [2048, 2048], P('tensor', 'dp'), may hold values from -1 to 1
- query_bias: bfloat16 [16, 128], P('tensor', 'dp'), may hold values from -1.75 to 1.75
- value_bias: bfloat16 [16, 128], P('tensor', 'dp'), may hold values from -1.75 to 1.75
- up_weight: bfloat16 [2048, 8192], P('dp', 'tensor'), may hold values from -0.125 to 0.125
- down_weight: bfloat16 [8192, 2048], P('tensor', 'dp'), may hold values from -0.0625 to 0.0625
- up_bias: bfloat16 [64, 128], P('tensor', 'dp'), may hold values from -3 to 3
- norm1_gain: bfloat16 [2048], P('dp'), may hold values from 0.5 to 1.5
- norm1_bias: bfloat16 [2048], P('dp'), may hold values from -1.75 to 1.75
- norm2_gain: bfloat16 [2048], P('dp'), may hold values from 0.5 to 1.5
- norm2_bias: bfloat16 [2048], P('dp'), may hold values from -1.75 to 1.75
- out_bias: bfloat16 [2048], P('dp'), may hold values from -1.75 to 1.75
- down_bias: bfloat16 [2048], P('dp'), may hold values from -1.75 to 1.75
- cotangent: bfloat16 [8192, 2048], P(('dp', 'tensor')), may hold values from -12 to 12
Outputs:
- layer_out: bfloat16 [8192, 2048], P(('dp', 'tensor'))
- input_grad: float32 [8192, 2048], P(('dp', 'tensor'))
- query_weight_grad: float32 [2048, 2048], P('dp', 'tensor')
- key_weight_grad: float32 [2048, 2048], P('dp', 'tensor')
- value_weight_grad: float32 [2048, 2048], P('dp', 'tensor')
- out_weight_grad: float32 [2048, 2048], P('tensor', 'dp')
- query_bias_grad: float32 [16, 128], P('tensor', 'dp')
- value_bias_grad: float32 [16, 128], P('tensor', 'dp')
- up_weight_grad: float32 [2048, 8192], P('dp', 'tensor')
- down_weight_grad: float32 [8192, 2048], P('tensor', 'dp')
- up_bias_grad: float32 [64, 128], P('tensor', 'dp')
- norm1_gain_grad: float32 [2048], P(('dp', 'tensor'))
- norm1_bias_grad: float32 [2048], P(('dp', 'tensor'))
- norm2_gain_grad: float32 [2048], P(('dp', 'tensor'))
- norm2_bias_grad: float32 [2048], P(('dp', 'tensor'))
- out_bias_grad: float32 [2048], P(('dp', 'tensor'))
- down_bias_grad: float32 [2048], P(('dp', 'tensor'))
The draws below stay inside these ranges and needn't reach their ends.
Inputs may be any that keep to these rules, and one draw needn't show every extreme that they name: Token j of a sequence is seen by token i when j <= i or j lies in the sequence's first prefix tokens.
All inputs are finite; a program needn't handle non-finite values.
Results may differ from the reference program's by a relative error of at most 0.012.
The reference program's roundings to bfloat16 on the way count: a program that leaves them out, or rounds other values in their place, can miss the bound.
Values may be sent and summed in bfloat16 or wider, within the bound.
A program may use at most 192 MiB of HBM per device.

```python
import jax
import jax.numpy as jnp
from jax import lax

D = 2048
HEADS = 16
HEAD_DIM = 128
FF = 8192
SEQ_LEN = 1024
SEQS = 8
TOKENS = 8192


def set_ends(drawn, stream_key, smallest, top_value):
    extent = drawn.shape
    place = [jax.random.randint(jax.random.fold_in(stream_key, axis), (), 0, extent[axis]) for axis in range(len(extent))]
    drawn = drawn.at[tuple(place)].set(smallest)
    longest = extent.index(max(extent))
    place[longest] = (place[longest] + 1) % extent[longest]
    return drawn.at[tuple(place)].set(top_value)


def raised(array, key, source, target, shards_of, factor):
    owner, partner = [(jnp.arange(array.shape[position]) // (array.shape[position] // shards_of)).reshape([-1 if axis == position else 1 for axis in range(array.ndim)]) for position in (source, target)]
    chosen = jax.random.permutation(key, shards_of)[partner]
    strong = (owner == chosen) | (owner == (partner + shards_of // 2) % shards_of)
    return jnp.where(strong, factor * array, array)


def steps_of(stream_key, dims, cuts, low, high):
    factor_of = 1.0
    for position, parts in cuts:
        steps = jax.random.uniform(jax.random.fold_in(jax.random.fold_in(stream_key, 6), position), (parts,), jnp.float32, low / len(cuts), high / len(cuts))
        factor_of = factor_of * jnp.repeat(jnp.exp(steps), dims[position] // parts).reshape((-1,) + (1,) * (len(dims) - 1 - position))
    return factor_of


def noise(key, extent, deviation, bound, cuts=(), kind=jnp.bfloat16):
    values = jax.random.normal(key, extent, jnp.float32) * deviation
    if len(cuts) > 0:
        values = steps_of(key, extent, cuts, -0.22, 0.18) * values
    return jnp.clip(values, min=-bound, max=bound).astype(kind)


def heavy_noise(stream_key, dims, width, reach, pieces, heavy, held_as=jnp.bfloat16):
    values = width * jax.random.normal(stream_key, dims, jnp.float32)
    if pieces:
        values = values * steps_of(stream_key, dims, pieces, -0.22, 0.18)
    return jnp.clip(raised(values, jax.random.fold_in(stream_key, 3), *heavy), -reach, reach).astype(held_as)


def setup_inputs(seed: int = 0) -> dict:
    seeds = jax.random.split(jax.random.key(seed), 19)
    tokens = noise(seeds[0], (TOKENS, D), 1.0, 6.0, ((0, 32),))
    prefix = set_ends(jax.random.randint(seeds[1], (SEQS,), SEQ_LEN // 10, SEQ_LEN // 2 + 1), jax.random.fold_in(seeds[1], 1), SEQ_LEN // 10, (SEQ_LEN // 2 + 1) - 1).astype(jnp.int32)
    query_weight = noise(seeds[2], (D, D), D ** -0.5, 0.125, ((0, 8), (1, 4)))
    key_weight = noise(seeds[3], (D, D), (D // 4) ** -0.5, 0.25, ((0, 8), (1, 4)))
    value_weight = noise(seeds[4], (D, D), D ** -0.5, 0.125, ((0, 8), (1, 4)))
    out_weight = noise(seeds[5], (D, D), (D // 64) ** -0.5, 1.0, ((0, 4), (1, 8)))
    query_bias = noise(seeds[6], (HEADS, HEAD_DIM), 0.3, 1.75, ((0, 4), (1, 8)))
    value_bias = noise(seeds[7], (HEADS, HEAD_DIM), 0.3, 1.75, ((0, 4), (1, 8)))
    up_weight = noise(seeds[8], (D, FF), D ** -0.5, 0.125, ((0, 8), (1, 4)))
    down_weight = noise(seeds[9], (FF, D), FF ** -0.5, 0.0625, ((0, 4), (1, 8)))
    up_bias = noise(seeds[10], (FF // 128, 128), 0.5, 3.0, ((0, 4), (1, 8)))
    norm1_gain = jnp.clip(1.0 + 0.1 * jax.random.normal(seeds[11], (D,), jnp.float32), 0.5, 1.5).astype(jnp.bfloat16)
    norm1_bias = noise(seeds[12], (D,), 0.3, 1.75, ((0, 8),))
    norm2_gain = jnp.clip(1.0 + 0.1 * jax.random.normal(seeds[13], (D,), jnp.float32), 0.5, 1.5).astype(jnp.bfloat16)
    norm2_bias = noise(seeds[14], (D,), 0.3, 1.75, ((0, 8),))
    out_bias = noise(seeds[15], (D,), 0.3, 1.75, ((0, 8),))
    down_bias = noise(seeds[16], (D,), 0.3, 1.75, ((0, 8),))
    cotangent = heavy_noise(seeds[17], (TOKENS, D), 1.0, 12.0, ((0, 32),), (0, 1, 32, 2.75))
    return {"tokens": tokens, "prefix": prefix, "query_weight": query_weight, "key_weight": key_weight, "value_weight": value_weight, "out_weight": out_weight, "query_bias": query_bias, "value_bias": value_bias, "up_weight": up_weight, "down_weight": down_weight, "up_bias": up_bias, "norm1_gain": norm1_gain, "norm1_bias": norm1_bias, "norm2_gain": norm2_gain, "norm2_bias": norm2_bias, "out_bias": out_bias, "down_bias": down_bias, "cotangent": cotangent}


@jax.custom_vjp
def low(v):
    return lax.optimization_barrier(v.astype(jnp.bfloat16)).astype(jnp.float32)

@jax.custom_vjp
def low_back(v):
    return v

def low_keep(v):
    return (low(v), None)

def low_pass(kept, grad):
    return (grad,)

def back_keep(v):
    return (v, None)

def back_low(kept, grad):
    return (low(grad),)
low.defvjp(low_keep, low_pass)
low_back.defvjp(back_keep, back_low)

def layer_norm(rows, gain, shift):
    center = rows - lax.optimization_barrier(jnp.mean(rows, axis=-1, keepdims=True))
    spread = lax.optimization_barrier(jnp.mean(center * center, axis=-1, keepdims=True))
    return center * lax.rsqrt(spread + 1e-05) * gain + shift

def gelu_exact(values):
    return jax.nn.gelu(values, approximate=False)

def matmul(left, right):
    return jnp.dot(left, right, precision=lax.Precision.HIGHEST, preferred_element_type=jnp.float32)

def attend(item, keys, values, prefix_len):
    q_block, start = item
    scores = jnp.einsum('hqd,hkd->hqk', q_block, keys, precision=lax.Precision.HIGHEST)
    scores = low_back(scores)
    rows = start + lax.broadcasted_iota(jnp.int32, scores.shape[1:], 0)
    cols = lax.broadcasted_iota(jnp.int32, scores.shape[1:], 1)
    seen = (cols <= rows) | (cols < prefix_len)
    scores = jnp.where(seen[None], scores, -1e+30)
    probs = jax.nn.softmax(scores, axis=-1)
    return jnp.einsum('hqk,hkd->hqd', low(probs), values, precision=lax.Precision.HIGHEST)

def one_sequence(rows, params, prefix_len):
    wq, wk, wv, wo, bq, bv, w1, w2, b1, g1, n1, g2, n2, bo, b2 = params
    length = rows.shape[0]
    block = min(512, length)
    count = length // block
    scale = HEAD_DIM ** (-0.5)
    h1 = low(layer_norm(rows, g1, n1))
    query = low((low_back(matmul(h1, wq)) + bq.reshape(-1)) * scale)
    keyed = low(low_back(matmul(h1, wk)))
    valued = low(low_back(matmul(h1, wv)) + bv.reshape(-1))
    q_heads = query.reshape(length, HEADS, HEAD_DIM).transpose(1, 0, 2)
    k_heads = keyed.reshape(length, HEADS, HEAD_DIM).transpose(1, 0, 2)
    v_heads = valued.reshape(length, HEADS, HEAD_DIM).transpose(1, 0, 2)
    q_blocks = q_heads.reshape(HEADS, count, block, HEAD_DIM).transpose(1, 0, 2, 3)
    starts = jnp.arange(count, dtype=jnp.int32) * block
    block_fn = jax.checkpoint(lambda item: attend(item, k_heads, v_heads, prefix_len))
    outs = lax.map(block_fn, (q_blocks, starts))
    mixed = outs.transpose(1, 0, 2, 3).reshape(HEADS, length, HEAD_DIM)
    mixed = mixed.transpose(1, 0, 2).reshape(length, HEADS * HEAD_DIM)
    attn_in = low_back(low(mixed))
    second = rows + low_back(matmul(attn_in, wo)) + bo
    h2 = low(layer_norm(second, g2, n2))
    hidden = low_back(matmul(h2, w1)) + b1.reshape(-1)
    gated = low(gelu_exact(hidden))
    return second + low_back(matmul(gated, w2)) + b2

def reference(tokens, prefix, query_weight, key_weight, value_weight, out_weight, query_bias, value_bias, up_weight, down_weight, up_bias, norm1_gain, norm1_bias, norm2_gain, norm2_bias, out_bias, down_bias, cotangent):
    params = tuple((p.astype(jnp.float32) for p in (query_weight, key_weight, value_weight, out_weight, query_bias, value_bias, up_weight, down_weight, up_bias, norm1_gain, norm1_bias, norm2_gain, norm2_bias, out_bias, down_bias)))
    inputs = tokens.astype(jnp.float32).reshape(SEQS, SEQ_LEN, D)
    cotans = cotangent.astype(jnp.float32).reshape(SEQS, SEQ_LEN, D)

    def step(carry, item):
        rows, cot, prefix_len = item
        result, back = jax.vjp(lambda xx, pp: one_sequence(xx, pp, prefix_len), rows, params)
        d_rows, d_params = back(cot)
        carry = jax.tree.map(jnp.add, carry, d_params)
        return (carry, (result.astype(jnp.bfloat16), d_rows))
    zeros = jax.tree.map(jnp.zeros_like, params)
    grads, (results, d_inputs) = lax.scan(step, zeros, (inputs, cotans, prefix.astype(jnp.int32)))
    gwq, gwk, gwv, gwo, gbq, gbv, gw1, gw2, gb1, gg1, gn1, gg2, gn2, gbo, gb2 = grads
    return (results.reshape(TOKENS, D), d_inputs.reshape(TOKENS, D), gwq, gwk, gwv, gwo, gbq, gbv, gw1, gw2, gb1, gg1, gn1, gg2, gn2, gbo, gb2)
```

```python
import functools

import jax
import jax.numpy as jnp
from jax import lax
from jax.experimental import pallas as pl
from jax.experimental.pallas import tpu as pltpu
from jax.sharding import PartitionSpec as P

MESH = pl.DeviceIdType.MESH
F32 = jnp.float32
BF16 = jnp.bfloat16
PREFIX_TOP = 512
VMEM_BYTES = 67043328


def split_of(count):
    inner = 1
    for size in range(1, count + 1):
        if size * size <= count and count % size == 0:
            inner = size
    return count // inner, inner


def remote(source, target, send_sem, recv_sem, dp, tensor):
    return pltpu.make_async_remote_copy(
        src_ref=source,
        dst_ref=target,
        send_sem=send_sem,
        recv_sem=recv_sem,
        device_id=(dp, tensor),
        device_id_type=MESH,
    )


def block_of(index, size):
    return pl.ds(pl.multiple_of(index * size, size), size)


class Spot:
    def __init__(self, count):
        self.outer, self.inner = split_of(count)
        self.count = count
        self.dp = lax.axis_index("dp")
        self.tensor = lax.axis_index("tensor")
        self.row = lax.div(self.dp, self.inner)
        self.column = lax.rem(self.dp, self.inner)
        self.core_peer = self.tensor + 1 - 2 * lax.rem(self.tensor, 2)
        self.x_peer = lax.rem(self.tensor + 2, 4)
        self.far_peer = lax.rem(self.core_peer + 2, 4)

    def across(self, step):
        return lax.rem(self.row + step, self.outer) * self.inner + self.column

    def beside(self, step, row=None):
        return (self.row if row is None else row) * self.inner + lax.rem(self.column + step, self.inner)

    def meet(self):
        barrier = pltpu.get_barrier_semaphore()
        for step in range(1, self.count):
            pl.semaphore_signal(
                barrier, inc=1, device_id=(lax.rem(self.dp + step, self.count), self.tensor), device_id_type=MESH
            )
        for peer in (self.core_peer, self.x_peer):
            pl.semaphore_signal(barrier, inc=1, device_id=(self.dp, peer), device_id_type=MESH)
        pl.semaphore_wait(barrier, self.count + 1)


class Spread:
    def __init__(self, spot, pieces, z_send, z_recv, y_send, y_recv):
        self.spot, self.pieces = spot, pieces
        self.sems = (z_send, z_recv, y_send, y_recv)
        self.sent = []
        self.todo = [(piece, step) for piece in range(len(pieces)) for step in range(1, spot.outer)]
        self.own_next = 0

    def send_rows(self, piece):
        source, target = self.pieces[piece]
        for step in range(1, self.spot.outer):
            copy = remote(
                source, target(self.spot.dp), self.sems[0].at[piece, step], self.sems[1].at[piece, step],
                self.spot.across(step), self.spot.tensor,
            )
            copy.start()
            self.sent.append(copy)

    def y_copies(self, piece, step):
        spot = self.spot
        source, target = self.pieces[piece]
        owner = spot.across(spot.outer - step) if step else spot.dp
        if step:
            source = target(owner)
        copies = []
        for side in range(1, spot.inner):
            copies.append(remote(
                source, target(owner), self.sems[2].at[piece, step, side], self.sems[3].at[piece, step, side],
                spot.beside(side), spot.tensor,
            ))
        return copies

    def send_own(self, upto):
        while self.own_next < min(upto, len(self.pieces)):
            for copy in self.y_copies(self.own_next, 0):
                copy.start()
                self.sent.append(copy)
            self.own_next += 1

    def forward(self, count):
        for _ in range(count):
            if not self.todo:
                return
            piece, step = self.todo.pop(0)
            source, target = self.pieces[piece]
            remote(
                source, target(self.spot.across(self.spot.outer - step)), self.sems[0].at[piece, step],
                self.sems[1].at[piece, step], self.spot.across(step), self.spot.tensor,
            ).wait_recv()
            for copy in self.y_copies(piece, step):
                copy.start()
                self.sent.append(copy)
            if step == self.spot.outer - 1:
                self.send_own(piece + 4)

    def arrived(self, piece):
        while self.todo and self.todo[0][0] <= piece:
            self.forward(1)
        for step in range(self.spot.outer):
            for copy in self.y_copies(piece, step):
                copy.wait_recv()

    def finish(self):
        for copy in self.sent:
            copy.wait_send()


class TensorGather:
    def __init__(self, spot, own, full, rows, send, recv):
        self.spot, self.full, self.rows, self.send, self.recv = spot, full, rows, send, recv
        place = self.at(spot.tensor)
        self.to_x = remote(own, place, send.at[0], recv.at[0], spot.dp, spot.x_peer)
        self.to_core = remote(own, place, send.at[1], recv.at[1], spot.dp, spot.core_peer)
        self.to_x.start()
        self.to_core.start()

    def at(self, index):
        return self.full.at[block_of(index, self.rows)]

    def pass_on(self):
        self.to_x.wait_recv()
        place = self.at(self.spot.x_peer)
        self.on = remote(place, place, self.send.at[2], self.recv.at[2], self.spot.dp, self.spot.core_peer)
        self.on.start()

    def finish(self):
        self.to_core.wait_recv()
        self.on.wait_recv()
        for copy in (self.to_x, self.to_core, self.on):
            copy.wait_send()


def tensor_sum(spot, product, core_send, core_recv, x_send, x_recv, send, recv, finish):
    width = core_send.shape[2]
    chunk = 512
    count = width // chunk

    def fill(rank, target):
        def body(index, carry):
            target[:, block_of(index, chunk)] = product(rank, index).astype(BF16)
            return carry

        lax.fori_loop(0, count, body, 0)

    copies = []
    for slot, rank in enumerate((spot.far_peer, spot.core_peer)):
        fill(rank, core_send.at[slot])
        copy = remote(core_send.at[slot], core_recv.at[slot], send.at[slot], recv.at[slot], spot.dp, spot.core_peer)
        copy.start()
        copies.append(copy)
    copies[0].wait_recv()

    def join(index, carry):
        where = block_of(index, chunk)
        x_send[:, where] = (product(spot.x_peer, index) + core_recv[0, :, where].astype(F32)).astype(BF16)
        return carry

    lax.fori_loop(0, count, join, 0)
    over = remote(x_send, x_recv, send.at[2], recv.at[2], spot.dp, spot.x_peer)
    over.start()
    copies[1].wait_recv()

    def end():
        over.wait_recv()

        def last(index, carry):
            where = block_of(index, chunk)
            total = product(spot.tensor, index) + core_recv[1, :, where].astype(F32) + x_recv[:, where].astype(F32)
            finish(index, total)
            return carry

        lax.fori_loop(0, count, last, 0)
        for copy in copies + [over]:
            copy.wait_send()

    return end


def normal_parts(rows):
    center = rows - jnp.mean(rows, axis=-1, keepdims=True)
    spread = jnp.mean(center * center, axis=-1, keepdims=True)
    return center, lax.rsqrt(spread + 1e-05)


def forward_kernel(
    heads,
    count,
    prefix,
    tokens,
    cotangent,
    small,
    qkv_shard,
    out_shard,
    up_shard,
    down_shard,
    wqkv,
    wo,
    w1,
    w2,
    h1_all,
    d_rows,
    qkv_all,
    mixed_all,
    lse_all,
    second,
    h2_all,
    gated_all,
    slope_all,
    sums,
    smalls,
    h1v,
    wqkv_v,
    qkv_v,
    mixed_v,
    lse_v,
    wo_v,
    core_send,
    core_recv,
    x_send,
    x_recv,
    h2v,
    w1_v,
    gated_v,
    slope_v,
    small_send,
    small_recv,
    z_send,
    z_recv,
    y_send,
    y_recv,
    g_send,
    g_recv,
    s_send,
    s_recv,
    local_sem,
):
    spot = Spot(count)
    rows, features = tokens.shape
    length = h1v.shape[0]
    depth = qkv_shard.shape[0]
    width = wo_v.shape[0]
    hidden = up_shard.shape[1]
    half = depth // 2
    tall = hidden // 2
    pieces = [
        (qkv_shard.at[pl.ds(part * half, half)],
         lambda owner, part=part: wqkv.at[block_of(owner * 2 + part, half)])
        for part in range(2)
    ]
    pieces.append((out_shard, lambda owner: wo.at[:, block_of(owner, depth)]))
    pieces += [
        (up_shard.at[pl.ds(part * half, half)],
         lambda owner, part=part: w1.at[block_of(owner * 2 + part, half)])
        for part in range(2)
    ]
    pieces += [
        (down_shard.at[pl.ds(part * tall, tall)],
         lambda owner, part=part: w2.at[pl.ds(part * tall, tall), block_of(owner, depth)])
        for part in range(2)
    ]
    spread = Spread(spot, pieces, z_send, z_recv, y_send, y_recv)
    locals_ = []

    def keep(source, target):
        copy = pltpu.make_async_copy(source, target, local_sem.at[len(locals_)])
        copy.start()
        locals_.append(copy)

    spot.meet()
    small_copies = []
    for step in range(1, count):
        copy = remote(
            small, smalls.at[spot.dp], small_send.at[step], small_recv.at[step],
            lax.rem(spot.dp + step, count), spot.tensor,
        )
        copy.start()
        small_copies.append(copy)
    for piece in range(len(pieces)):
        spread.send_rows(piece)
    spread.send_own(4)
    for source, target in pieces:
        keep(source, target(spot.dp))
    smalls[spot.dp] = small[...]
    for step, copy in enumerate(small_copies):
        remote(
            small, smalls.at[lax.rem(spot.dp + count - step - 1, count)], small_send.at[step + 1],
            small_recv.at[step + 1], spot.dp, spot.core_peer,
        ).wait_recv()
    total = smalls[0]
    for index in range(1, count):
        total = total + smalls[index]
    sums[...] = total

    strip = 32
    base = spot.tensor * rows

    def norm1(index, carry):
        where = block_of(index, strip)
        center, scale = normal_parts(tokens[where, :].astype(F32))
        h1v[pl.ds(pl.multiple_of(base + index * strip, strip), strip), :] = (
            center * scale * sums[0:1, :] + sums[1:2, :]
        ).astype(BF16)
        return carry

    lax.fori_loop(0, rows // strip, norm1, 0)
    gather1 = TensorGather(spot, h1v.at[block_of(spot.tensor, rows)], h1v, rows, g_send.at[0], g_recv.at[0])
    gather_d = TensorGather(spot, cotangent, d_rows, rows, g_send.at[1], g_recv.at[1])
    keep(cotangent, d_rows.at[block_of(spot.tensor, rows)])
    spread.forward(spot.outer - 1)
    gather1.pass_on()
    spread.forward(spot.outer - 1)
    gather1.finish()
    keep(h1v, h1_all)
    gather_d.pass_on()
    spread.arrived(0)
    spread.arrived(1)
    for copy in locals_[:2]:
        copy.wait()
    load = pltpu.make_async_copy(wqkv, wqkv_v, local_sem.at[14])
    load.start()
    spread.forward(1)
    load.wait()

    def project(index, carry):
        where = block_of(index, rows)
        for part in range(3):
            lanes = slice(part * width, (part + 1) * width)
            value = jnp.dot(h1v[where, :], wqkv_v[:, lanes], preferred_element_type=F32) + sums[6:7, lanes]
            if part == 0:
                value = value * (width // heads) ** -0.5
            qkv_v[where, lanes] = value.astype(BF16)
        return carry

    lax.fori_loop(0, length // rows, project, 0)
    keep(qkv_v, qkv_all)
    spread.forward(2)
    size = width // heads
    limit = prefix[0]
    bench = 256

    for block in range(length // bench):
        reach = min(length, max((block + 1) * bench, PREFIX_TOP))
        span = slice(block * bench, (block + 1) * bench)

        def attend(head, carry, block=block, span=span, reach=reach):
            line = block * bench + lax.broadcasted_iota(jnp.int32, (bench, reach), 0)
            place = lax.broadcasted_iota(jnp.int32, (bench, reach), 1)
            seen = (place <= line) | (place < limit)
            q = qkv_v[span, block_of(head, size)]
            k = qkv_v[0:reach, pl.ds(pl.multiple_of(width + head * size, size), size)]
            v = qkv_v[0:reach, pl.ds(pl.multiple_of(2 * width + head * size, size), size)]
            scores = lax.dot_general(q, k, (((1,), (1,)), ((), ())), preferred_element_type=F32)
            scores = jnp.where(seen, scores, -1e30)
            top = jnp.max(scores, axis=-1, keepdims=True)
            expd = jnp.exp(scores - top)
            total = jnp.sum(expd, axis=-1, keepdims=True)
            probs = (expd * (1.0 / total)).astype(BF16)
            mixed_v[span, block_of(head, size)] = jnp.dot(probs, v, preferred_element_type=F32).astype(BF16)
            lse_v[head, span, :] = jnp.broadcast_to(top + jnp.log(total), (bench, 128))
            return carry

        lax.fori_loop(0, heads, attend, 0)
        if block % 2 == 1:
            spread.forward(1)
    keep(mixed_v, mixed_all)
    keep(lse_v, lse_all)
    spread.arrived(2)
    locals_[2].wait()
    load = pltpu.make_async_copy(wo, wo_v, local_sem.at[14])
    load.start()
    load.wait()

    def out_part(rank, index):
        return jnp.dot(mixed_v[block_of(rank, rows), :], wo_v[:, block_of(index, 512)], preferred_element_type=F32)

    def take_second(index, total):
        where = block_of(index, 512)
        second[:, where] = tokens[:, where].astype(F32) + total + sums[4:5, where]

    end = tensor_sum(
        spot, out_part, core_send, core_recv, x_send, x_recv, s_send.at[0], s_recv.at[0], take_second
    )
    spread.forward(spot.outer - 1)
    end()

    def norm2(index, carry):
        where = block_of(index, strip)
        center, scale = normal_parts(second[where, :])
        h2v[pl.ds(pl.multiple_of(base + index * strip, strip), strip), :] = (
            center * scale * sums[2:3, :] + sums[3:4, :]
        ).astype(BF16)
        return carry

    lax.fori_loop(0, rows // strip, norm2, 0)
    gather2 = TensorGather(spot, h2v.at[block_of(spot.tensor, rows)], h2v, rows, g_send.at[2], g_recv.at[2])
    spread.forward(spot.outer - 1)
    gather2.pass_on()
    gather2.finish()
    gather_d.finish()
    keep(h2v, h2_all)
    spread.arrived(3)
    spread.arrived(4)
    for copy in locals_[3:5]:
        copy.wait()
    load = pltpu.make_async_copy(w1, w1_v, local_sem.at[14])
    load.start()
    spread.forward(1)
    load.wait()
    stored = []
    for block in range(length // rows):
        slot = block % 2
        if block >= 2:
            stored[block - 2].wait()

        def lift(index, carry, block=block, slot=slot):
            where = block_of(index, 512)
            u = jnp.dot(
                h2v[block * rows : (block + 1) * rows, :], w1_v[:, where], preferred_element_type=F32
            ) + sums[7:8, where]
            below = 0.5 * (1.0 + lax.erf(u * 0.7071067811865476))
            gated_v[block * rows : (block + 1) * rows, where] = (u * below).astype(BF16)
            slope_v[slot, :, where] = below + u * (0.3989422804014327 * jnp.exp(-0.5 * u * u))
            return carry

        lax.fori_loop(0, hidden // 512, lift, 0)
        copy = pltpu.make_async_copy(
            slope_v.at[slot], slope_all.at[pl.ds(block * rows, rows)], local_sem.at[15 + slot]
        )
        copy.start()
        stored.append(copy)
        spread.forward(1)
    keep(gated_v, gated_all)
    spread.arrived(5)
    spread.arrived(6)
    spread.finish()
    for copy in small_copies:
        copy.wait_send()
    for copy in locals_[5:] + stored[-2:]:
        copy.wait()


def forward_call(heads, count, prefix, tokens, cotangent, small, qkv_shard, out_shard, up_shard, down_shard):
    rows, features = tokens.shape
    length = rows * 4
    depth, triple = qkv_shard.shape
    width = out_shard.shape[0]
    hidden = up_shard.shape[1]
    outer, inner = split_of(count)
    shape = jax.ShapeDtypeStruct
    hbm = pl.BlockSpec(memory_space=pl.ANY)
    vmem = pl.BlockSpec(memory_space=pltpu.VMEM)
    dma = pltpu.SemaphoreType.DMA
    pieces = 7
    return pl.pallas_call(
        functools.partial(forward_kernel, heads, count),
        out_shape=[
            shape((features, triple), BF16),
            shape((width, features), BF16),
            shape((features, hidden), BF16),
            shape((hidden, features), BF16),
            shape((length, features), BF16),
            shape((length, features), BF16),
            shape((length, triple), BF16),
            shape((length, width), BF16),
            shape((heads, length, 128), F32),
            shape((rows, features), F32),
            shape((length, features), BF16),
            shape((length, hidden), BF16),
            shape((length, hidden), F32),
            shape((8, features), F32),
        ],
        in_specs=[pl.BlockSpec(memory_space=pltpu.SMEM)] + [vmem] * 7,
        out_specs=[hbm] * 9 + [vmem] + [hbm] * 3 + [vmem],
        scratch_shapes=[
            pltpu.VMEM((count, 8, features), F32),
            pltpu.VMEM((length, features), BF16),
            pltpu.VMEM((features, triple), BF16),
            pltpu.VMEM((length, triple), BF16),
            pltpu.VMEM((length, width), BF16),
            pltpu.VMEM((heads, length, 128), F32),
            pltpu.VMEM((width, features), BF16),
            pltpu.VMEM((2, rows, features), BF16),
            pltpu.VMEM((2, rows, features), BF16),
            pltpu.VMEM((rows, features), BF16),
            pltpu.VMEM((rows, features), BF16),
            pltpu.VMEM((length, features), BF16),
            pltpu.VMEM((features, hidden), BF16),
            pltpu.VMEM((length, hidden), BF16),
            pltpu.VMEM((2, rows, hidden), F32),
            dma((count,)),
            dma((count,)),
            dma((pieces, outer)),
            dma((pieces, outer)),
            dma((pieces, outer, inner)),
            dma((pieces, outer, inner)),
            dma((3, 3)),
            dma((3, 3)),
            dma((1, 3)),
            dma((1, 3)),
            dma((17,)),
        ],
        compiler_params=pltpu.CompilerParams(
            collective_id=0, has_side_effects=True, vmem_limit_bytes=VMEM_BYTES
        ),
    )(prefix, tokens, cotangent, small, qkv_shard, out_shard, up_shard, down_shard)


def pack_small(features, query_bias, value_bias, up_bias, vectors):
    devices = lax.axis_size("dp")
    me = lax.axis_index("dp")
    rows = []
    for part in vectors:
        start = me * part.shape[0]
        rows.append(lax.dynamic_update_slice(jnp.zeros((features,), F32), part.astype(F32), (start,)))

    def spread_rows(part):
        wide = jnp.zeros((part.shape[0], part.shape[1] * devices), F32)
        return lax.dynamic_update_slice(wide, part.astype(F32), (0, me * part.shape[1])).reshape(-1)

    q = spread_rows(query_bias)
    joint = jnp.concatenate([q, jnp.zeros_like(q), spread_rows(value_bias)])
    rows.append(jnp.pad(joint, (0, features - joint.size)))
    u = spread_rows(up_bias)
    rows.append(jnp.pad(u, (0, features - u.size)))
    return jnp.stack(rows)


def layer_norm(rows, gain, shift):
    center = rows - jnp.mean(rows, axis=-1, keepdims=True)
    spread = jnp.mean(center * center, axis=-1, keepdims=True)
    return center * lax.rsqrt(spread + 1e-05) * gain + shift


def gelu_exact(values):
    return jax.nn.gelu(values, approximate=False)


def head_major(matrix, heads):
    return matrix.reshape(matrix.shape[0], heads, -1).transpose(1, 0, 2)


def row_major(stacked):
    return stacked.transpose(1, 0, 2).reshape(stacked.shape[1], -1)


def masked_scores(q_block, keys, start, prefix_len):
    scores = jnp.einsum("hqd,hkd->hqk", q_block, keys, preferred_element_type=jnp.float32)
    rows = start + lax.broadcasted_iota(jnp.int32, scores.shape[1:], 0)
    cols = lax.broadcasted_iota(jnp.int32, scores.shape[1:], 1)
    seen = (cols <= rows) | (cols < prefix_len)
    return jnp.where(seen[None], scores, -1e30)


def to_blocks(stacked, count):
    heads, length = (stacked.shape[0], stacked.shape[1])
    return stacked.reshape((heads, count, length // count) + stacked.shape[2:]).swapaxes(0, 1)


def from_blocks(blocked):
    count, heads, block = (blocked.shape[0], blocked.shape[1], blocked.shape[2])
    return blocked.swapaxes(0, 1).reshape((heads, count * block) + blocked.shape[3:])


def contract_rows(left, right):
    return jnp.einsum("ld,le->de", left, right, preferred_element_type=jnp.float32)


def times_transpose(left, right):
    return jnp.einsum("le,de->ld", left, right, preferred_element_type=jnp.float32)


def plain(
    tokens,
    prefix,
    query_weight,
    key_weight,
    value_weight,
    out_weight,
    query_bias,
    value_bias,
    up_weight,
    down_weight,
    up_bias,
    norm1_gain,
    norm1_bias,
    norm2_gain,
    norm2_bias,
    out_bias,
    down_bias,
    cotangent,
):
    f32 = jnp.float32
    bf16 = jnp.bfloat16
    devices = lax.axis_size("dp")
    small = (query_bias, value_bias, up_bias, norm1_gain, norm1_bias, norm2_gain, norm2_bias, out_bias, down_bias)
    packed = jnp.concatenate([part.reshape(-1) for part in small])
    packed = lax.all_gather(packed, "dp", axis=0, tiled=False)
    pieces = []
    offset = 0
    for part in small:
        piece = packed[:, offset : offset + part.size].reshape((devices,) + part.shape)
        offset += part.size
        pieces.append(jnp.moveaxis(piece, 0, -2).reshape(part.shape[:-1] + (-1,)))
    bq, bv, b1, g1, n1, g2, n2, bo, b2 = pieces
    wq, wk, wv, wo = (
        lax.all_gather(query_weight, "dp", axis=0, tiled=True),
        lax.all_gather(key_weight, "dp", axis=0, tiled=True),
        lax.all_gather(value_weight, "dp", axis=0, tiled=True),
        lax.all_gather(out_weight, "dp", axis=1, tiled=True),
    )
    w1, w2 = (
        lax.all_gather(up_weight, "dp", axis=0, tiled=True),
        lax.all_gather(down_weight, "dp", axis=1, tiled=True),
    )
    g1f, n1f, g2f, n2f = (g1.astype(f32), n1.astype(f32), g2.astype(f32), n2.astype(f32))
    bof, b2f = (bo.astype(f32), b2.astype(f32))
    heads = bq.shape[0]
    head_size = bq.shape[1]
    scale = head_size ** (-0.5)
    prefix_len = prefix[0]
    xf = tokens.astype(f32)
    h1 = layer_norm(xf, g1f, n1f).astype(bf16)
    rows1 = lax.all_gather(h1, "tensor", axis=0, tiled=True)
    length = rows1.shape[0]
    block = min(512, length)
    count = length // block
    query = (
        (jnp.dot(rows1, wq, preferred_element_type=f32) + bq.astype(f32).reshape(-1)) * scale
    ).astype(bf16)
    keyed = jnp.dot(rows1, wk, preferred_element_type=f32).astype(bf16)
    valued = (jnp.dot(rows1, wv, preferred_element_type=f32) + bv.astype(f32).reshape(-1)).astype(
        bf16
    )
    q_heads = head_major(query, heads)
    k_heads = head_major(keyed, heads)
    v_heads = head_major(valued, heads)
    q_blocks = to_blocks(q_heads, count)
    starts = jnp.arange(count, dtype=jnp.int32) * block

    def forward_block(item):
        q_block, start = item
        scores = masked_scores(q_block, k_heads, start, prefix_len)
        top = jnp.max(scores, axis=-1, keepdims=True)
        expd = jnp.exp(scores - top)
        total = jnp.sum(expd, axis=-1, keepdims=True)
        probs = (expd / total).astype(bf16)
        outv = jnp.einsum("hqk,hkd->hqd", probs, v_heads, preferred_element_type=f32)
        return (outv.astype(bf16), (top + jnp.log(total))[..., 0])

    o_blocks, lse_blocks = lax.map(forward_block, (q_blocks, starts))
    mixed = row_major(from_blocks(o_blocks))
    attn_part = jnp.dot(mixed, wo, preferred_element_type=f32)
    attn_total = lax.psum_scatter(attn_part.astype(bf16), "tensor", scatter_dimension=0, tiled=True).astype(f32)
    second = xf + attn_total + bof
    h2 = layer_norm(second, g2f, n2f).astype(bf16)
    rows2 = lax.all_gather(h2, "tensor", axis=0, tiled=True)
    hidden = jnp.dot(rows2, w1, preferred_element_type=f32) + b1.astype(f32).reshape(-1)
    gated = gelu_exact(hidden).astype(bf16)
    mlp_part = jnp.dot(gated, w2, preferred_element_type=f32)
    mlp_total = lax.psum_scatter(
        mlp_part.astype(jnp.bfloat16), "tensor", scatter_dimension=0, tiled=True
    ).astype(jnp.float32)
    layer_out = (second + mlp_total + b2f).astype(bf16)
    d_out = cotangent.astype(f32)
    g_b2 = jnp.sum(d_out, axis=0)
    d_rows = lax.all_gather(cotangent, "tensor", axis=0, tiled=True)
    d_gated = times_transpose(d_rows, w2)
    d_hidden = jax.vjp(gelu_exact, hidden)[1](d_gated)[0]
    g_b1 = jnp.sum(d_hidden, axis=0).reshape(b1.shape)
    d_hidden_low = d_hidden.astype(bf16)
    d_h2_part = times_transpose(d_hidden_low, w1)
    g_w2 = contract_rows(gated, d_rows)
    g_w1 = contract_rows(rows2, d_hidden_low)
    d_h2 = lax.psum_scatter(d_h2_part.astype(bf16), "tensor", scatter_dimension=0, tiled=True).astype(f32)
    norm2_back = jax.vjp(layer_norm, second, g2f, n2f)[1]
    d_second_ln, g_g2, g_n2 = norm2_back(d_h2)
    d_second = d_out + d_second_ln
    g_bo = jnp.sum(d_second, axis=0)
    d_second_low = d_second.astype(bf16)
    back_rows = lax.all_gather(d_second_low, "tensor", axis=0, tiled=True)
    g_wo = contract_rows(mixed, back_rows)
    d_mixed = times_transpose(back_rows, wo).astype(bf16)
    do_blocks = to_blocks(head_major(d_mixed, heads), count)

    def backward_block(carry, item):
        d_keys, d_vals = carry
        q_block, do_block, lse_block, start = item
        scores = masked_scores(q_block, k_heads, start, prefix_len)
        probs = jnp.exp(scores - lse_block[..., None])
        d_probs = jnp.einsum("hqd,hkd->hqk", do_block, v_heads, preferred_element_type=f32)
        d_vals = d_vals + jnp.einsum(
            "hqk,hqd->hkd", probs.astype(bf16), do_block, preferred_element_type=f32
        )
        inner = jnp.sum(probs * d_probs, axis=-1, keepdims=True)
        d_scores = (probs * (d_probs - inner)).astype(bf16)
        d_query = jnp.einsum("hqk,hkd->hqd", d_scores, k_heads, preferred_element_type=f32)
        d_keys = d_keys + jnp.einsum("hqk,hqd->hkd", d_scores, q_block, preferred_element_type=f32)
        return ((d_keys, d_vals), d_query)

    empty = jnp.zeros(k_heads.shape, f32)
    (d_keys, d_vals), dq_blocks = lax.scan(
        backward_block, (empty, empty), (q_blocks, do_blocks, lse_blocks, starts)
    )
    d_query = row_major(from_blocks(dq_blocks)) * scale
    d_keys = row_major(d_keys)
    d_vals = row_major(d_vals)
    g_bq = jnp.sum(d_query, axis=0).reshape(bq.shape)
    g_bv = jnp.sum(d_vals, axis=0).reshape(bv.shape)
    dq_low, dk_low, dv_low = (d_query.astype(bf16), d_keys.astype(bf16), d_vals.astype(bf16))
    g_wq = contract_rows(rows1, dq_low)
    g_wk = contract_rows(rows1, dk_low)
    g_wv = contract_rows(rows1, dv_low)
    d_h1_part = (
        times_transpose(dq_low, wq) + times_transpose(dk_low, wk) + times_transpose(dv_low, wv)
    )
    d_h1 = lax.psum_scatter(d_h1_part.astype(bf16), "tensor", scatter_dimension=0, tiled=True).astype(f32)
    norm1_back = jax.vjp(layer_norm, xf, g1f, n1f)[1]
    d_input_ln, g_g1, g_n1 = norm1_back(d_h1)
    input_grad = d_second + d_input_ln
    def scatter(part, dim):
        return lax.psum_scatter(part.astype(bf16), "dp", scatter_dimension=dim, tiled=True).astype(f32)

    s_w2, s_w1, s_wo = scatter(g_w2, 1), scatter(g_w1, 0), scatter(g_wo, 1)
    s_wq, s_wk, s_wv = scatter(g_wq, 0), scatter(g_wk, 0), scatter(g_wv, 0)

    def by_device(part):
        return jnp.moveaxis(part.reshape(part.shape[:-1] + (devices, -1)), -2, 0).reshape(devices, -1)

    rows = [by_device(part) for part in (g_bq, g_bv, g_b1, g_g1, g_n1, g_g2, g_n2, g_bo, g_b2)]
    total = lax.psum_scatter(jnp.concatenate(rows, axis=1), "dp", scatter_dimension=0, tiled=True)[0]
    offset = 0
    outs = []
    for part in (query_bias, value_bias, up_bias):
        outs.append(total[offset : offset + part.size].reshape(part.shape))
        offset += part.size
    s_bq, s_bv, s_b1 = outs
    vectors = lax.psum_scatter(
        total[offset:].reshape(6, lax.axis_size("tensor"), -1), "tensor", scatter_dimension=1, tiled=True
    ).reshape(6, -1)
    s_g1, s_n1, s_g2, s_n2, s_bo, s_b2 = (vectors[index] for index in range(6))
    return (
        layer_out,
        input_grad,
        s_wq,
        s_wk,
        s_wv,
        s_wo,
        s_bq,
        s_bv,
        s_w1,
        s_w2,
        s_b1,
        s_g1,
        s_n1,
        s_g2,
        s_n2,
        s_bo,
        s_b2,
    )


def fast(
    tokens,
    prefix,
    query_weight,
    key_weight,
    value_weight,
    out_weight,
    query_bias,
    value_bias,
    up_weight,
    down_weight,
    up_bias,
    norm1_gain,
    norm1_bias,
    norm2_gain,
    norm2_bias,
    out_bias,
    down_bias,
    cotangent,
):
    f32 = jnp.float32
    bf16 = jnp.bfloat16
    devices = lax.axis_size("dp")
    heads = query_bias.shape[0]
    row_features = tokens.shape[1]
    small = pack_small(
        row_features, query_bias, value_bias, up_bias,
        (norm1_gain, norm1_bias, norm2_gain, norm2_bias, out_bias, down_bias),
    )
    w_qkv, wo, w1, w2, rows1, d_rows, qkv, mixed, lse, second, rows2, gated, slope, sums = forward_call(
        heads, devices, prefix, tokens, cotangent, small,
        jnp.concatenate([query_weight, key_weight, value_weight], axis=1), out_weight, up_weight, down_weight,
    )
    g1f, n1f, g2f, n2f, bof, b2f = (sums[index] for index in range(6))
    bq, bv, b1 = (
        jnp.zeros((part.shape[0], part.shape[1] * devices), bf16) for part in (query_bias, value_bias, up_bias)
    )
    heads = bq.shape[0]
    head_size = bq.shape[1]
    scale = head_size ** (-0.5)
    prefix_len = prefix[0]
    xf = tokens.astype(f32)
    length = rows1.shape[0]
    block = min(512, length)
    count = length // block
    wq, wk, wv = jnp.split(w_qkv, 3, axis=1)
    query, keyed, valued = jnp.split(qkv, 3, axis=1)
    q_heads = head_major(query, heads)
    k_heads = head_major(keyed, heads)
    v_heads = head_major(valued, heads)
    q_blocks = to_blocks(q_heads, count)
    starts = jnp.arange(count, dtype=jnp.int32) * block

    lse_blocks = to_blocks(lse[:, :, 0], count)
    mlp_part = jnp.dot(gated, w2, preferred_element_type=f32)
    mlp_total = lax.psum_scatter(
        mlp_part.astype(jnp.bfloat16), "tensor", scatter_dimension=0, tiled=True
    ).astype(jnp.float32)
    layer_out = (second + mlp_total + b2f).astype(bf16)
    d_out = cotangent.astype(f32)
    g_b2 = jnp.sum(d_out, axis=0)
    d_gated = times_transpose(d_rows, w2)
    d_hidden = d_gated * slope
    g_b1 = jnp.sum(d_hidden, axis=0).reshape(b1.shape)
    d_hidden_low = d_hidden.astype(bf16)
    d_h2_part = times_transpose(d_hidden_low, w1)
    g_w2 = contract_rows(gated, d_rows)
    g_w1 = contract_rows(rows2, d_hidden_low)
    d_h2 = lax.psum_scatter(d_h2_part.astype(bf16), "tensor", scatter_dimension=0, tiled=True).astype(f32)
    norm2_back = jax.vjp(layer_norm, second, g2f, n2f)[1]
    d_second_ln, g_g2, g_n2 = norm2_back(d_h2)
    d_second = d_out + d_second_ln
    g_bo = jnp.sum(d_second, axis=0)
    d_second_low = d_second.astype(bf16)
    back_rows = lax.all_gather(d_second_low, "tensor", axis=0, tiled=True)
    g_wo = contract_rows(mixed, back_rows)
    d_mixed = times_transpose(back_rows, wo).astype(bf16)
    do_blocks = to_blocks(head_major(d_mixed, heads), count)

    def backward_block(carry, item):
        d_keys, d_vals = carry
        q_block, do_block, lse_block, start = item
        scores = masked_scores(q_block, k_heads, start, prefix_len)
        probs = jnp.exp(scores - lse_block[..., None])
        d_probs = jnp.einsum("hqd,hkd->hqk", do_block, v_heads, preferred_element_type=f32)
        d_vals = d_vals + jnp.einsum(
            "hqk,hqd->hkd", probs.astype(bf16), do_block, preferred_element_type=f32
        )
        inner = jnp.sum(probs * d_probs, axis=-1, keepdims=True)
        d_scores = (probs * (d_probs - inner)).astype(bf16)
        d_query = jnp.einsum("hqk,hkd->hqd", d_scores, k_heads, preferred_element_type=f32)
        d_keys = d_keys + jnp.einsum("hqk,hqd->hkd", d_scores, q_block, preferred_element_type=f32)
        return ((d_keys, d_vals), d_query)

    empty = jnp.zeros(k_heads.shape, f32)
    (d_keys, d_vals), dq_blocks = lax.scan(
        backward_block, (empty, empty), (q_blocks, do_blocks, lse_blocks, starts)
    )
    d_query = row_major(from_blocks(dq_blocks)) * scale
    d_keys = row_major(d_keys)
    d_vals = row_major(d_vals)
    g_bq = jnp.sum(d_query, axis=0).reshape(bq.shape)
    g_bv = jnp.sum(d_vals, axis=0).reshape(bv.shape)
    dq_low, dk_low, dv_low = (d_query.astype(bf16), d_keys.astype(bf16), d_vals.astype(bf16))
    g_wq = contract_rows(rows1, dq_low)
    g_wk = contract_rows(rows1, dk_low)
    g_wv = contract_rows(rows1, dv_low)
    d_h1_part = (
        times_transpose(dq_low, wq) + times_transpose(dk_low, wk) + times_transpose(dv_low, wv)
    )
    d_h1 = lax.psum_scatter(d_h1_part.astype(bf16), "tensor", scatter_dimension=0, tiled=True).astype(f32)
    norm1_back = jax.vjp(layer_norm, xf, g1f, n1f)[1]
    d_input_ln, g_g1, g_n1 = norm1_back(d_h1)
    input_grad = d_second + d_input_ln
    def scatter(part, dim):
        return lax.psum_scatter(part.astype(bf16), "dp", scatter_dimension=dim, tiled=True).astype(f32)

    s_w2, s_w1, s_wo = scatter(g_w2, 1), scatter(g_w1, 0), scatter(g_wo, 1)
    s_wq, s_wk, s_wv = scatter(g_wq, 0), scatter(g_wk, 0), scatter(g_wv, 0)

    def by_device(part):
        return jnp.moveaxis(part.reshape(part.shape[:-1] + (devices, -1)), -2, 0).reshape(devices, -1)

    rows = [by_device(part) for part in (g_bq, g_bv, g_b1, g_g1, g_n1, g_g2, g_n2, g_bo, g_b2)]
    total = lax.psum_scatter(jnp.concatenate(rows, axis=1), "dp", scatter_dimension=0, tiled=True)[0]
    offset = 0
    outs = []
    for part in (query_bias, value_bias, up_bias):
        outs.append(total[offset : offset + part.size].reshape(part.shape))
        offset += part.size
    s_bq, s_bv, s_b1 = outs
    vectors = lax.psum_scatter(
        total[offset:].reshape(6, lax.axis_size("tensor"), -1), "tensor", scatter_dimension=1, tiled=True
    ).reshape(6, -1)
    s_g1, s_n1, s_g2, s_n2, s_bo, s_b2 = (vectors[index] for index in range(6))
    return (
        layer_out,
        input_grad,
        s_wq,
        s_wk,
        s_wv,
        s_wo,
        s_bq,
        s_bv,
        s_w1,
        s_w2,
        s_b1,
        s_g1,
        s_n1,
        s_g2,
        s_n2,
        s_bo,
        s_b2,
    )


def local(*args):
    tokens, query_weight, up_weight = args[0], args[2], args[8]
    devices = lax.axis_size("dp")
    features = tokens.shape[1]
    share = features // devices
    fits = (
        lax.axis_size("tensor") == 4
        and devices <= 8
        and share % 128 == 0
        and tokens.shape[0] == 256
        and 3 * query_weight.shape[1] <= features
        and up_weight.shape[1] <= features
    )
    return fast(*args) if fits else plain(*args)


def solution(mesh):
    in_specs = (
        P(("dp", "tensor"), None),
        P("dp"),
        P("dp", "tensor"),
        P("dp", "tensor"),
        P("dp", "tensor"),
        P("tensor", "dp"),
        P("tensor", "dp"),
        P("tensor", "dp"),
        P("dp", "tensor"),
        P("tensor", "dp"),
        P("tensor", "dp"),
        P("dp"),
        P("dp"),
        P("dp"),
        P("dp"),
        P("dp"),
        P("dp"),
        P(("dp", "tensor"), None),
    )
    out_specs = (
        P(("dp", "tensor"), None),
        P(("dp", "tensor"), None),
        P("dp", "tensor"),
        P("dp", "tensor"),
        P("dp", "tensor"),
        P("tensor", "dp"),
        P("tensor", "dp"),
        P("tensor", "dp"),
        P("dp", "tensor"),
        P("tensor", "dp"),
        P("tensor", "dp"),
        P(("dp", "tensor")),
        P(("dp", "tensor")),
        P(("dp", "tensor")),
        P(("dp", "tensor")),
        P(("dp", "tensor")),
        P(("dp", "tensor")),
    )
    return jax.shard_map(local, mesh=mesh, in_specs=in_specs, out_specs=out_specs, check_vma=False)
```

```python
import functools

import jax
import jax.numpy as jnp
from jax import lax
from jax.experimental import pallas as pl
from jax.experimental.pallas import tpu as pltpu
from jax.sharding import PartitionSpec as P

MESH = pl.DeviceIdType.MESH
F32 = jnp.float32
BF16 = jnp.bfloat16
PREFIX_TOP = 512
VMEM_BYTES = 67043328


def split_of(count):
    inner = 1
    for size in range(1, count + 1):
        if size * size <= count and count % size == 0:
            inner = size
    return count // inner, inner


def remote(source, target, send_sem, recv_sem, dp, tensor):
    return pltpu.make_async_remote_copy(
        src_ref=source,
        dst_ref=target,
        send_sem=send_sem,
        recv_sem=recv_sem,
        device_id=(dp, tensor),
        device_id_type=MESH,
    )


def block_of(index, size):
    return pl.ds(pl.multiple_of(index * size, size), size)


class Spot:
    def __init__(self, count):
        self.outer, self.inner = split_of(count)
        self.count = count
        self.dp = lax.axis_index("dp")
        self.tensor = lax.axis_index("tensor")
        self.row = lax.div(self.dp, self.inner)
        self.column = lax.rem(self.dp, self.inner)
        self.core_peer = self.tensor + 1 - 2 * lax.rem(self.tensor, 2)
        self.x_peer = lax.rem(self.tensor + 2, 4)
        self.far_peer = lax.rem(self.core_peer + 2, 4)

    def across(self, step):
        return lax.rem(self.row + step, self.outer) * self.inner + self.column

    def beside(self, step, row=None):
        return (self.row if row is None else row) * self.inner + lax.rem(self.column + step, self.inner)

    def meet(self, far=False):
        barrier = pltpu.get_barrier_semaphore()
        for step in range(1, self.count):
            pl.semaphore_signal(
                barrier, inc=1, device_id=(lax.rem(self.dp + step, self.count), self.tensor), device_id_type=MESH
            )
        for peer in (self.core_peer, self.x_peer) + ((self.far_peer,) if far else ()):
            pl.semaphore_signal(barrier, inc=1, device_id=(self.dp, peer), device_id_type=MESH)
        pl.semaphore_wait(barrier, self.count + 1 + far)

    def release(self, ready):
        for peer in (self.core_peer, self.x_peer):
            pl.semaphore_signal(ready, inc=1, device_id=(self.dp, peer), device_id_type=MESH)


class Spread:
    def __init__(self, spot, pieces, z_send, z_recv, y_send, y_recv):
        self.spot, self.pieces = spot, pieces
        self.sems = (z_send, z_recv, y_send, y_recv)
        self.sent = []
        self.todo = [(piece, step) for piece in range(len(pieces)) for step in range(1, spot.outer)]
        self.own_next = 0

    def send_rows(self, piece):
        source, target = self.pieces[piece]
        for step in range(1, self.spot.outer):
            copy = remote(
                source, target(self.spot.dp), self.sems[0].at[piece, step], self.sems[1].at[piece, step],
                self.spot.across(step), self.spot.tensor,
            )
            copy.start()
            self.sent.append(copy)

    def y_copies(self, piece, step):
        spot = self.spot
        source, target = self.pieces[piece]
        owner = spot.across(spot.outer - step) if step else spot.dp
        if step:
            source = target(owner)
        copies = []
        for side in range(1, spot.inner):
            copies.append(remote(
                source, target(owner), self.sems[2].at[piece, step, side], self.sems[3].at[piece, step, side],
                spot.beside(side), spot.tensor,
            ))
        return copies

    def send_own(self, upto):
        while self.own_next < min(upto, len(self.pieces)):
            for copy in self.y_copies(self.own_next, 0):
                copy.start()
                self.sent.append(copy)
            self.own_next += 1

    def forward(self, count):
        for _ in range(count):
            if not self.todo:
                return
            piece, step = self.todo.pop(0)
            source, target = self.pieces[piece]
            remote(
                source, target(self.spot.across(self.spot.outer - step)), self.sems[0].at[piece, step],
                self.sems[1].at[piece, step], self.spot.across(step), self.spot.tensor,
            ).wait_recv()
            for copy in self.y_copies(piece, step):
                copy.start()
                self.sent.append(copy)
            if step == self.spot.outer - 1:
                self.send_own(piece + 4)

    def arrived(self, piece):
        while self.todo and self.todo[0][0] <= piece:
            self.forward(1)
        for step in range(self.spot.outer):
            for copy in self.y_copies(piece, step):
                copy.wait_recv()

    def finish(self):
        for copy in self.sent:
            copy.wait_send()


class TensorGather:
    def __init__(self, spot, own, full, rows, send, recv):
        self.spot, self.full, self.rows, self.send, self.recv = spot, full, rows, send, recv
        place = self.at(spot.tensor)
        self.to_x = remote(own, place, send.at[0], recv.at[0], spot.dp, spot.x_peer)
        self.to_core = remote(own, place, send.at[1], recv.at[1], spot.dp, spot.core_peer)
        self.to_x.start()
        self.to_core.start()

    def at(self, index):
        return self.full.at[block_of(index, self.rows)]

    def pass_on(self):
        self.to_x.wait_recv()
        place = self.at(self.spot.x_peer)
        self.on = remote(place, place, self.send.at[2], self.recv.at[2], self.spot.dp, self.spot.core_peer)
        self.on.start()

    def finish(self):
        self.to_core.wait_recv()
        self.on.wait_recv()
        for copy in (self.to_x, self.to_core, self.on):
            copy.wait_send()


def tensor_sum(spot, product, core_send, core_recv, x_send, x_recv, send, recv, finish):
    width = core_send.shape[2]
    chunk = 512
    count = width // chunk

    def fill(rank, target):
        def body(index, carry):
            target[:, block_of(index, chunk)] = product(rank, index).astype(BF16)
            return carry

        lax.fori_loop(0, count, body, 0)

    copies = []
    for slot, rank in enumerate((spot.far_peer, spot.core_peer)):
        fill(rank, core_send.at[slot])
        copy = remote(core_send.at[slot], core_recv.at[slot], send.at[slot], recv.at[slot], spot.dp, spot.core_peer)
        copy.start()
        copies.append(copy)
    copies[0].wait_recv()

    def join(index, carry):
        where = block_of(index, chunk)
        x_send[:, where] = (product(spot.x_peer, index) + core_recv[0, :, where].astype(F32)).astype(BF16)
        return carry

    lax.fori_loop(0, count, join, 0)
    over = remote(x_send, x_recv, send.at[2], recv.at[2], spot.dp, spot.x_peer)
    over.start()
    copies[1].wait_recv()

    def end():
        over.wait_recv()

        def last(index, carry):
            where = block_of(index, chunk)
            total = product(spot.tensor, index) + core_recv[1, :, where].astype(F32) + x_recv[:, where].astype(F32)
            finish(index, total)
            return carry

        lax.fori_loop(0, count, last, 0)
        for copy in copies + [over]:
            copy.wait_send()

    return end


def normal_parts(rows):
    center = rows - jnp.mean(rows, axis=-1, keepdims=True)
    spread = jnp.mean(center * center, axis=-1, keepdims=True)
    return center, lax.rsqrt(spread + 1e-05)


def forward_kernel(
    heads,
    count,
    prefix,
    tokens,
    cotangent,
    small,
    qkv_shard,
    out_shard,
    up_shard,
    down_shard,
    wqkv,
    wo,
    w1,
    w2,
    h1_all,
    d_rows,
    qkv_all,
    mixed_all,
    lse_all,
    second,
    h2_all,
    gated_all,
    slope_all,
    sums,
    smalls,
    h1v,
    wqkv_v,
    qkv_v,
    mixed_v,
    lse_v,
    wo_v,
    core_send,
    core_recv,
    x_send,
    x_recv,
    h2v,
    w1_v,
    gated_v,
    slope_v,
    small_send,
    small_recv,
    z_send,
    z_recv,
    y_send,
    y_recv,
    g_send,
    g_recv,
    s_send,
    s_recv,
    local_sem,
):
    spot = Spot(count)
    rows, features = tokens.shape
    length = h1v.shape[0]
    depth = qkv_shard.shape[0]
    width = wo_v.shape[0]
    hidden = up_shard.shape[1]
    half = depth // 2
    tall = hidden // 2
    pieces = [
        (qkv_shard.at[pl.ds(part * half, half)],
         lambda owner, part=part: wqkv.at[block_of(owner * 2 + part, half)])
        for part in range(2)
    ]
    pieces.append((out_shard, lambda owner: wo.at[:, block_of(owner, depth)]))
    pieces += [
        (up_shard.at[pl.ds(part * half, half)],
         lambda owner, part=part: w1.at[block_of(owner * 2 + part, half)])
        for part in range(2)
    ]
    pieces += [
        (down_shard.at[pl.ds(part * tall, tall)],
         lambda owner, part=part: w2.at[pl.ds(part * tall, tall), block_of(owner, depth)])
        for part in range(2)
    ]
    spread = Spread(spot, pieces, z_send, z_recv, y_send, y_recv)
    locals_ = []

    def keep(source, target):
        copy = pltpu.make_async_copy(source, target, local_sem.at[len(locals_)])
        copy.start()
        locals_.append(copy)

    spot.meet()
    small_copies = []
    for step in range(1, count):
        copy = remote(
            small, smalls.at[spot.dp], small_send.at[step], small_recv.at[step],
            lax.rem(spot.dp + step, count), spot.tensor,
        )
        copy.start()
        small_copies.append(copy)
    for piece in range(len(pieces)):
        spread.send_rows(piece)
    spread.send_own(4)
    for source, target in pieces:
        keep(source, target(spot.dp))
    smalls[spot.dp] = small[...]
    for step, copy in enumerate(small_copies):
        remote(
            small, smalls.at[lax.rem(spot.dp + count - step - 1, count)], small_send.at[step + 1],
            small_recv.at[step + 1], spot.dp, spot.core_peer,
        ).wait_recv()
    total = smalls[0]
    for index in range(1, count):
        total = total + smalls[index]
    sums[...] = total

    strip = 32
    base = spot.tensor * rows

    def norm1(index, carry):
        where = block_of(index, strip)
        center, scale = normal_parts(tokens[where, :].astype(F32))
        h1v[pl.ds(pl.multiple_of(base + index * strip, strip), strip), :] = (
            center * scale * sums[0:1, :] + sums[1:2, :]
        ).astype(BF16)
        return carry

    lax.fori_loop(0, rows // strip, norm1, 0)
    gather1 = TensorGather(spot, h1v.at[block_of(spot.tensor, rows)], h1v, rows, g_send.at[0], g_recv.at[0])
    gather_d = TensorGather(spot, cotangent, d_rows, rows, g_send.at[1], g_recv.at[1])
    keep(cotangent, d_rows.at[block_of(spot.tensor, rows)])
    spread.forward(spot.outer - 1)
    gather1.pass_on()
    spread.forward(spot.outer - 1)
    gather1.finish()
    keep(h1v, h1_all)
    gather_d.pass_on()
    spread.arrived(0)
    spread.arrived(1)
    for copy in locals_[:2]:
        copy.wait()
    load = pltpu.make_async_copy(wqkv, wqkv_v, local_sem.at[14])
    load.start()
    spread.forward(1)
    load.wait()

    def project(index, carry):
        where = block_of(index, rows)
        for part in range(3):
            lanes = slice(part * width, (part + 1) * width)
            value = jnp.dot(h1v[where, :], wqkv_v[:, lanes], preferred_element_type=F32) + sums[6:7, lanes]
            if part == 0:
                value = value * (width // heads) ** -0.5
            qkv_v[where, lanes] = value.astype(BF16)
        return carry

    lax.fori_loop(0, length // rows, project, 0)
    keep(qkv_v, qkv_all)
    spread.forward(2)
    size = width // heads
    limit = prefix[0]
    bench = 256

    for block in range(length // bench):
        reach = min(length, max((block + 1) * bench, PREFIX_TOP))
        span = slice(block * bench, (block + 1) * bench)

        def attend(head, carry, block=block, span=span, reach=reach):
            line = block * bench + lax.broadcasted_iota(jnp.int32, (bench, reach), 0)
            place = lax.broadcasted_iota(jnp.int32, (bench, reach), 1)
            seen = (place <= line) | (place < limit)
            q = qkv_v[span, block_of(head, size)]
            k = qkv_v[0:reach, pl.ds(pl.multiple_of(width + head * size, size), size)]
            v = qkv_v[0:reach, pl.ds(pl.multiple_of(2 * width + head * size, size), size)]
            scores = lax.dot_general(q, k, (((1,), (1,)), ((), ())), preferred_element_type=F32)
            scores = jnp.where(seen, scores, -1e30)
            top = jnp.max(scores, axis=-1, keepdims=True)
            expd = jnp.exp(scores - top)
            total = jnp.sum(expd, axis=-1, keepdims=True)
            probs = (expd * (1.0 / total)).astype(BF16)
            mixed_v[span, block_of(head, size)] = jnp.dot(probs, v, preferred_element_type=F32).astype(BF16)
            lse_v[head, span, :] = jnp.broadcast_to(top + jnp.log(total), (bench, 128))
            return carry

        lax.fori_loop(0, heads, attend, 0)
        if block % 2 == 1:
            spread.forward(1)
    keep(mixed_v, mixed_all)
    keep(lse_v, lse_all)
    spread.arrived(2)
    locals_[2].wait()
    load = pltpu.make_async_copy(wo, wo_v, local_sem.at[14])
    load.start()
    load.wait()

    def out_part(rank, index):
        return jnp.dot(mixed_v[block_of(rank, rows), :], wo_v[:, block_of(index, 512)], preferred_element_type=F32)

    def take_second(index, total):
        where = block_of(index, 512)
        second[:, where] = tokens[:, where].astype(F32) + total + sums[4:5, where]

    end = tensor_sum(
        spot, out_part, core_send, core_recv, x_send, x_recv, s_send.at[0], s_recv.at[0], take_second
    )
    spread.forward(spot.outer - 1)
    end()

    def norm2(index, carry):
        where = block_of(index, strip)
        center, scale = normal_parts(second[where, :])
        h2v[pl.ds(pl.multiple_of(base + index * strip, strip), strip), :] = (
            center * scale * sums[2:3, :] + sums[3:4, :]
        ).astype(BF16)
        return carry

    lax.fori_loop(0, rows // strip, norm2, 0)
    gather2 = TensorGather(spot, h2v.at[block_of(spot.tensor, rows)], h2v, rows, g_send.at[2], g_recv.at[2])
    spread.forward(spot.outer - 1)
    gather2.pass_on()
    gather2.finish()
    gather_d.finish()
    keep(h2v, h2_all)
    spread.arrived(3)
    spread.arrived(4)
    for copy in locals_[3:5]:
        copy.wait()
    load = pltpu.make_async_copy(w1, w1_v, local_sem.at[14])
    load.start()
    spread.forward(1)
    load.wait()
    stored = []
    for block in range(length // rows):
        slot = block % 2
        if block >= 2:
            stored[block - 2].wait()

        def lift(index, carry, block=block, slot=slot):
            where = block_of(index, 512)
            u = jnp.dot(
                h2v[block * rows : (block + 1) * rows, :], w1_v[:, where], preferred_element_type=F32
            ) + sums[7:8, where]
            below = 0.5 * (1.0 + lax.erf(u * 0.7071067811865476))
            gated_v[block * rows : (block + 1) * rows, where] = (u * below).astype(BF16)
            slope_v[slot, :, where] = below + u * (0.3989422804014327 * jnp.exp(-0.5 * u * u))
            return carry

        lax.fori_loop(0, hidden // 512, lift, 0)
        copy = pltpu.make_async_copy(
            slope_v.at[slot], slope_all.at[pl.ds(block * rows, rows)], local_sem.at[15 + slot]
        )
        copy.start()
        stored.append(copy)
        spread.forward(1)
    keep(gated_v, gated_all)
    spread.arrived(5)
    spread.arrived(6)
    spread.finish()
    for copy in small_copies:
        copy.wait_send()
    for copy in locals_[5:] + stored[-2:]:
        copy.wait()


def forward_call(heads, count, prefix, tokens, cotangent, small, qkv_shard, out_shard, up_shard, down_shard):
    rows, features = tokens.shape
    length = rows * 4
    depth, triple = qkv_shard.shape
    width = out_shard.shape[0]
    hidden = up_shard.shape[1]
    outer, inner = split_of(count)
    shape = jax.ShapeDtypeStruct
    hbm = pl.BlockSpec(memory_space=pl.ANY)
    vmem = pl.BlockSpec(memory_space=pltpu.VMEM)
    dma = pltpu.SemaphoreType.DMA
    pieces = 7
    return pl.pallas_call(
        functools.partial(forward_kernel, heads, count),
        out_shape=[
            shape((features, triple), BF16),
            shape((width, features), BF16),
            shape((features, hidden), BF16),
            shape((hidden, features), BF16),
            shape((length, features), BF16),
            shape((length, features), BF16),
            shape((length, triple), BF16),
            shape((length, width), BF16),
            shape((heads, length, 128), F32),
            shape((rows, features), F32),
            shape((length, features), BF16),
            shape((length, hidden), BF16),
            shape((length, hidden), F32),
            shape((8, features), F32),
        ],
        in_specs=[pl.BlockSpec(memory_space=pltpu.SMEM)] + [vmem] * 7,
        out_specs=[hbm] * 9 + [vmem] + [hbm] * 3 + [vmem],
        scratch_shapes=[
            pltpu.VMEM((count, 8, features), F32),
            pltpu.VMEM((length, features), BF16),
            pltpu.VMEM((features, triple), BF16),
            pltpu.VMEM((length, triple), BF16),
            pltpu.VMEM((length, width), BF16),
            pltpu.VMEM((heads, length, 128), F32),
            pltpu.VMEM((width, features), BF16),
            pltpu.VMEM((2, rows, features), BF16),
            pltpu.VMEM((2, rows, features), BF16),
            pltpu.VMEM((rows, features), BF16),
            pltpu.VMEM((rows, features), BF16),
            pltpu.VMEM((length, features), BF16),
            pltpu.VMEM((features, hidden), BF16),
            pltpu.VMEM((length, hidden), BF16),
            pltpu.VMEM((2, rows, hidden), F32),
            dma((count,)),
            dma((count,)),
            dma((pieces, outer)),
            dma((pieces, outer)),
            dma((pieces, outer, inner)),
            dma((pieces, outer, inner)),
            dma((3, 3)),
            dma((3, 3)),
            dma((1, 3)),
            dma((1, 3)),
            dma((17,)),
        ],
        compiler_params=pltpu.CompilerParams(
            collective_id=0, has_side_effects=True, vmem_limit_bytes=VMEM_BYTES
        ),
    )(prefix, tokens, cotangent, small, qkv_shard, out_shard, up_shard, down_shard)
class Reduce:
    def __init__(self, spot, left, right, lanes, landing, target, shared, index, last):
        self.spot, self.left, self.right, self.lanes = spot, left, right, lanes
        self.landing, self.target, self.shared, self.index, self.last = landing, target, shared, index, last
        self.width = lanes.stop - lanes.start
        self.share = target.shape[0]
        self.stepped = {}
        self.held = False

    def block(self, owner, take):
        turned = jnp.transpose(self.left[:, block_of(owner, self.share)])
        for start in range(0, self.width, 512):
            source = self.right[:, self.lanes.start + start : self.lanes.start + start + 512]
            take(slice(start, start + 512), jnp.dot(turned, source, preferred_element_type=F32))

    def y_copy(self, step):
        shared = self.shared
        area = pl.ds(0, self.width)
        return remote(
            shared["y_out"].at[step, :, area], shared["y_in"].at[step, :, area], shared["y_send"].at[step],
            shared["y_recv"].at[step], self.spot.beside(1), self.spot.tensor,
        )

    def z_copy(self, step):
        shared = self.shared
        return remote(
            shared["z_out"].at[step, :, pl.ds(0, self.width)], self.landing.at[step - 1],
            shared["z_send"].at[step], shared["z_recv"].at[self.index, step], self.spot.across(step),
            self.spot.tensor,
        )

    def produce(self, step):
        shared, spot = self.shared, self.spot
        row = lax.rem(spot.row + step, spot.outer)
        if step in shared["y_busy"]:
            shared["y_busy"].pop(step).wait_send()

        def take(where, value):
            shared["y_out"][step, :, where] = value.astype(BF16)

        self.block(spot.beside(1, row), take)
        if self.index > 0:
            pl.semaphore_wait(shared["credit"], 1)
        copy = self.y_copy(step)
        copy.start()
        shared["y_busy"][step] = copy

    def hold(self):
        self.held = True
        for step in range(self.spot.outer):

            def take(where, value, step=step):
                self.shared["z_out"][step, :, where] = value.astype(BF16)

            self.block(self.spot.across(step), take)

    def serve(self, step):
        shared, spot = self.shared, self.spot
        self.y_copy(step).wait_recv()
        if step in shared["z_busy"]:
            shared["z_busy"].pop(step).wait_send()
        y_in, z_out = shared["y_in"], shared["z_out"]
        if self.held:
            for start in range(0, self.width, 512):
                where = slice(start, start + 512)
                z_out[step, :, where] = (z_out[step, :, where].astype(F32) + y_in[step, :, where].astype(F32)).astype(BF16)
        else:

            def take(where, value):
                z_out[step, :, where] = (value + y_in[step, :, where].astype(F32)).astype(BF16)

            self.block(spot.across(step), take)
        if not self.last:
            pl.semaphore_signal(
                shared["credit"], inc=1, device_id=(spot.beside(1), spot.tensor), device_id_type=MESH
            )
        if step:
            copy = self.z_copy(step)
            copy.start()
            shared["z_busy"][step] = copy

    def settle(self):
        shared, spot = self.shared, self.spot
        for step in range(1, spot.outer):
            self.z_copy(step).wait_recv()
        loads, stores = [], []
        chunks = self.width // 512
        for chunk in range(chunks):
            loads.append(pltpu.make_async_copy(
                self.landing.at[:, :, pl.ds(chunk * 512, 512)], shared["z_stage"].at[chunk % 2],
                shared["stage_sem"].at[chunk % 2],
            ))
            stores.append(pltpu.make_async_copy(
                shared["o_stage"].at[chunk % 2], self.target.at[:, pl.ds(chunk * 512, 512)],
                shared["stage_sem"].at[2 + chunk % 2],
            ))
        loads[0].start()
        for chunk in range(chunks):
            loads[chunk].wait()
            if chunk + 1 < chunks:
                loads[chunk + 1].start()
            if chunk >= 2:
                stores[chunk - 2].wait()
            total = shared["z_out"][0, :, chunk * 512 : (chunk + 1) * 512].astype(F32)
            for step in range(spot.outer - 1):
                total = total + shared["z_stage"][chunk % 2, step].astype(F32)
            shared["o_stage"][chunk % 2] = total
            stores[chunk].start()
        for store in stores[-2:]:
            store.wait()


def row_dot(left, right):
    return lax.dot_general(left, right, (((1,), (1,)), ((), ())), preferred_element_type=F32)


def backward_kernel(
    heads,
    count,
    prefix,
    sums,
    tokens,
    cotangent,
    wqkv,
    wo,
    w1,
    w2,
    h1_all,
    d_rows,
    qkv_all,
    mixed_all,
    lse_v,
    second,
    h2_all,
    gated_all,
    slope_all,
    layer_out,
    input_grad,
    grad_down,
    grad_up,
    grad_out,
    grad_qkv,
    vector_sums,
    bias_sums,
    land_down,
    land_up,
    land_out,
    land_qkv,
    weight_v,
    buf1,
    buf2,
    buf3,
    buf4,
    buf5,
    core_send,
    core_recv,
    x_send,
    x_recv,
    y_in,
    y_out,
    z_out,
    z_stage,
    o_stage,
    spare,
    line,
    dk_sum,
    dv_sum,
    vectors,
    biases,
    vector_in,
    bias_in,
    part_sum,
    part_in,
    y_send,
    y_recv,
    z_send,
    z_recv,
    g_send,
    g_recv,
    s_send,
    s_recv,
    v_send,
    v_recv,
    b_send,
    b_recv,
    t_send,
    t_recv,
    stage_sem,
    load_sem,
    credit,
    ready,
):
    spot = Spot(count)
    rows, features = line.shape
    length = buf1.shape[0]
    width = wo.shape[0]
    hidden = w1.shape[1]
    triple = 3 * width
    size = width // heads
    scale = size ** -0.5
    tail = slice(triple, triple + width)
    shared = {
        "y_in": y_in, "y_out": y_out, "z_out": z_out, "z_stage": z_stage, "o_stage": o_stage, "y_send": y_send,
        "y_recv": y_recv, "z_send": z_send, "z_recv": z_recv, "credit": credit, "stage_sem": stage_sem,
        "y_busy": {}, "z_busy": {},
    }
    down = Reduce(spot, buf1, buf2, slice(0, hidden), land_down, grad_down, shared, 0, False)
    up = Reduce(spot, buf4, buf3, slice(0, hidden), land_up, grad_up, shared, 1, False)
    out = Reduce(spot, buf1, buf2, tail, land_out, grad_out, shared, 2, False)
    qkv = Reduce(spot, buf4, buf5, slice(0, triple), land_qkv, grad_qkv, shared, 3, True)

    def fetch(source, target, slot):
        copy = pltpu.make_async_copy(source, target, load_sem.at[slot])
        copy.start()
        return copy

    load_a = fetch(d_rows, buf1, 0)
    load_b = fetch(gated_all, buf2, 1)
    load_w = fetch(w2, weight_v, 2)
    slopes = [fetch(slope_all.at[pl.ds(part * rows, rows)], (spare, input_grad)[part % 2], 3 + part % 2) for part in range(2)]
    load_h = fetch(h2_all, buf4, 5)
    load_c = fetch(cotangent, line, 6)
    spot.meet(True)
    vectors[...] = jnp.zeros_like(vectors)
    biases[...] = jnp.zeros_like(biases)
    load_a.wait()
    load_b.wait()
    order = list(range(1, spot.outer)) + [0]
    for step in order:
        down.produce(step)
    load_w.wait()
    for part in range(length // rows):
        held = (spare, input_grad)[part % 2]
        slopes[part].wait()

        def lower(index, carry, part=part, held=held):
            where = block_of(index, 512)
            span = slice(part * rows, (part + 1) * rows)
            du = row_dot(buf1[span, :], weight_v[where, :]) * held[:, where]
            biases[pl.ds(index, 1), :] += jnp.sum(du, axis=0, keepdims=True)
            buf3[span, where] = du.astype(BF16)
            return carry

        lax.fori_loop(0, hidden // 512, lower, 0)
        if part + 2 < length // rows:
            slopes.append(fetch(slope_all.at[pl.ds((part + 2) * rows, rows)], held, 3 + part % 2))
    load_w = fetch(w1, weight_v, 2)
    load_s = fetch(second, spare, 3)
    down.hold()
    load_q = fetch(qkv_all, buf2.at[:, pl.ds(0, triple)], 0)
    load_m = fetch(mixed_all, buf2.at[:, pl.ds(triple, width)], 1)
    load_w.wait()
    load_h.wait()

    def h2_part(rank, index):
        return row_dot(buf3[block_of(rank, rows), :], weight_v[block_of(index, 512), :])

    def take_h2(index, total):
        input_grad[:, block_of(index, 512)] = total

    tensor = (core_send, core_recv, x_send, x_recv)
    end = tensor_sum(spot, h2_part, *tensor, s_send, s_recv, take_h2)
    down.serve(1)
    up.produce(1)
    down.serve(2)
    up.produce(2)
    end()
    spot.release(ready)
    load_o = fetch(wo, weight_v.at[pl.ds(0, width)], 2)
    load_s.wait()
    load_c.wait()
    strip = 32
    base = spot.tensor * rows

    def norm_back(rows_of, gain, grads, keep, first):
        center, inverse = normal_parts(rows_of)
        normal = center * inverse
        vectors[first : first + 1, :] += jnp.sum(grads * normal, axis=0, keepdims=True)
        vectors[first + 1 : first + 2, :] += jnp.sum(grads, axis=0, keepdims=True)
        scaled = grads * gain
        mean = jnp.mean(scaled, axis=-1, keepdims=True)
        slope = jnp.mean(scaled * normal, axis=-1, keepdims=True)
        return keep + inverse * (scaled - mean - normal * slope)

    def back2(index, carry):
        where = block_of(index, strip)
        dy = line[where, :].astype(F32)
        dx = norm_back(spare[where, :], sums[2:3, :], input_grad[where, :], dy, 2)
        vectors[4:5, :] += jnp.sum(dx, axis=0, keepdims=True)
        vectors[5:6, :] += jnp.sum(dy, axis=0, keepdims=True)
        input_grad[where, :] = dx
        buf1[pl.ds(pl.multiple_of(base + index * strip, strip), strip), :] = dx.astype(BF16)
        return carry

    lax.fori_loop(0, rows // strip, back2, 0)
    gather = TensorGather(spot, buf1.at[block_of(spot.tensor, rows)], buf1, rows, g_send, g_recv)
    load_t = fetch(tokens, line, 6)
    down.serve(3)
    up.produce(3)
    gather.pass_on()
    load_o.wait()
    gather.finish()
    load_q.wait()
    load_m.wait()

    def mix_back(index, carry):
        where = block_of(index, rows)
        buf5[where, tail] = row_dot(buf1[where, :], weight_v[0:width, :]).astype(BF16)
        return carry

    lax.fori_loop(0, length // rows, mix_back, 0)
    load_w = fetch(wqkv, weight_v.at[:, pl.ds(0, triple)], 2)
    limit = prefix[0]
    bench = 256

    def attend(head, carry):
        q_at = block_of(head, size)
        k_at = pl.ds(pl.multiple_of(width + head * size, size), size)
        v_at = pl.ds(pl.multiple_of(2 * width + head * size, size), size)
        o_at = pl.ds(pl.multiple_of(triple + head * size, size), size)
        dk_sum[...] = jnp.zeros_like(dk_sum)
        dv_sum[...] = jnp.zeros_like(dv_sum)
        for block in range(length // bench):
            reach = min(length, max((block + 1) * bench, PREFIX_TOP))
            span = slice(block * bench, (block + 1) * bench)
            row_of = block * bench + lax.broadcasted_iota(jnp.int32, (bench, reach), 0)
            place = lax.broadcasted_iota(jnp.int32, (bench, reach), 1)
            seen = (place <= row_of) | (place < limit)
            q = buf2[span, q_at]
            k = buf2[0:reach, k_at]
            v = buf2[0:reach, v_at]
            do = buf5[span, o_at]
            scores = jnp.where(seen, row_dot(q, k), -1e30)
            probs = jnp.exp(scores - lse_v[head, span, 0:1])
            d_probs = row_dot(do, v)
            inner = jnp.sum(probs * d_probs, axis=-1, keepdims=True)
            d_scores = (probs * (d_probs - inner)).astype(BF16)
            flip = (((0,), (0,)), ((), ()))
            dv_sum[0:reach, :] += lax.dot_general(probs.astype(BF16), do, flip, preferred_element_type=F32)
            dk_sum[0:reach, :] += lax.dot_general(d_scores, q, flip, preferred_element_type=F32)
            dq = jnp.dot(d_scores, k, preferred_element_type=F32) * scale
            biases[4:5, q_at] += jnp.sum(dq, axis=0, keepdims=True)
            buf5[span, q_at] = dq.astype(BF16)
        buf5[:, k_at] = dk_sum[...].astype(BF16)
        buf5[:, v_at] = dv_sum[...].astype(BF16)
        biases[5:6, q_at] += jnp.sum(dv_sum[...], axis=0, keepdims=True)
        return carry

    half = heads // 2
    lax.fori_loop(0, half, attend, 0)
    down.serve(0)
    up.produce(0)
    lax.fori_loop(half, heads, attend, 0)
    load_w.wait()

    def h1_part(rank, index):
        return row_dot(buf5[block_of(rank, rows), 0:triple], weight_v[block_of(index, 512), 0:triple])

    def take_h1(index, total):
        spare[:, block_of(index, 512)] = total

    pl.semaphore_wait(ready, 2)
    end = tensor_sum(spot, h1_part, *tensor, s_send, s_recv, take_h1)
    up.serve(1)
    out.produce(1)
    end()
    spot.release(ready)
    load_w = fetch(w2, weight_v, 2)
    load_t.wait()

    def back1(index, carry):
        where = block_of(index, strip)
        dx = norm_back(line[where, :].astype(F32), sums[0:1, :], spare[where, :], input_grad[where, :], 0)
        input_grad[where, :] = dx
        return carry

    lax.fori_loop(0, rows // strip, back1, 0)
    load_s = fetch(second, spare, 3)
    share = grad_up.shape[0]
    vector_copies, bias_copies = [], []
    for step in range(1, count):
        peer = lax.rem(spot.dp + step, count)
        vector_copies.append(remote(
            vectors.at[:, block_of(peer, share)], vector_in.at[spot.dp], v_send.at[step], v_recv.at[step], peer,
            spot.tensor,
        ))
        bias_copies.append(remote(biases, bias_in.at[spot.dp], b_send.at[step], b_recv.at[step], peer, spot.tensor))
    for copy in vector_copies + bias_copies:
        copy.start()
    vector_in[spot.dp] = vectors[:, block_of(spot.dp, share)]
    bias_in[spot.dp] = biases[...]
    up.serve(2)
    out.produce(2)
    down.settle()
    up.serve(3)
    out.produce(3)
    for copy in vector_copies + bias_copies:
        copy.wait_recv()
    total, bias_total = vector_in[0], bias_in[0]
    for index in range(1, count):
        total = total + vector_in[index]
        bias_total = bias_total + bias_in[index]
    part_sum[...] = total
    bias_sums[...] = bias_total
    part_copies = [
        remote(part_sum, part_in.at[spot.tensor], t_send.at[slot], t_recv.at[slot], spot.dp, peer)
        for slot, peer in enumerate((spot.x_peer, spot.core_peer, spot.far_peer))
    ]
    for copy in part_copies:
        copy.start()
    part_in[spot.tensor] = part_sum[...]
    up.serve(0)
    out.produce(0)
    load_b = fetch(gated_all, buf3, 0)
    load_h = fetch(h1_all, buf4, 1)
    for copy in part_copies:
        copy.wait_recv()
    vector_sums[...] = part_in[0] + part_in[1] + part_in[2] + part_in[3]
    load_h.wait()
    load_b.wait()
    load_w.wait()
    load_s.wait()
    out.serve(1)
    qkv.produce(1)
    out.serve(2)
    qkv.produce(2)
    out.serve(3)
    qkv.produce(3)
    up.settle()
    out.serve(0)
    qkv.produce(0)

    def down_part(rank, index):
        return jnp.dot(buf3[block_of(rank, rows), :], weight_v[:, block_of(index, 512)], preferred_element_type=F32)

    def take_out(index, total):
        where = block_of(index, 512)
        layer_out[:, where] = (spare[:, where] + total + sums[5:6, where]).astype(BF16)

    pl.semaphore_wait(ready, 2)
    end = tensor_sum(spot, down_part, *tensor, s_send, s_recv, take_out)
    out.settle()
    qkv.serve(1)
    end()
    qkv.serve(2)
    qkv.serve(3)
    qkv.serve(0)
    for copy in vector_copies + bias_copies + part_copies:
        copy.wait_send()
    qkv.settle()
    for copy in list(shared["y_busy"].values()) + list(shared["z_busy"].values()):
        copy.wait_send()


def backward_call(heads, count, prefix, sums, tokens, cotangent, weights, saved):
    rows, features = tokens.shape
    length = rows * 4
    share = features // count
    wqkv, wo, w1, w2 = weights
    width, hidden, triple = wo.shape[0], w1.shape[1], wqkv.shape[1]
    outer, inner = split_of(count)
    shape = jax.ShapeDtypeStruct
    hbm = pl.BlockSpec(memory_space=pl.ANY)
    vmem = pl.BlockSpec(memory_space=pltpu.VMEM)
    dma = pltpu.SemaphoreType.DMA
    regular = pltpu.SemaphoreType.REGULAR
    wide = (length, features)
    return pl.pallas_call(
        functools.partial(backward_kernel, heads, count),
        out_shape=[
            shape((rows, features), BF16),
            shape((rows, features), F32),
            shape((share, hidden), F32),
            shape((share, hidden), F32),
            shape((share, width), F32),
            shape((share, triple), F32),
            shape((8, share), F32),
            shape((8, 512), F32),
            shape((outer - 1, share, hidden), BF16),
            shape((outer - 1, share, hidden), BF16),
            shape((outer - 1, share, width), BF16),
            shape((outer - 1, share, triple), BF16),
        ],
        in_specs=[pl.BlockSpec(memory_space=pltpu.SMEM), vmem] + [hbm] * 10 + [vmem] + [hbm] * 4,
        out_specs=[vmem] * 2 + [hbm] * 4 + [vmem] * 2 + [hbm] * 4,
        scratch_shapes=[
            pltpu.VMEM((hidden, features), BF16),
            pltpu.VMEM(wide, BF16),
            pltpu.VMEM(wide, BF16),
            pltpu.VMEM(wide, BF16),
            pltpu.VMEM(wide, BF16),
            pltpu.VMEM(wide, BF16),
            pltpu.VMEM((2, rows, features), BF16),
            pltpu.VMEM((2, rows, features), BF16),
            pltpu.VMEM((rows, features), BF16),
            pltpu.VMEM((rows, features), BF16),
            pltpu.VMEM((outer, share, hidden), BF16),
            pltpu.VMEM((outer, share, hidden), BF16),
            pltpu.VMEM((outer, share, hidden), BF16),
            pltpu.VMEM((2, outer - 1, share, 512), BF16),
            pltpu.VMEM((2, share, 512), F32),
            pltpu.VMEM((rows, features), F32),
            pltpu.VMEM((rows, features), BF16),
            pltpu.VMEM((length, width // heads), F32),
            pltpu.VMEM((length, width // heads), F32),
            pltpu.VMEM((8, features), F32),
            pltpu.VMEM((8, 512), F32),
            pltpu.VMEM((count, 8, share), F32),
            pltpu.VMEM((count, 8, 512), F32),
            pltpu.VMEM((8, share), F32),
            pltpu.VMEM((4, 8, share), F32),
            dma((outer,)),
            dma((outer,)),
            dma((outer,)),
            dma((4, outer)),
            dma((3,)),
            dma((3,)),
            dma((3,)),
            dma((3,)),
            dma((count,)),
            dma((count,)),
            dma((count,)),
            dma((count,)),
            dma((3,)),
            dma((3,)),
            dma((4,)),
            dma((7,)),
            regular,
            regular,
        ],
        compiler_params=pltpu.CompilerParams(
            collective_id=1, has_side_effects=True, vmem_limit_bytes=VMEM_BYTES
        ),
    )(prefix, sums, tokens, cotangent, wqkv, wo, w1, w2, *saved)


def pack_small(features, query_bias, value_bias, up_bias, vectors):
    devices = lax.axis_size("dp")
    me = lax.axis_index("dp")
    rows = []
    for part in vectors:
        start = me * part.shape[0]
        rows.append(lax.dynamic_update_slice(jnp.zeros((features,), F32), part.astype(F32), (start,)))

    def spread_rows(part):
        wide = jnp.zeros((part.shape[0], part.shape[1] * devices), F32)
        return lax.dynamic_update_slice(wide, part.astype(F32), (0, me * part.shape[1])).reshape(-1)

    q = spread_rows(query_bias)
    joint = jnp.concatenate([q, jnp.zeros_like(q), spread_rows(value_bias)])
    rows.append(jnp.pad(joint, (0, features - joint.size)))
    u = spread_rows(up_bias)
    rows.append(jnp.pad(u, (0, features - u.size)))
    return jnp.stack(rows)


def layer_norm(rows, gain, shift):
    center = rows - jnp.mean(rows, axis=-1, keepdims=True)
    spread = jnp.mean(center * center, axis=-1, keepdims=True)
    return center * lax.rsqrt(spread + 1e-05) * gain + shift


def gelu_exact(values):
    return jax.nn.gelu(values, approximate=False)


def head_major(matrix, heads):
    return matrix.reshape(matrix.shape[0], heads, -1).transpose(1, 0, 2)


def row_major(stacked):
    return stacked.transpose(1, 0, 2).reshape(stacked.shape[1], -1)


def masked_scores(q_block, keys, start, prefix_len):
    scores = jnp.einsum("hqd,hkd->hqk", q_block, keys, preferred_element_type=jnp.float32)
    rows = start + lax.broadcasted_iota(jnp.int32, scores.shape[1:], 0)
    cols = lax.broadcasted_iota(jnp.int32, scores.shape[1:], 1)
    seen = (cols <= rows) | (cols < prefix_len)
    return jnp.where(seen[None], scores, -1e30)


def to_blocks(stacked, count):
    heads, length = (stacked.shape[0], stacked.shape[1])
    return stacked.reshape((heads, count, length // count) + stacked.shape[2:]).swapaxes(0, 1)


def from_blocks(blocked):
    count, heads, block = (blocked.shape[0], blocked.shape[1], blocked.shape[2])
    return blocked.swapaxes(0, 1).reshape((heads, count * block) + blocked.shape[3:])


def contract_rows(left, right):
    return jnp.einsum("ld,le->de", left, right, preferred_element_type=jnp.float32)


def times_transpose(left, right):
    return jnp.einsum("le,de->ld", left, right, preferred_element_type=jnp.float32)


def plain(
    tokens,
    prefix,
    query_weight,
    key_weight,
    value_weight,
    out_weight,
    query_bias,
    value_bias,
    up_weight,
    down_weight,
    up_bias,
    norm1_gain,
    norm1_bias,
    norm2_gain,
    norm2_bias,
    out_bias,
    down_bias,
    cotangent,
):
    f32 = jnp.float32
    bf16 = jnp.bfloat16
    devices = lax.axis_size("dp")
    small = (query_bias, value_bias, up_bias, norm1_gain, norm1_bias, norm2_gain, norm2_bias, out_bias, down_bias)
    packed = jnp.concatenate([part.reshape(-1) for part in small])
    packed = lax.all_gather(packed, "dp", axis=0, tiled=False)
    pieces = []
    offset = 0
    for part in small:
        piece = packed[:, offset : offset + part.size].reshape((devices,) + part.shape)
        offset += part.size
        pieces.append(jnp.moveaxis(piece, 0, -2).reshape(part.shape[:-1] + (-1,)))
    bq, bv, b1, g1, n1, g2, n2, bo, b2 = pieces
    wq, wk, wv, wo = (
        lax.all_gather(query_weight, "dp", axis=0, tiled=True),
        lax.all_gather(key_weight, "dp", axis=0, tiled=True),
        lax.all_gather(value_weight, "dp", axis=0, tiled=True),
        lax.all_gather(out_weight, "dp", axis=1, tiled=True),
    )
    w1, w2 = (
        lax.all_gather(up_weight, "dp", axis=0, tiled=True),
        lax.all_gather(down_weight, "dp", axis=1, tiled=True),
    )
    g1f, n1f, g2f, n2f = (g1.astype(f32), n1.astype(f32), g2.astype(f32), n2.astype(f32))
    bof, b2f = (bo.astype(f32), b2.astype(f32))
    heads = bq.shape[0]
    head_size = bq.shape[1]
    scale = head_size ** (-0.5)
    prefix_len = prefix[0]
    xf = tokens.astype(f32)
    h1 = layer_norm(xf, g1f, n1f).astype(bf16)
    rows1 = lax.all_gather(h1, "tensor", axis=0, tiled=True)
    length = rows1.shape[0]
    block = min(512, length)
    count = length // block
    query = (
        (jnp.dot(rows1, wq, preferred_element_type=f32) + bq.astype(f32).reshape(-1)) * scale
    ).astype(bf16)
    keyed = jnp.dot(rows1, wk, preferred_element_type=f32).astype(bf16)
    valued = (jnp.dot(rows1, wv, preferred_element_type=f32) + bv.astype(f32).reshape(-1)).astype(
        bf16
    )
    q_heads = head_major(query, heads)
    k_heads = head_major(keyed, heads)
    v_heads = head_major(valued, heads)
    q_blocks = to_blocks(q_heads, count)
    starts = jnp.arange(count, dtype=jnp.int32) * block

    def forward_block(item):
        q_block, start = item
        scores = masked_scores(q_block, k_heads, start, prefix_len)
        top = jnp.max(scores, axis=-1, keepdims=True)
        expd = jnp.exp(scores - top)
        total = jnp.sum(expd, axis=-1, keepdims=True)
        probs = (expd / total).astype(bf16)
        outv = jnp.einsum("hqk,hkd->hqd", probs, v_heads, preferred_element_type=f32)
        return (outv.astype(bf16), (top + jnp.log(total))[..., 0])

    o_blocks, lse_blocks = lax.map(forward_block, (q_blocks, starts))
    mixed = row_major(from_blocks(o_blocks))
    attn_part = jnp.dot(mixed, wo, preferred_element_type=f32)
    attn_total = lax.psum_scatter(attn_part.astype(bf16), "tensor", scatter_dimension=0, tiled=True).astype(f32)
    second = xf + attn_total + bof
    h2 = layer_norm(second, g2f, n2f).astype(bf16)
    rows2 = lax.all_gather(h2, "tensor", axis=0, tiled=True)
    hidden = jnp.dot(rows2, w1, preferred_element_type=f32) + b1.astype(f32).reshape(-1)
    gated = gelu_exact(hidden).astype(bf16)
    mlp_part = jnp.dot(gated, w2, preferred_element_type=f32)
    mlp_total = lax.psum_scatter(
        mlp_part.astype(jnp.bfloat16), "tensor", scatter_dimension=0, tiled=True
    ).astype(jnp.float32)
    layer_out = (second + mlp_total + b2f).astype(bf16)
    d_out = cotangent.astype(f32)
    g_b2 = jnp.sum(d_out, axis=0)
    d_rows = lax.all_gather(cotangent, "tensor", axis=0, tiled=True)
    d_gated = times_transpose(d_rows, w2)
    d_hidden = jax.vjp(gelu_exact, hidden)[1](d_gated)[0]
    g_b1 = jnp.sum(d_hidden, axis=0).reshape(b1.shape)
    d_hidden_low = d_hidden.astype(bf16)
    d_h2_part = times_transpose(d_hidden_low, w1)
    g_w2 = contract_rows(gated, d_rows)
    g_w1 = contract_rows(rows2, d_hidden_low)
    d_h2 = lax.psum_scatter(d_h2_part.astype(bf16), "tensor", scatter_dimension=0, tiled=True).astype(f32)
    norm2_back = jax.vjp(layer_norm, second, g2f, n2f)[1]
    d_second_ln, g_g2, g_n2 = norm2_back(d_h2)
    d_second = d_out + d_second_ln
    g_bo = jnp.sum(d_second, axis=0)
    d_second_low = d_second.astype(bf16)
    back_rows = lax.all_gather(d_second_low, "tensor", axis=0, tiled=True)
    g_wo = contract_rows(mixed, back_rows)
    d_mixed = times_transpose(back_rows, wo).astype(bf16)
    do_blocks = to_blocks(head_major(d_mixed, heads), count)

    def backward_block(carry, item):
        d_keys, d_vals = carry
        q_block, do_block, lse_block, start = item
        scores = masked_scores(q_block, k_heads, start, prefix_len)
        probs = jnp.exp(scores - lse_block[..., None])
        d_probs = jnp.einsum("hqd,hkd->hqk", do_block, v_heads, preferred_element_type=f32)
        d_vals = d_vals + jnp.einsum(
            "hqk,hqd->hkd", probs.astype(bf16), do_block, preferred_element_type=f32
        )
        inner = jnp.sum(probs * d_probs, axis=-1, keepdims=True)
        d_scores = (probs * (d_probs - inner)).astype(bf16)
        d_query = jnp.einsum("hqk,hkd->hqd", d_scores, k_heads, preferred_element_type=f32)
        d_keys = d_keys + jnp.einsum("hqk,hqd->hkd", d_scores, q_block, preferred_element_type=f32)
        return ((d_keys, d_vals), d_query)

    empty = jnp.zeros(k_heads.shape, f32)
    (d_keys, d_vals), dq_blocks = lax.scan(
        backward_block, (empty, empty), (q_blocks, do_blocks, lse_blocks, starts)
    )
    d_query = row_major(from_blocks(dq_blocks)) * scale
    d_keys = row_major(d_keys)
    d_vals = row_major(d_vals)
    g_bq = jnp.sum(d_query, axis=0).reshape(bq.shape)
    g_bv = jnp.sum(d_vals, axis=0).reshape(bv.shape)
    dq_low, dk_low, dv_low = (d_query.astype(bf16), d_keys.astype(bf16), d_vals.astype(bf16))
    g_wq = contract_rows(rows1, dq_low)
    g_wk = contract_rows(rows1, dk_low)
    g_wv = contract_rows(rows1, dv_low)
    d_h1_part = (
        times_transpose(dq_low, wq) + times_transpose(dk_low, wk) + times_transpose(dv_low, wv)
    )
    d_h1 = lax.psum_scatter(d_h1_part.astype(bf16), "tensor", scatter_dimension=0, tiled=True).astype(f32)
    norm1_back = jax.vjp(layer_norm, xf, g1f, n1f)[1]
    d_input_ln, g_g1, g_n1 = norm1_back(d_h1)
    input_grad = d_second + d_input_ln
    def scatter(part, dim):
        return lax.psum_scatter(part.astype(bf16), "dp", scatter_dimension=dim, tiled=True).astype(f32)

    s_w2, s_w1, s_wo = scatter(g_w2, 1), scatter(g_w1, 0), scatter(g_wo, 1)
    s_wq, s_wk, s_wv = scatter(g_wq, 0), scatter(g_wk, 0), scatter(g_wv, 0)

    def by_device(part):
        return jnp.moveaxis(part.reshape(part.shape[:-1] + (devices, -1)), -2, 0).reshape(devices, -1)

    rows = [by_device(part) for part in (g_bq, g_bv, g_b1, g_g1, g_n1, g_g2, g_n2, g_bo, g_b2)]
    total = lax.psum_scatter(jnp.concatenate(rows, axis=1), "dp", scatter_dimension=0, tiled=True)[0]
    offset = 0
    outs = []
    for part in (query_bias, value_bias, up_bias):
        outs.append(total[offset : offset + part.size].reshape(part.shape))
        offset += part.size
    s_bq, s_bv, s_b1 = outs
    vectors = lax.psum_scatter(
        total[offset:].reshape(6, lax.axis_size("tensor"), -1), "tensor", scatter_dimension=1, tiled=True
    ).reshape(6, -1)
    s_g1, s_n1, s_g2, s_n2, s_bo, s_b2 = (vectors[index] for index in range(6))
    return (
        layer_out,
        input_grad,
        s_wq,
        s_wk,
        s_wv,
        s_wo,
        s_bq,
        s_bv,
        s_w1,
        s_w2,
        s_b1,
        s_g1,
        s_n1,
        s_g2,
        s_n2,
        s_bo,
        s_b2,
    )


def fast(
    tokens,
    prefix,
    query_weight,
    key_weight,
    value_weight,
    out_weight,
    query_bias,
    value_bias,
    up_weight,
    down_weight,
    up_bias,
    norm1_gain,
    norm1_bias,
    norm2_gain,
    norm2_bias,
    out_bias,
    down_bias,
    cotangent,
):
    devices = lax.axis_size("dp")
    me = lax.axis_index("dp")
    heads = query_bias.shape[0]
    small = pack_small(
        tokens.shape[1], query_bias, value_bias, up_bias,
        (norm1_gain, norm1_bias, norm2_gain, norm2_bias, out_bias, down_bias),
    )
    results = forward_call(
        heads, devices, prefix, tokens, cotangent, small,
        jnp.concatenate([query_weight, key_weight, value_weight], axis=1), out_weight, up_weight, down_weight,
    )
    layer_out, input_grad, g_w2, g_w1, g_wo, g_qkv, vectors, biases, *_ = backward_call(
        heads, devices, prefix, results[-1], tokens, cotangent, results[:4], results[4:-1]
    )
    g_wq, g_wk, g_wv = jnp.split(g_qkv, 3, axis=1)
    vectors = vectors.reshape(8, lax.axis_size("tensor"), -1)
    vectors = lax.dynamic_index_in_dim(vectors, lax.axis_index("tensor"), axis=1, keepdims=False)

    def own(flat, part):
        whole = flat.reshape(part.shape[0], -1)
        return lax.dynamic_slice_in_dim(whole, me * part.shape[1], part.shape[1], axis=1)

    width = out_weight.shape[0]
    up_size = up_bias.size * devices
    g_b1 = own(biases[: up_size // 512].reshape(-1), up_bias)
    g_bq = own(biases[4, :width], query_bias)
    g_bv = own(biases[5, :width], value_bias)
    return (
        layer_out, input_grad, g_wq, g_wk, g_wv, g_wo.T, g_bq, g_bv, g_w1, g_w2.T, g_b1,
        vectors[0], vectors[1], vectors[2], vectors[3], vectors[4], vectors[5],
    )


def local(*args):
    tokens, query_weight, up_weight = args[0], args[2], args[8]
    devices = lax.axis_size("dp")
    features = tokens.shape[1]
    share = features // devices
    fits = (
        lax.axis_size("tensor") == 4
        and devices == 8
        and share % 128 == 0
        and tokens.shape[0] == 256
        and query_weight.shape[1] == 512
        and features == 2048
        and up_weight.shape[1] == 2048
    )
    return fast(*args) if fits else plain(*args)


def solution(mesh):
    in_specs = (
        P(("dp", "tensor"), None),
        P("dp"),
        P("dp", "tensor"),
        P("dp", "tensor"),
        P("dp", "tensor"),
        P("tensor", "dp"),
        P("tensor", "dp"),
        P("tensor", "dp"),
        P("dp", "tensor"),
        P("tensor", "dp"),
        P("tensor", "dp"),
        P("dp"),
        P("dp"),
        P("dp"),
        P("dp"),
        P("dp"),
        P("dp"),
        P(("dp", "tensor"), None),
    )
    out_specs = (
        P(("dp", "tensor"), None),
        P(("dp", "tensor"), None),
        P("dp", "tensor"),
        P("dp", "tensor"),
        P("dp", "tensor"),
        P("tensor", "dp"),
        P("tensor", "dp"),
        P("tensor", "dp"),
        P("dp", "tensor"),
        P("tensor", "dp"),
        P("tensor", "dp"),
        P(("dp", "tensor")),
        P(("dp", "tensor")),
        P(("dp", "tensor")),
        P(("dp", "tensor")),
        P(("dp", "tensor")),
        P(("dp", "tensor")),
    )
    return jax.shard_map(local, mesh=mesh, in_specs=in_specs, out_specs=out_specs, check_vma=False)
```

```python
import functools

import jax
import jax.numpy as jnp
from jax import lax
from jax.experimental import pallas as pl
from jax.experimental.pallas import tpu as pltpu
from jax.sharding import PartitionSpec as P

MESH = pl.DeviceIdType.MESH
F32 = jnp.float32
BF16 = jnp.bfloat16
PREFIX_TOP = 512
VMEM_BYTES = 67043328


def split_of(count):
    inner = 1
    for size in range(1, count + 1):
        if size * size <= count and count % size == 0:
            inner = size
    return count // inner, inner


def remote(source, target, send_sem, recv_sem, dp, tensor):
    return pltpu.make_async_remote_copy(
        src_ref=source,
        dst_ref=target,
        send_sem=send_sem,
        recv_sem=recv_sem,
        device_id=(dp, tensor),
        device_id_type=MESH,
    )


def block_of(index, size):
    return pl.ds(pl.multiple_of(index * size, size), size)


class Spot:
    def __init__(self, count):
        self.outer, self.inner = split_of(count)
        self.count = count
        self.dp = lax.axis_index("dp")
        self.tensor = lax.axis_index("tensor")
        self.row = lax.div(self.dp, self.inner)
        self.column = lax.rem(self.dp, self.inner)
        self.core_peer = self.tensor + 1 - 2 * lax.rem(self.tensor, 2)
        self.x_peer = lax.rem(self.tensor + 2, 4)
        self.far_peer = lax.rem(self.core_peer + 2, 4)

    def across(self, step):
        return lax.rem(self.row + step, self.outer) * self.inner + self.column

    def beside(self, step, row=None):
        return (self.row if row is None else row) * self.inner + lax.rem(self.column + step, self.inner)

    def meet(self, far=False):
        barrier = pltpu.get_barrier_semaphore()
        for step in range(1, self.count):
            pl.semaphore_signal(
                barrier, inc=1, device_id=(lax.rem(self.dp + step, self.count), self.tensor), device_id_type=MESH
            )
        for peer in (self.core_peer, self.x_peer) + ((self.far_peer,) if far else ()):
            pl.semaphore_signal(barrier, inc=1, device_id=(self.dp, peer), device_id_type=MESH)
        pl.semaphore_wait(barrier, self.count + 1 + far)

    def release(self, ready):
        for peer in (self.core_peer, self.x_peer):
            pl.semaphore_signal(ready, inc=1, device_id=(self.dp, peer), device_id_type=MESH)


class Spread:
    AHEAD = 3

    def __init__(self, spot, pieces, late, own_at, sems):
        self.spot, self.pieces, self.late, self.sems = spot, pieces, late, sems
        self.flows = [(piece, 0) for piece in range(len(pieces)) if piece != late] + [(late, 0), (late, 1)]
        self.own_at = own_at
        self.order = (2, jnp.where(spot.row == 0, 3, 1), jnp.where(spot.row == 0, 1, 3))
        self.sent = []
        self.todo = [(flow, place) for flow in range(len(self.flows)) for place in range(3)]
        for piece in own_at[None]:
            self.send_own(piece)
        for flow in range(self.AHEAD):
            self.send_rows(flow)

    def owner(self, row, side):
        return row * 2 + lax.rem(self.spot.column + side, 2)

    def launch(self, condition, copy):
        if condition is None:
            copy().start()
        else:
            pl.when(condition)(lambda: copy().start())
        self.sent.append((condition, copy))

    def along(self, flow, step, source_row, target_row, send_slot):
        piece, side = self.flows[flow]
        source, target = self.pieces[piece]
        place = target(self.owner(source_row, side))
        if source_row is not self.spot.row or side:
            source = place
        return remote(
            source, place, self.sems[0].at[flow, send_slot], self.sems[1].at[flow, step],
            target_row * 2 + self.spot.column, self.spot.tensor,
        )

    def send_rows(self, flow):
        row = self.spot.row
        if self.flows[flow][1]:
            self.beside(self.late, 0, row).wait_recv()
        for step, condition in ((2, None), (1, row != 3), (3, row != 0)):
            self.launch(
                condition,
                functools.partial(self.along, flow, step, row, lax.rem(row + step, 4), step),
            )

    def hand_over(self, flow):
        row = self.spot.row
        self.launch(
            (row == 1) | (row == 2),
            lambda: self.along(flow, 2 * row - 1, lax.rem(row + 2, 4), (row - 1) * 3, 0),
        )

    def beside(self, piece, step, source_row):
        spot = self.spot
        source, target = self.pieces[piece]
        place = target(self.owner(source_row, 0))
        if source_row is not spot.row:
            source = place
        return remote(
            source, place, self.sems[2].at[piece, step], self.sems[3].at[piece, step], spot.beside(1), spot.tensor
        )

    def beside_arrival(self, piece, step, source_row):
        source, target = self.pieces[piece]
        return remote(
            source, target(self.owner(source_row, 1)), self.sems[2].at[piece, step], self.sems[3].at[piece, step],
            self.spot.beside(1), self.spot.tensor,
        )

    def send_own(self, piece):
        self.launch(None, functools.partial(self.beside, piece, 0, self.spot.row))

    def forward(self, count):
        for _ in range(count):
            if not self.todo:
                return
            flow, place = self.todo.pop(0)
            step = self.order[place]
            row = lax.rem(self.spot.row + 4 - step, 4)
            self.along(flow, step, row, self.spot.row, 0).wait_recv()
            if place == 0:
                self.hand_over(flow)
            piece = self.flows[flow][0]
            if piece != self.late:
                self.launch(None, functools.partial(self.beside, piece, step, row))
            if place == 2:
                if flow + self.AHEAD < len(self.flows):
                    self.send_rows(flow + self.AHEAD)
                for own in self.own_at.get(flow, ()):
                    self.send_own(own)

    def arrived(self, piece):
        while self.todo and self.flows[self.todo[0][0]][0] <= piece:
            self.forward(1)
        if piece != self.late:
            for step in range(4):
                self.beside_arrival(piece, step, lax.rem(self.spot.row + 4 - step, 4)).wait_recv()

    def finish(self):
        for condition, copy in self.sent:
            if condition is None:
                copy().wait_send()
            else:
                pl.when(condition)(lambda copy=copy: copy().wait_send())


class TensorGather:
    def __init__(self, spot, own, full, rows, send, recv):
        self.spot, self.full, self.rows, self.send, self.recv = spot, full, rows, send, recv
        place = self.at(spot.tensor)
        self.to_x = remote(own, place, send.at[0], recv.at[0], spot.dp, spot.x_peer)
        self.to_core = remote(own, place, send.at[1], recv.at[1], spot.dp, spot.core_peer)
        self.to_x.start()
        self.to_core.start()

    def at(self, index):
        return self.full.at[block_of(index, self.rows)]

    def pass_on(self):
        self.to_x.wait_recv()
        place = self.at(self.spot.x_peer)
        self.on = remote(place, place, self.send.at[2], self.recv.at[2], self.spot.dp, self.spot.core_peer)
        self.on.start()

    def finish(self):
        self.to_core.wait_recv()
        self.on.wait_recv()
        for copy in (self.to_x, self.to_core, self.on):
            copy.wait_send()


def tensor_sum(spot, product, core_send, core_recv, x_send, x_recv, send, recv, finish):
    width = core_send.shape[2]
    chunk = 512
    count = width // chunk

    def fill(rank, target):
        def body(index, carry):
            target[:, block_of(index, chunk)] = product(rank, index).astype(BF16)
            return carry

        lax.fori_loop(0, count, body, 0)

    copies = []
    for slot, rank in enumerate((spot.far_peer, spot.core_peer)):
        fill(rank, core_send.at[slot])
        copy = remote(core_send.at[slot], core_recv.at[slot], send.at[slot], recv.at[slot], spot.dp, spot.core_peer)
        copy.start()
        copies.append(copy)
    copies[0].wait_recv()

    def join(index, carry):
        where = block_of(index, chunk)
        x_send[:, where] = (product(spot.x_peer, index) + core_recv[0, :, where].astype(F32)).astype(BF16)
        return carry

    lax.fori_loop(0, count, join, 0)
    over = remote(x_send, x_recv, send.at[2], recv.at[2], spot.dp, spot.x_peer)
    over.start()
    copies[1].wait_recv()

    def end():
        over.wait_recv()

        def last(index, carry):
            where = block_of(index, chunk)
            total = product(spot.tensor, index) + core_recv[1, :, where].astype(F32) + x_recv[:, where].astype(F32)
            finish(index, total)
            return carry

        lax.fori_loop(0, count, last, 0)
        for copy in copies + [over]:
            copy.wait_send()

    return end


def normal_parts(rows):
    center = rows - jnp.mean(rows, axis=-1, keepdims=True)
    spread = jnp.mean(center * center, axis=-1, keepdims=True)
    return center, lax.rsqrt(spread + 1e-05)


def forward_kernel(
    heads,
    count,
    prefix,
    tokens,
    cotangent,
    small,
    qkv_shard,
    out_shard,
    up_shard,
    down_shard,
    wqkv,
    wo,
    w1,
    w2,
    h1_all,
    d_rows,
    qkv_all,
    mixed_all,
    lse_all,
    second,
    h2_all,
    gated_all,
    slope_all,
    sums,
    smalls,
    h1v,
    wqkv_v,
    qkv_v,
    mixed_v,
    lse_v,
    wo_v,
    core_send,
    core_recv,
    x_send,
    x_recv,
    h2v,
    w1_v,
    gated_v,
    slope_v,
    small_send,
    small_recv,
    z_send,
    z_recv,
    y_send,
    y_recv,
    g_send,
    g_recv,
    s_send,
    s_recv,
    local_sem,
):
    spot = Spot(count)
    rows, features = tokens.shape
    length = h1v.shape[0]
    depth = qkv_shard.shape[0]
    width = wo_v.shape[0]
    hidden = up_shard.shape[1]
    half = depth // 2
    tall = hidden // 2
    pieces = [
        (qkv_shard.at[pl.ds(part * half, half)],
         lambda owner, part=part: wqkv.at[block_of(owner * 2 + part, half)])
        for part in range(2)
    ]
    pieces.append((out_shard, lambda owner: wo.at[:, block_of(owner, depth)]))
    pieces += [
        (up_shard.at[:, pl.ds(part * tall, tall)],
         lambda owner, part=part: w1.at[block_of(owner, depth), pl.ds(part * tall, tall)])
        for part in range(2)
    ]
    pieces += [
        (down_shard.at[pl.ds(part * tall, tall)],
         lambda owner, part=part: w2.at[pl.ds(part * tall, tall), block_of(owner, depth)])
        for part in range(2)
    ]
    locals_ = []

    def keep(source, target):
        copy = pltpu.make_async_copy(source, target, local_sem.at[len(locals_)])
        copy.start()
        locals_.append(copy)

    spot.meet()
    small_copies = []
    for step in range(1, count):
        copy = remote(
            small, smalls.at[spot.dp], small_send.at[step], small_recv.at[step],
            lax.rem(spot.dp + step, count), spot.tensor,
        )
        copy.start()
        small_copies.append(copy)
    spread = Spread(
        spot, pieces, 6, {None: (0, 1, 2, 3), 0: (4,), 1: (6,), 2: (5,)}, (z_send, z_recv, y_send, y_recv)
    )
    for source, target in pieces:
        keep(source, target(spot.dp))
    smalls[spot.dp] = small[...]
    for step in range(1, count):
        owner = lax.rem(spot.dp + count - step, count)
        remote(
            small, smalls.at[owner], small_send.at[step], small_recv.at[step], spot.dp, spot.core_peer
        ).wait_recv()
    sums[...] = jnp.zeros_like(sums)
    joint = smalls[0, 0:24, :]
    for index in range(1, count):
        joint = joint + smalls[index, 0:24, :]
    lanes = 128
    for head in range(heads):
        sums[6:7, head * lanes : (head + 1) * lanes] = joint[head : head + 1, :]
        start = 2 * width + head * lanes
        sums[6:7, start : start + lanes] = joint[4 + head : 5 + head, :]
    for line in range(hidden // lanes):
        sums[7:8, line * lanes : (line + 1) * lanes] = joint[8 + line : 9 + line, :]
    for owner in range(count):
        for part in range(2):
            start = owner * depth + part * lanes
            sums[0:6, start : start + lanes] = smalls[owner, 24 + 8 * part : 30 + 8 * part, :]

    strip = 32
    base = spot.tensor * rows

    def norm1(index, carry):
        where = block_of(index, strip)
        center, scale = normal_parts(tokens[where, :].astype(F32))
        h1v[pl.ds(pl.multiple_of(base + index * strip, strip), strip), :] = (
            center * scale * sums[0:1, :] + sums[1:2, :]
        ).astype(BF16)
        return carry

    lax.fori_loop(0, rows // strip, norm1, 0)
    gather1 = TensorGather(spot, h1v.at[block_of(spot.tensor, rows)], h1v, rows, g_send.at[0], g_recv.at[0])
    gather_d = TensorGather(spot, cotangent, d_rows, rows, g_send.at[1], g_recv.at[1])
    keep(cotangent, d_rows.at[block_of(spot.tensor, rows)])
    spread.forward(1)
    gather1.pass_on()
    spread.forward(2)
    gather_d.pass_on()
    gather1.finish()
    keep(h1v, h1_all)
    spread.forward(6)
    spread.arrived(0)
    spread.arrived(1)
    for copy in locals_[:2]:
        copy.wait()
    load = pltpu.make_async_copy(wqkv, wqkv_v, local_sem.at[14])
    load.start()
    load.wait()

    def project(index, carry):
        where = block_of(index, rows)
        for part in range(3):
            lanes = slice(part * width, (part + 1) * width)
            value = jnp.dot(h1v[where, :], wqkv_v[:, lanes], preferred_element_type=F32) + sums[6:7, lanes]
            if part == 0:
                value = value * (width // heads) ** -0.5
            qkv_v[where, lanes] = value.astype(BF16)
        return carry

    lax.fori_loop(0, length // rows, project, 0)
    keep(qkv_v, qkv_all)
    spread.forward(3)
    size = width // heads
    limit = prefix[0]
    bench = 256

    for block in range(length // bench):
        reach = min(length, max((block + 1) * bench, PREFIX_TOP))
        span = slice(block * bench, (block + 1) * bench)

        def attend(head, carry, block=block, span=span, reach=reach):
            line = block * bench + lax.broadcasted_iota(jnp.int32, (bench, reach), 0)
            place = lax.broadcasted_iota(jnp.int32, (bench, reach), 1)
            seen = (place <= line) | (place < limit)
            q = qkv_v[span, block_of(head, size)]
            k = qkv_v[0:reach, pl.ds(pl.multiple_of(width + head * size, size), size)]
            v = qkv_v[0:reach, pl.ds(pl.multiple_of(2 * width + head * size, size), size)]
            scores = lax.dot_general(q, k, (((1,), (1,)), ((), ())), preferred_element_type=F32)
            scores = jnp.where(seen, scores, -1e30)
            top = jnp.max(scores, axis=-1, keepdims=True)
            expd = jnp.exp(scores - top)
            total = jnp.sum(expd, axis=-1, keepdims=True)
            probs = (expd * (1.0 / total)).astype(BF16)
            mixed_v[span, block_of(head, size)] = jnp.dot(probs, v, preferred_element_type=F32).astype(BF16)
            lse_v[head, span, :] = jnp.broadcast_to(top + jnp.log(total), (bench, 128))
            return carry

        lax.fori_loop(0, heads, attend, 0)
        if block == 2:
            spread.forward(2)
    keep(mixed_v, mixed_all)
    keep(lse_v, lse_all)
    spread.forward(1)
    spread.arrived(2)
    locals_[2].wait()
    load = pltpu.make_async_copy(wo, wo_v, local_sem.at[14])
    load.start()
    load.wait()

    def out_part(rank, index):
        return jnp.dot(mixed_v[block_of(rank, rows), :], wo_v[:, block_of(index, 512)], preferred_element_type=F32)

    def take_second(index, total):
        where = block_of(index, 512)
        second[:, where] = tokens[:, where].astype(F32) + total + sums[4:5, where]

    end = tensor_sum(
        spot, out_part, core_send, core_recv, x_send, x_recv, s_send.at[0], s_recv.at[0], take_second
    )
    end()

    def norm2(index, carry):
        where = block_of(index, strip)
        center, scale = normal_parts(second[where, :])
        h2v[pl.ds(pl.multiple_of(base + index * strip, strip), strip), :] = (
            center * scale * sums[2:3, :] + sums[3:4, :]
        ).astype(BF16)
        return carry

    lax.fori_loop(0, rows // strip, norm2, 0)
    gather2 = TensorGather(spot, h2v.at[block_of(spot.tensor, rows)], h2v, rows, g_send.at[2], g_recv.at[2])
    gather2.pass_on()
    spread.forward(3)
    gather2.finish()
    gather_d.finish()
    keep(h2v, h2_all)
    stored = []
    for part in range(2):
        spread.arrived(3 + part)
        locals_[3 + part].wait()
        lanes_of = pl.ds(part * tall, tall)
        load = pltpu.make_async_copy(w1.at[:, lanes_of], w1_v.at[:, lanes_of], local_sem.at[14])
        load.start()
        load.wait()
        for block in range(length // rows):
            slot = block % 2
            if len(stored) >= 2:
                stored[-2].wait()

            def lift(index, carry, block=block, slot=slot, part=part):
                where = block_of(part * (tall // 512) + index, 512)
                u = jnp.dot(
                    h2v[block * rows : (block + 1) * rows, :], w1_v[:, where], preferred_element_type=F32
                ) + sums[7:8, where]
                below = 0.5 * (1.0 + lax.erf(u * 0.7071067811865476))
                gated_v[block * rows : (block + 1) * rows, where] = (u * below).astype(BF16)
                slope_v[slot, :, block_of(index, 512)] = below + u * (0.3989422804014327 * jnp.exp(-0.5 * u * u))
                return carry

            lax.fori_loop(0, tall // 512, lift, 0)
            copy = pltpu.make_async_copy(
                slope_v.at[slot], slope_all.at[pl.ds(block * rows, rows), lanes_of], local_sem.at[15 + slot]
            )
            copy.start()
            stored.append(copy)
        if part == 0:
            spread.forward(3)
    keep(gated_v, gated_all)
    spread.arrived(6)
    spread.arrived(5)
    spread.finish()
    for copy in small_copies:
        copy.wait_send()
    for copy in locals_[5:] + stored[-2:]:
        copy.wait()


def forward_call(heads, count, prefix, tokens, cotangent, small, qkv_shard, out_shard, up_shard, down_shard):
    rows, features = tokens.shape
    length = rows * 4
    depth, triple = qkv_shard.shape
    width = out_shard.shape[0]
    hidden = up_shard.shape[1]
    outer, inner = split_of(count)
    shape = jax.ShapeDtypeStruct
    hbm = pl.BlockSpec(memory_space=pl.ANY)
    vmem = pl.BlockSpec(memory_space=pltpu.VMEM)
    dma = pltpu.SemaphoreType.DMA
    pieces = 7
    return pl.pallas_call(
        functools.partial(forward_kernel, heads, count),
        out_shape=[
            shape((features, triple), BF16),
            shape((width, features), BF16),
            shape((features, hidden), BF16),
            shape((hidden, features), BF16),
            shape((length, features), BF16),
            shape((length, features), BF16),
            shape((length, triple), BF16),
            shape((length, width), BF16),
            shape((heads, length, 128), F32),
            shape((rows, features), F32),
            shape((length, features), BF16),
            shape((length, hidden), BF16),
            shape((length, hidden), F32),
            shape((8, features), F32),
        ],
        in_specs=[pl.BlockSpec(memory_space=pltpu.SMEM)] + [vmem] * 7,
        out_specs=[hbm] * 9 + [vmem] + [hbm] * 3 + [vmem],
        scratch_shapes=[
            pltpu.VMEM((count, 40, 128), F32),
            pltpu.VMEM((length, features), BF16),
            pltpu.VMEM((features, triple), BF16),
            pltpu.VMEM((length, triple), BF16),
            pltpu.VMEM((length, width), BF16),
            pltpu.VMEM((heads, length, 128), F32),
            pltpu.VMEM((width, features), BF16),
            pltpu.VMEM((2, rows, features), BF16),
            pltpu.VMEM((2, rows, features), BF16),
            pltpu.VMEM((rows, features), BF16),
            pltpu.VMEM((rows, features), BF16),
            pltpu.VMEM((length, features), BF16),
            pltpu.VMEM((features, hidden), BF16),
            pltpu.VMEM((length, hidden), BF16),
            pltpu.VMEM((2, rows, hidden // 2), F32),
            dma((count,)),
            dma((count,)),
            dma((pieces + 1, outer)),
            dma((pieces + 1, outer)),
            dma((pieces, outer)),
            dma((pieces, outer)),
            dma((3, 3)),
            dma((3, 3)),
            dma((1, 3)),
            dma((1, 3)),
            dma((17,)),
        ],
        compiler_params=pltpu.CompilerParams(
            collective_id=0, has_side_effects=True, vmem_limit_bytes=VMEM_BYTES
        ),
    )(prefix, tokens, cotangent, small, qkv_shard, out_shard, up_shard, down_shard)
class Reduce:
    def __init__(self, spot, left, right, lanes, landing, target, shared, index, last):
        self.spot, self.left, self.right, self.lanes = spot, left, right, lanes
        self.landing, self.target, self.shared, self.index, self.last = landing, target, shared, index, last
        self.width = lanes.stop - lanes.start
        self.share = target.shape[0]
        self.stepped = {}
        self.held = False

    def block(self, owner, take):
        turned = jnp.transpose(self.left[:, block_of(owner, self.share)])
        for start in range(0, self.width, 512):
            source = self.right[:, self.lanes.start + start : self.lanes.start + start + 512]
            take(slice(start, start + 512), jnp.dot(turned, source, preferred_element_type=F32))

    def y_copy(self, step):
        shared = self.shared
        area = pl.ds(0, self.width)
        return remote(
            shared["y_out"].at[step, :, area], shared["y_in"].at[step, :, area], shared["y_send"].at[step],
            shared["y_recv"].at[step], self.spot.beside(1), self.spot.tensor,
        )

    def z_copy(self, step):
        shared = self.shared
        return remote(
            shared["z_out"].at[step, :, pl.ds(0, self.width)], self.landing.at[step - 1],
            shared["z_send"].at[step], shared["z_recv"].at[self.index, step], self.spot.across(step),
            self.spot.tensor,
        )

    def produce(self, step):
        shared, spot = self.shared, self.spot
        row = lax.rem(spot.row + step, spot.outer)
        if step in shared["y_busy"]:
            shared["y_busy"].pop(step).wait_send()

        def take(where, value):
            shared["y_out"][step, :, where] = value.astype(BF16)

        self.block(spot.beside(1, row), take)
        if self.index > 0:
            pl.semaphore_wait(shared["credit"], 1)
        copy = self.y_copy(step)
        copy.start()
        shared["y_busy"][step] = copy

    def hold(self):
        self.held = True
        for step in range(self.spot.outer):

            def take(where, value, step=step):
                self.shared["z_out"][step, :, where] = value.astype(BF16)

            self.block(self.spot.across(step), take)

    def serve(self, step):
        shared, spot = self.shared, self.spot
        self.y_copy(step).wait_recv()
        if step in shared["z_busy"]:
            shared["z_busy"].pop(step).wait_send()
        y_in, z_out = shared["y_in"], shared["z_out"]
        if self.held:
            for start in range(0, self.width, 512):
                where = slice(start, start + 512)
                z_out[step, :, where] = (z_out[step, :, where].astype(F32) + y_in[step, :, where].astype(F32)).astype(BF16)
        else:

            def take(where, value):
                z_out[step, :, where] = (value + y_in[step, :, where].astype(F32)).astype(BF16)

            self.block(spot.across(step), take)
        if not self.last:
            pl.semaphore_signal(
                shared["credit"], inc=1, device_id=(spot.beside(1), spot.tensor), device_id_type=MESH
            )
        if step:
            copy = self.z_copy(step)
            copy.start()
            shared["z_busy"][step] = copy

    def settle(self):
        shared, spot = self.shared, self.spot
        for step in range(1, spot.outer):
            self.z_copy(step).wait_recv()
        loads, stores = [], []
        chunks = self.width // 512
        for chunk in range(chunks):
            loads.append(pltpu.make_async_copy(
                self.landing.at[:, :, pl.ds(chunk * 512, 512)], shared["z_stage"].at[chunk % 2],
                shared["stage_sem"].at[chunk % 2],
            ))
            stores.append(pltpu.make_async_copy(
                shared["o_stage"].at[chunk % 2], self.target.at[:, pl.ds(chunk * 512, 512)],
                shared["stage_sem"].at[2 + chunk % 2],
            ))
        loads[0].start()
        for chunk in range(chunks):
            loads[chunk].wait()
            if chunk + 1 < chunks:
                loads[chunk + 1].start()
            if chunk >= 2:
                stores[chunk - 2].wait()
            total = shared["z_out"][0, :, chunk * 512 : (chunk + 1) * 512].astype(F32)
            for step in range(spot.outer - 1):
                total = total + shared["z_stage"][chunk % 2, step].astype(F32)
            shared["o_stage"][chunk % 2] = total
            stores[chunk].start()
        for store in stores[-2:]:
            store.wait()


def row_dot(left, right):
    return lax.dot_general(left, right, (((1,), (1,)), ((), ())), preferred_element_type=F32)


def backward_kernel(
    heads,
    count,
    prefix,
    sums,
    tokens,
    cotangent,
    wqkv,
    wo,
    w1,
    w2,
    h1_all,
    d_rows,
    qkv_all,
    mixed_all,
    lse_v,
    second,
    h2_all,
    gated_all,
    slope_all,
    layer_out,
    input_grad,
    grad_down,
    grad_up,
    grad_out,
    grad_qkv,
    vector_sums,
    bias_sums,
    land_down,
    land_up,
    land_out,
    land_qkv,
    weight_v,
    buf1,
    buf2,
    buf3,
    buf4,
    buf5,
    core_send,
    core_recv,
    x_send,
    x_recv,
    y_in,
    y_out,
    z_out,
    z_stage,
    o_stage,
    spare,
    line,
    dk_sum,
    dv_sum,
    vectors,
    biases,
    vector_in,
    bias_in,
    part_sum,
    part_in,
    y_send,
    y_recv,
    z_send,
    z_recv,
    g_send,
    g_recv,
    s_send,
    s_recv,
    v_send,
    v_recv,
    b_send,
    b_recv,
    t_send,
    t_recv,
    stage_sem,
    load_sem,
    credit,
    ready,
):
    spot = Spot(count)
    rows, features = line.shape
    length = buf1.shape[0]
    width = wo.shape[0]
    hidden = w1.shape[1]
    triple = 3 * width
    size = width // heads
    scale = size ** -0.5
    tail = slice(triple, triple + width)
    shared = {
        "y_in": y_in, "y_out": y_out, "z_out": z_out, "z_stage": z_stage, "o_stage": o_stage, "y_send": y_send,
        "y_recv": y_recv, "z_send": z_send, "z_recv": z_recv, "credit": credit, "stage_sem": stage_sem,
        "y_busy": {}, "z_busy": {},
    }
    down = Reduce(spot, buf1, buf2, slice(0, hidden), land_down, grad_down, shared, 0, False)
    up = Reduce(spot, buf4, buf3, slice(0, hidden), land_up, grad_up, shared, 1, False)
    out = Reduce(spot, buf1, buf2, tail, land_out, grad_out, shared, 2, False)
    qkv = Reduce(spot, buf4, buf5, slice(0, triple), land_qkv, grad_qkv, shared, 3, True)

    def fetch(source, target, slot):
        copy = pltpu.make_async_copy(source, target, load_sem.at[slot])
        copy.start()
        return copy

    load_a = fetch(d_rows, buf1, 0)
    load_b = fetch(gated_all, buf2, 1)
    load_w = fetch(w2, weight_v, 2)
    slopes = [fetch(slope_all.at[pl.ds(part * rows, rows)], (spare, input_grad)[part % 2], 3 + part % 2) for part in range(2)]
    load_h = fetch(h2_all, buf4, 5)
    load_c = fetch(cotangent, line, 6)
    spot.meet(True)
    vectors[...] = jnp.zeros_like(vectors)
    biases[...] = jnp.zeros_like(biases)
    load_a.wait()
    load_b.wait()
    order = list(range(1, spot.outer)) + [0]
    for step in order:
        down.produce(step)
    load_w.wait()
    for part in range(length // rows):
        held = (spare, input_grad)[part % 2]
        slopes[part].wait()

        def lower(index, carry, part=part, held=held):
            where = block_of(index, 512)
            span = slice(part * rows, (part + 1) * rows)
            du = row_dot(buf1[span, :], weight_v[where, :]) * held[:, where]
            biases[pl.ds(index, 1), :] += jnp.sum(du, axis=0, keepdims=True)
            buf3[span, where] = du.astype(BF16)
            return carry

        lax.fori_loop(0, hidden // 512, lower, 0)
        if part + 2 < length // rows:
            slopes.append(fetch(slope_all.at[pl.ds((part + 2) * rows, rows)], held, 3 + part % 2))
    load_w = fetch(w1, weight_v, 2)
    load_s = fetch(second, spare, 3)
    down.hold()
    load_q = fetch(qkv_all, buf2.at[:, pl.ds(0, triple)], 0)
    load_m = fetch(mixed_all, buf2.at[:, pl.ds(triple, width)], 1)
    load_w.wait()
    load_h.wait()

    def h2_part(rank, index):
        return row_dot(buf3[block_of(rank, rows), :], weight_v[block_of(index, 512), :])

    def take_h2(index, total):
        input_grad[:, block_of(index, 512)] = total

    tensor = (core_send, core_recv, x_send, x_recv)
    end = tensor_sum(spot, h2_part, *tensor, s_send, s_recv, take_h2)
    down.serve(1)
    up.produce(1)
    down.serve(2)
    up.produce(2)
    end()
    spot.release(ready)
    load_o = fetch(wo, weight_v.at[pl.ds(0, width)], 2)
    load_s.wait()
    load_c.wait()
    strip = 32
    base = spot.tensor * rows

    def norm_back(rows_of, gain, grads, keep, first):
        center, inverse = normal_parts(rows_of)
        normal = center * inverse
        vectors[first : first + 1, :] += jnp.sum(grads * normal, axis=0, keepdims=True)
        vectors[first + 1 : first + 2, :] += jnp.sum(grads, axis=0, keepdims=True)
        scaled = grads * gain
        mean = jnp.mean(scaled, axis=-1, keepdims=True)
        slope = jnp.mean(scaled * normal, axis=-1, keepdims=True)
        return keep + inverse * (scaled - mean - normal * slope)

    def back2(index, carry):
        where = block_of(index, strip)
        dy = line[where, :].astype(F32)
        dx = norm_back(spare[where, :], sums[2:3, :], input_grad[where, :], dy, 2)
        vectors[4:5, :] += jnp.sum(dx, axis=0, keepdims=True)
        vectors[5:6, :] += jnp.sum(dy, axis=0, keepdims=True)
        input_grad[where, :] = dx
        buf1[pl.ds(pl.multiple_of(base + index * strip, strip), strip), :] = dx.astype(BF16)
        return carry

    lax.fori_loop(0, rows // strip, back2, 0)
    gather = TensorGather(spot, buf1.at[block_of(spot.tensor, rows)], buf1, rows, g_send, g_recv)
    load_t = fetch(tokens, line, 6)
    down.serve(3)
    up.produce(3)
    gather.pass_on()
    load_o.wait()
    gather.finish()
    load_q.wait()
    load_m.wait()

    def mix_back(index, carry):
        where = block_of(index, rows)
        buf5[where, tail] = row_dot(buf1[where, :], weight_v[0:width, :]).astype(BF16)
        return carry

    lax.fori_loop(0, length // rows, mix_back, 0)
    load_w = fetch(wqkv, weight_v.at[:, pl.ds(0, triple)], 2)
    limit = prefix[0]
    bench = 256

    def attend(head, carry):
        q_at = block_of(head, size)
        k_at = pl.ds(pl.multiple_of(width + head * size, size), size)
        v_at = pl.ds(pl.multiple_of(2 * width + head * size, size), size)
        o_at = pl.ds(pl.multiple_of(triple + head * size, size), size)
        dk_sum[...] = jnp.zeros_like(dk_sum)
        dv_sum[...] = jnp.zeros_like(dv_sum)
        for block in range(length // bench):
            reach = min(length, max((block + 1) * bench, PREFIX_TOP))
            span = slice(block * bench, (block + 1) * bench)
            row_of = block * bench + lax.broadcasted_iota(jnp.int32, (bench, reach), 0)
            place = lax.broadcasted_iota(jnp.int32, (bench, reach), 1)
            seen = (place <= row_of) | (place < limit)
            q = buf2[span, q_at]
            k = buf2[0:reach, k_at]
            v = buf2[0:reach, v_at]
            do = buf5[span, o_at]
            scores = jnp.where(seen, row_dot(q, k), -1e30)
            probs = jnp.exp(scores - lse_v[head, span, 0:1])
            d_probs = row_dot(do, v)
            inner = jnp.sum(probs * d_probs, axis=-1, keepdims=True)
            d_scores = (probs * (d_probs - inner)).astype(BF16)
            flip = (((0,), (0,)), ((), ()))
            dv_sum[0:reach, :] += lax.dot_general(probs.astype(BF16), do, flip, preferred_element_type=F32)
            dk_sum[0:reach, :] += lax.dot_general(d_scores, q, flip, preferred_element_type=F32)
            dq = jnp.dot(d_scores, k, preferred_element_type=F32) * scale
            biases[4:5, q_at] += jnp.sum(dq, axis=0, keepdims=True)
            buf5[span, q_at] = dq.astype(BF16)
        buf5[:, k_at] = dk_sum[...].astype(BF16)
        buf5[:, v_at] = dv_sum[...].astype(BF16)
        biases[5:6, q_at] += jnp.sum(dv_sum[...], axis=0, keepdims=True)
        return carry

    half = heads // 2
    lax.fori_loop(0, half, attend, 0)
    down.serve(0)
    up.produce(0)
    lax.fori_loop(half, heads, attend, 0)
    load_w.wait()

    def h1_part(rank, index):
        return row_dot(buf5[block_of(rank, rows), 0:triple], weight_v[block_of(index, 512), 0:triple])

    def take_h1(index, total):
        spare[:, block_of(index, 512)] = total

    pl.semaphore_wait(ready, 2)
    end = tensor_sum(spot, h1_part, *tensor, s_send, s_recv, take_h1)
    up.serve(1)
    out.produce(1)
    end()
    spot.release(ready)
    load_w = fetch(w2, weight_v, 2)
    load_t.wait()

    def back1(index, carry):
        where = block_of(index, strip)
        dx = norm_back(line[where, :].astype(F32), sums[0:1, :], spare[where, :], input_grad[where, :], 0)
        input_grad[where, :] = dx
        return carry

    lax.fori_loop(0, rows // strip, back1, 0)
    load_s = fetch(second, spare, 3)
    share = grad_up.shape[0]
    vector_copies, bias_copies = [], []
    for step in range(1, count):
        peer = lax.rem(spot.dp + step, count)
        vector_copies.append(remote(
            vectors.at[:, block_of(peer, share)], vector_in.at[spot.dp], v_send.at[step], v_recv.at[step], peer,
            spot.tensor,
        ))
        bias_copies.append(remote(biases, bias_in.at[spot.dp], b_send.at[step], b_recv.at[step], peer, spot.tensor))
    for copy in vector_copies + bias_copies:
        copy.start()
    vector_in[spot.dp] = vectors[:, block_of(spot.dp, share)]
    bias_in[spot.dp] = biases[...]
    up.serve(2)
    out.produce(2)
    down.settle()
    up.serve(3)
    out.produce(3)
    for copy in vector_copies + bias_copies:
        copy.wait_recv()
    total, bias_total = vector_in[0], bias_in[0]
    for index in range(1, count):
        total = total + vector_in[index]
        bias_total = bias_total + bias_in[index]
    part_sum[...] = total
    bias_sums[...] = bias_total
    part_copies = [
        remote(part_sum, part_in.at[spot.tensor], t_send.at[slot], t_recv.at[slot], spot.dp, peer)
        for slot, peer in enumerate((spot.x_peer, spot.core_peer, spot.far_peer))
    ]
    for copy in part_copies:
        copy.start()
    part_in[spot.tensor] = part_sum[...]
    up.serve(0)
    out.produce(0)
    load_b = fetch(gated_all, buf3, 0)
    load_h = fetch(h1_all, buf4, 1)
    for copy in part_copies:
        copy.wait_recv()
    vector_sums[...] = part_in[0] + part_in[1] + part_in[2] + part_in[3]
    load_h.wait()
    load_b.wait()
    load_w.wait()
    load_s.wait()
    out.serve(1)
    qkv.produce(1)
    out.serve(2)
    qkv.produce(2)
    out.serve(3)
    qkv.produce(3)
    up.settle()
    out.serve(0)
    qkv.produce(0)

    def down_part(rank, index):
        return jnp.dot(buf3[block_of(rank, rows), :], weight_v[:, block_of(index, 512)], preferred_element_type=F32)

    def take_out(index, total):
        where = block_of(index, 512)
        layer_out[:, where] = (spare[:, where] + total + sums[5:6, where]).astype(BF16)

    pl.semaphore_wait(ready, 2)
    end = tensor_sum(spot, down_part, *tensor, s_send, s_recv, take_out)
    out.settle()
    qkv.serve(1)
    end()
    qkv.serve(2)
    qkv.serve(3)
    qkv.serve(0)
    for copy in vector_copies + bias_copies + part_copies:
        copy.wait_send()
    qkv.settle()
    for copy in list(shared["y_busy"].values()) + list(shared["z_busy"].values()):
        copy.wait_send()


def backward_call(heads, count, prefix, sums, tokens, cotangent, weights, saved):
    rows, features = tokens.shape
    length = rows * 4
    share = features // count
    wqkv, wo, w1, w2 = weights
    width, hidden, triple = wo.shape[0], w1.shape[1], wqkv.shape[1]
    outer, inner = split_of(count)
    shape = jax.ShapeDtypeStruct
    hbm = pl.BlockSpec(memory_space=pl.ANY)
    vmem = pl.BlockSpec(memory_space=pltpu.VMEM)
    dma = pltpu.SemaphoreType.DMA
    regular = pltpu.SemaphoreType.REGULAR
    wide = (length, features)
    return pl.pallas_call(
        functools.partial(backward_kernel, heads, count),
        out_shape=[
            shape((rows, features), BF16),
            shape((rows, features), F32),
            shape((share, hidden), F32),
            shape((share, hidden), F32),
            shape((share, width), F32),
            shape((share, triple), F32),
            shape((8, share), F32),
            shape((8, 512), F32),
            shape((outer - 1, share, hidden), BF16),
            shape((outer - 1, share, hidden), BF16),
            shape((outer - 1, share, width), BF16),
            shape((outer - 1, share, triple), BF16),
        ],
        in_specs=[pl.BlockSpec(memory_space=pltpu.SMEM), vmem] + [hbm] * 10 + [vmem] + [hbm] * 4,
        out_specs=[vmem] * 2 + [hbm] * 4 + [vmem] * 2 + [hbm] * 4,
        scratch_shapes=[
            pltpu.VMEM((hidden, features), BF16),
            pltpu.VMEM(wide, BF16),
            pltpu.VMEM(wide, BF16),
            pltpu.VMEM(wide, BF16),
            pltpu.VMEM(wide, BF16),
            pltpu.VMEM(wide, BF16),
            pltpu.VMEM((2, rows, features), BF16),
            pltpu.VMEM((2, rows, features), BF16),
            pltpu.VMEM((rows, features), BF16),
            pltpu.VMEM((rows, features), BF16),
            pltpu.VMEM((outer, share, hidden), BF16),
            pltpu.VMEM((outer, share, hidden), BF16),
            pltpu.VMEM((outer, share, hidden), BF16),
            pltpu.VMEM((2, outer - 1, share, 512), BF16),
            pltpu.VMEM((2, share, 512), F32),
            pltpu.VMEM((rows, features), F32),
            pltpu.VMEM((rows, features), BF16),
            pltpu.VMEM((length, width // heads), F32),
            pltpu.VMEM((length, width // heads), F32),
            pltpu.VMEM((8, features), F32),
            pltpu.VMEM((8, 512), F32),
            pltpu.VMEM((count, 8, share), F32),
            pltpu.VMEM((count, 8, 512), F32),
            pltpu.VMEM((8, share), F32),
            pltpu.VMEM((4, 8, share), F32),
            dma((outer,)),
            dma((outer,)),
            dma((outer,)),
            dma((4, outer)),
            dma((3,)),
            dma((3,)),
            dma((3,)),
            dma((3,)),
            dma((count,)),
            dma((count,)),
            dma((count,)),
            dma((count,)),
            dma((3,)),
            dma((3,)),
            dma((4,)),
            dma((7,)),
            regular,
            regular,
        ],
        compiler_params=pltpu.CompilerParams(
            collective_id=1, has_side_effects=True, vmem_limit_bytes=VMEM_BYTES
        ),
    )(prefix, sums, tokens, cotangent, wqkv, wo, w1, w2, *saved)


def pack_small(biases, vectors):
    devices = lax.axis_size("dp")
    parts = jnp.concatenate(biases, axis=0)
    lane = lax.broadcasted_iota(jnp.int32, (parts.shape[0], parts.shape[1] * devices), 1)
    wide = jnp.where(lane // parts.shape[1] == lax.axis_index("dp"), jnp.tile(parts, (1, devices)), 0)
    halves = jnp.pad(jnp.stack(vectors), ((0, 2), (0, 0)))
    return jnp.concatenate([wide, halves[:, :128], halves[:, 128:]], axis=0).astype(F32)


def layer_norm(rows, gain, shift):
    center = rows - jnp.mean(rows, axis=-1, keepdims=True)
    spread = jnp.mean(center * center, axis=-1, keepdims=True)
    return center * lax.rsqrt(spread + 1e-05) * gain + shift


def gelu_exact(values):
    return jax.nn.gelu(values, approximate=False)


def head_major(matrix, heads):
    return matrix.reshape(matrix.shape[0], heads, -1).transpose(1, 0, 2)


def row_major(stacked):
    return stacked.transpose(1, 0, 2).reshape(stacked.shape[1], -1)


def masked_scores(q_block, keys, start, prefix_len):
    scores = jnp.einsum("hqd,hkd->hqk", q_block, keys, preferred_element_type=jnp.float32)
    rows = start + lax.broadcasted_iota(jnp.int32, scores.shape[1:], 0)
    cols = lax.broadcasted_iota(jnp.int32, scores.shape[1:], 1)
    seen = (cols <= rows) | (cols < prefix_len)
    return jnp.where(seen[None], scores, -1e30)


def to_blocks(stacked, count):
    heads, length = (stacked.shape[0], stacked.shape[1])
    return stacked.reshape((heads, count, length // count) + stacked.shape[2:]).swapaxes(0, 1)


def from_blocks(blocked):
    count, heads, block = (blocked.shape[0], blocked.shape[1], blocked.shape[2])
    return blocked.swapaxes(0, 1).reshape((heads, count * block) + blocked.shape[3:])


def contract_rows(left, right):
    return jnp.einsum("ld,le->de", left, right, preferred_element_type=jnp.float32)


def times_transpose(left, right):
    return jnp.einsum("le,de->ld", left, right, preferred_element_type=jnp.float32)


def plain(
    tokens,
    prefix,
    query_weight,
    key_weight,
    value_weight,
    out_weight,
    query_bias,
    value_bias,
    up_weight,
    down_weight,
    up_bias,
    norm1_gain,
    norm1_bias,
    norm2_gain,
    norm2_bias,
    out_bias,
    down_bias,
    cotangent,
):
    f32 = jnp.float32
    bf16 = jnp.bfloat16
    devices = lax.axis_size("dp")
    small = (query_bias, value_bias, up_bias, norm1_gain, norm1_bias, norm2_gain, norm2_bias, out_bias, down_bias)
    packed = jnp.concatenate([part.reshape(-1) for part in small])
    packed = lax.all_gather(packed, "dp", axis=0, tiled=False)
    pieces = []
    offset = 0
    for part in small:
        piece = packed[:, offset : offset + part.size].reshape((devices,) + part.shape)
        offset += part.size
        pieces.append(jnp.moveaxis(piece, 0, -2).reshape(part.shape[:-1] + (-1,)))
    bq, bv, b1, g1, n1, g2, n2, bo, b2 = pieces
    wq, wk, wv, wo = (
        lax.all_gather(query_weight, "dp", axis=0, tiled=True),
        lax.all_gather(key_weight, "dp", axis=0, tiled=True),
        lax.all_gather(value_weight, "dp", axis=0, tiled=True),
        lax.all_gather(out_weight, "dp", axis=1, tiled=True),
    )
    w1, w2 = (
        lax.all_gather(up_weight, "dp", axis=0, tiled=True),
        lax.all_gather(down_weight, "dp", axis=1, tiled=True),
    )
    g1f, n1f, g2f, n2f = (g1.astype(f32), n1.astype(f32), g2.astype(f32), n2.astype(f32))
    bof, b2f = (bo.astype(f32), b2.astype(f32))
    heads = bq.shape[0]
    head_size = bq.shape[1]
    scale = head_size ** (-0.5)
    prefix_len = prefix[0]
    xf = tokens.astype(f32)
    h1 = layer_norm(xf, g1f, n1f).astype(bf16)
    rows1 = lax.all_gather(h1, "tensor", axis=0, tiled=True)
    length = rows1.shape[0]
    block = min(512, length)
    count = length // block
    query = (
        (jnp.dot(rows1, wq, preferred_element_type=f32) + bq.astype(f32).reshape(-1)) * scale
    ).astype(bf16)
    keyed = jnp.dot(rows1, wk, preferred_element_type=f32).astype(bf16)
    valued = (jnp.dot(rows1, wv, preferred_element_type=f32) + bv.astype(f32).reshape(-1)).astype(
        bf16
    )
    q_heads = head_major(query, heads)
    k_heads = head_major(keyed, heads)
    v_heads = head_major(valued, heads)
    q_blocks = to_blocks(q_heads, count)
    starts = jnp.arange(count, dtype=jnp.int32) * block

    def forward_block(item):
        q_block, start = item
        scores = masked_scores(q_block, k_heads, start, prefix_len)
        top = jnp.max(scores, axis=-1, keepdims=True)
        expd = jnp.exp(scores - top)
        total = jnp.sum(expd, axis=-1, keepdims=True)
        probs = (expd / total).astype(bf16)
        outv = jnp.einsum("hqk,hkd->hqd", probs, v_heads, preferred_element_type=f32)
        return (outv.astype(bf16), (top + jnp.log(total))[..., 0])

    o_blocks, lse_blocks = lax.map(forward_block, (q_blocks, starts))
    mixed = row_major(from_blocks(o_blocks))
    attn_part = jnp.dot(mixed, wo, preferred_element_type=f32)
    attn_total = lax.psum_scatter(attn_part.astype(bf16), "tensor", scatter_dimension=0, tiled=True).astype(f32)
    second = xf + attn_total + bof
    h2 = layer_norm(second, g2f, n2f).astype(bf16)
    rows2 = lax.all_gather(h2, "tensor", axis=0, tiled=True)
    hidden = jnp.dot(rows2, w1, preferred_element_type=f32) + b1.astype(f32).reshape(-1)
    gated = gelu_exact(hidden).astype(bf16)
    mlp_part = jnp.dot(gated, w2, preferred_element_type=f32)
    mlp_total = lax.psum_scatter(
        mlp_part.astype(jnp.bfloat16), "tensor", scatter_dimension=0, tiled=True
    ).astype(jnp.float32)
    layer_out = (second + mlp_total + b2f).astype(bf16)
    d_out = cotangent.astype(f32)
    g_b2 = jnp.sum(d_out, axis=0)
    d_rows = lax.all_gather(cotangent, "tensor", axis=0, tiled=True)
    d_gated = times_transpose(d_rows, w2)
    d_hidden = jax.vjp(gelu_exact, hidden)[1](d_gated)[0]
    g_b1 = jnp.sum(d_hidden, axis=0).reshape(b1.shape)
    d_hidden_low = d_hidden.astype(bf16)
    d_h2_part = times_transpose(d_hidden_low, w1)
    g_w2 = contract_rows(gated, d_rows)
    g_w1 = contract_rows(rows2, d_hidden_low)
    d_h2 = lax.psum_scatter(d_h2_part.astype(bf16), "tensor", scatter_dimension=0, tiled=True).astype(f32)
    norm2_back = jax.vjp(layer_norm, second, g2f, n2f)[1]
    d_second_ln, g_g2, g_n2 = norm2_back(d_h2)
    d_second = d_out + d_second_ln
    g_bo = jnp.sum(d_second, axis=0)
    d_second_low = d_second.astype(bf16)
    back_rows = lax.all_gather(d_second_low, "tensor", axis=0, tiled=True)
    g_wo = contract_rows(mixed, back_rows)
    d_mixed = times_transpose(back_rows, wo).astype(bf16)
    do_blocks = to_blocks(head_major(d_mixed, heads), count)

    def backward_block(carry, item):
        d_keys, d_vals = carry
        q_block, do_block, lse_block, start = item
        scores = masked_scores(q_block, k_heads, start, prefix_len)
        probs = jnp.exp(scores - lse_block[..., None])
        d_probs = jnp.einsum("hqd,hkd->hqk", do_block, v_heads, preferred_element_type=f32)
        d_vals = d_vals + jnp.einsum(
            "hqk,hqd->hkd", probs.astype(bf16), do_block, preferred_element_type=f32
        )
        inner = jnp.sum(probs * d_probs, axis=-1, keepdims=True)
        d_scores = (probs * (d_probs - inner)).astype(bf16)
        d_query = jnp.einsum("hqk,hkd->hqd", d_scores, k_heads, preferred_element_type=f32)
        d_keys = d_keys + jnp.einsum("hqk,hqd->hkd", d_scores, q_block, preferred_element_type=f32)
        return ((d_keys, d_vals), d_query)

    empty = jnp.zeros(k_heads.shape, f32)
    (d_keys, d_vals), dq_blocks = lax.scan(
        backward_block, (empty, empty), (q_blocks, do_blocks, lse_blocks, starts)
    )
    d_query = row_major(from_blocks(dq_blocks)) * scale
    d_keys = row_major(d_keys)
    d_vals = row_major(d_vals)
    g_bq = jnp.sum(d_query, axis=0).reshape(bq.shape)
    g_bv = jnp.sum(d_vals, axis=0).reshape(bv.shape)
    dq_low, dk_low, dv_low = (d_query.astype(bf16), d_keys.astype(bf16), d_vals.astype(bf16))
    g_wq = contract_rows(rows1, dq_low)
    g_wk = contract_rows(rows1, dk_low)
    g_wv = contract_rows(rows1, dv_low)
    d_h1_part = (
        times_transpose(dq_low, wq) + times_transpose(dk_low, wk) + times_transpose(dv_low, wv)
    )
    d_h1 = lax.psum_scatter(d_h1_part.astype(bf16), "tensor", scatter_dimension=0, tiled=True).astype(f32)
    norm1_back = jax.vjp(layer_norm, xf, g1f, n1f)[1]
    d_input_ln, g_g1, g_n1 = norm1_back(d_h1)
    input_grad = d_second + d_input_ln
    def scatter(part, dim):
        return lax.psum_scatter(part.astype(bf16), "dp", scatter_dimension=dim, tiled=True).astype(f32)

    s_w2, s_w1, s_wo = scatter(g_w2, 1), scatter(g_w1, 0), scatter(g_wo, 1)
    s_wq, s_wk, s_wv = scatter(g_wq, 0), scatter(g_wk, 0), scatter(g_wv, 0)

    def by_device(part):
        return jnp.moveaxis(part.reshape(part.shape[:-1] + (devices, -1)), -2, 0).reshape(devices, -1)

    rows = [by_device(part) for part in (g_bq, g_bv, g_b1, g_g1, g_n1, g_g2, g_n2, g_bo, g_b2)]
    total = lax.psum_scatter(jnp.concatenate(rows, axis=1), "dp", scatter_dimension=0, tiled=True)[0]
    offset = 0
    outs = []
    for part in (query_bias, value_bias, up_bias):
        outs.append(total[offset : offset + part.size].reshape(part.shape))
        offset += part.size
    s_bq, s_bv, s_b1 = outs
    vectors = lax.psum_scatter(
        total[offset:].reshape(6, lax.axis_size("tensor"), -1), "tensor", scatter_dimension=1, tiled=True
    ).reshape(6, -1)
    s_g1, s_n1, s_g2, s_n2, s_bo, s_b2 = (vectors[index] for index in range(6))
    return (
        layer_out,
        input_grad,
        s_wq,
        s_wk,
        s_wv,
        s_wo,
        s_bq,
        s_bv,
        s_w1,
        s_w2,
        s_b1,
        s_g1,
        s_n1,
        s_g2,
        s_n2,
        s_bo,
        s_b2,
    )


def fast(
    tokens,
    prefix,
    query_weight,
    key_weight,
    value_weight,
    out_weight,
    query_bias,
    value_bias,
    up_weight,
    down_weight,
    up_bias,
    norm1_gain,
    norm1_bias,
    norm2_gain,
    norm2_bias,
    out_bias,
    down_bias,
    cotangent,
):
    devices = lax.axis_size("dp")
    me = lax.axis_index("dp")
    heads = query_bias.shape[0]
    small = pack_small(
        (query_bias, value_bias, up_bias), (norm1_gain, norm1_bias, norm2_gain, norm2_bias, out_bias, down_bias)
    )
    results = forward_call(
        heads, devices, prefix, tokens, cotangent, small,
        jnp.concatenate([query_weight, key_weight, value_weight], axis=1), out_weight, up_weight, down_weight,
    )
    layer_out, input_grad, g_w2, g_w1, g_wo, g_qkv, vectors, biases, *_ = backward_call(
        heads, devices, prefix, results[-1], tokens, cotangent, results[:4], results[4:-1]
    )
    g_wq, g_wk, g_wv = jnp.split(g_qkv, 3, axis=1)
    vectors = vectors.reshape(8, lax.axis_size("tensor"), -1)
    vectors = lax.dynamic_index_in_dim(vectors, lax.axis_index("tensor"), axis=1, keepdims=False)

    def own(flat, part):
        whole = flat.reshape(part.shape[0], -1)
        return lax.dynamic_slice_in_dim(whole, me * part.shape[1], part.shape[1], axis=1)

    width = out_weight.shape[0]
    up_size = up_bias.size * devices
    g_b1 = own(biases[: up_size // 512].reshape(-1), up_bias)
    g_bq = own(biases[4, :width], query_bias)
    g_bv = own(biases[5, :width], value_bias)
    return (
        layer_out, input_grad, g_wq, g_wk, g_wv, g_wo.T, g_bq, g_bv, g_w1, g_w2.T, g_b1,
        vectors[0], vectors[1], vectors[2], vectors[3], vectors[4], vectors[5],
    )


def local(*args):
    tokens, query_weight, up_weight = args[0], args[2], args[8]
    devices = lax.axis_size("dp")
    features = tokens.shape[1]
    share = features // devices
    fits = (
        lax.axis_size("tensor") == 4
        and devices == 8
        and share % 128 == 0
        and tokens.shape[0] == 256
        and query_weight.shape[1] == 512
        and args[6].shape[0] == 4
        and features == 2048
        and up_weight.shape[1] == 2048
    )
    return fast(*args) if fits else plain(*args)


def solution(mesh):
    in_specs = (
        P(("dp", "tensor"), None),
        P("dp"),
        P("dp", "tensor"),
        P("dp", "tensor"),
        P("dp", "tensor"),
        P("tensor", "dp"),
        P("tensor", "dp"),
        P("tensor", "dp"),
        P("dp", "tensor"),
        P("tensor", "dp"),
        P("tensor", "dp"),
        P("dp"),
        P("dp"),
        P("dp"),
        P("dp"),
        P("dp"),
        P("dp"),
        P(("dp", "tensor"), None),
    )
    out_specs = (
        P(("dp", "tensor"), None),
        P(("dp", "tensor"), None),
        P("dp", "tensor"),
        P("dp", "tensor"),
        P("dp", "tensor"),
        P("tensor", "dp"),
        P("tensor", "dp"),
        P("tensor", "dp"),
        P("dp", "tensor"),
        P("tensor", "dp"),
        P("tensor", "dp"),
        P(("dp", "tensor")),
        P(("dp", "tensor")),
        P(("dp", "tensor")),
        P(("dp", "tensor")),
        P(("dp", "tensor")),
        P(("dp", "tensor")),
    )
    return jax.shard_map(local, mesh=mesh, in_specs=in_specs, out_specs=out_specs, check_vma=False)
```

```python
import functools

import jax
import jax.numpy as jnp
from jax import lax
from jax.experimental import pallas as pl
from jax.experimental.pallas import tpu as pltpu
from jax.sharding import PartitionSpec as P

MESH = pl.DeviceIdType.MESH
F32 = jnp.float32
BF16 = jnp.bfloat16
PREFIX_TOP = 512
VMEM_BYTES = 67043328


def split_of(count):
    inner = 1
    for size in range(1, count + 1):
        if size * size <= count and count % size == 0:
            inner = size
    return count // inner, inner


def remote(source, target, send_sem, recv_sem, dp, tensor):
    return pltpu.make_async_remote_copy(
        src_ref=source,
        dst_ref=target,
        send_sem=send_sem,
        recv_sem=recv_sem,
        device_id=(dp, tensor),
        device_id_type=MESH,
    )


def block_of(index, size):
    return pl.ds(pl.multiple_of(index * size, size), size)


class Spot:
    def __init__(self, count):
        self.outer, self.inner = split_of(count)
        self.count = count
        self.dp = lax.axis_index("dp")
        self.tensor = lax.axis_index("tensor")
        self.row = lax.div(self.dp, self.inner)
        self.column = lax.rem(self.dp, self.inner)
        self.core_peer = self.tensor + 1 - 2 * lax.rem(self.tensor, 2)
        self.x_peer = lax.rem(self.tensor + 2, 4)
        self.far_peer = lax.rem(self.core_peer + 2, 4)

    def across(self, step):
        return lax.rem(self.row + step, self.outer) * self.inner + self.column

    def beside(self, step, row=None):
        return (self.row if row is None else row) * self.inner + lax.rem(self.column + step, self.inner)

    def meet(self, far=False):
        barrier = pltpu.get_barrier_semaphore()
        for step in range(1, self.count):
            pl.semaphore_signal(
                barrier, inc=1, device_id=(lax.rem(self.dp + step, self.count), self.tensor), device_id_type=MESH
            )
        for peer in (self.core_peer, self.x_peer) + ((self.far_peer,) if far else ()):
            pl.semaphore_signal(barrier, inc=1, device_id=(self.dp, peer), device_id_type=MESH)
        pl.semaphore_wait(barrier, self.count + 1 + far)

    def release(self, ready):
        for peer in (self.core_peer, self.x_peer):
            pl.semaphore_signal(ready, inc=1, device_id=(self.dp, peer), device_id_type=MESH)


class Spread:
    AHEAD = 3

    def __init__(self, spot, pieces, late, own_at, sems):
        self.spot, self.pieces, self.late, self.sems = spot, pieces, late, sems
        self.flows = [(piece, 0) for piece in range(len(pieces)) if piece != late] + [(late, 0), (late, 1)]
        self.own_at = own_at
        self.order = (2, jnp.where(spot.row == 0, 3, 1), jnp.where(spot.row == 0, 1, 3))
        self.sent = []
        self.todo = [(flow, place) for flow in range(len(self.flows)) for place in range(3)]
        for piece in own_at[None]:
            self.send_own(piece)
        for flow in range(self.AHEAD):
            self.send_rows(flow)

    def owner(self, row, side):
        return row * 2 + lax.rem(self.spot.column + side, 2)

    def launch(self, condition, copy):
        if condition is None:
            copy().start()
        else:
            pl.when(condition)(lambda: copy().start())
        self.sent.append((condition, copy))

    def along(self, flow, step, source_row, target_row, send_slot):
        piece, side = self.flows[flow]
        source, target = self.pieces[piece]
        place = target(self.owner(source_row, side))
        if source_row is not self.spot.row or side:
            source = place
        return remote(
            source, place, self.sems[0].at[flow, send_slot], self.sems[1].at[flow, step],
            target_row * 2 + self.spot.column, self.spot.tensor,
        )

    def send_rows(self, flow):
        row = self.spot.row
        if self.flows[flow][1]:
            self.beside(self.late, 0, row).wait_recv()
        for step, condition in ((2, None), (1, row != 3), (3, row != 0)):
            self.launch(
                condition,
                functools.partial(self.along, flow, step, row, lax.rem(row + step, 4), step),
            )

    def hand_over(self, flow):
        row = self.spot.row
        self.launch(
            (row == 1) | (row == 2),
            lambda: self.along(flow, 2 * row - 1, lax.rem(row + 2, 4), (row - 1) * 3, 0),
        )

    def beside(self, piece, step, source_row):
        spot = self.spot
        source, target = self.pieces[piece]
        place = target(self.owner(source_row, 0))
        if source_row is not spot.row:
            source = place
        return remote(
            source, place, self.sems[2].at[piece, step], self.sems[3].at[piece, step], spot.beside(1), spot.tensor
        )

    def beside_arrival(self, piece, step, source_row):
        source, target = self.pieces[piece]
        return remote(
            source, target(self.owner(source_row, 1)), self.sems[2].at[piece, step], self.sems[3].at[piece, step],
            self.spot.beside(1), self.spot.tensor,
        )

    def send_own(self, piece):
        self.launch(None, functools.partial(self.beside, piece, 0, self.spot.row))

    def forward(self, count):
        for _ in range(count):
            if not self.todo:
                return
            flow, place = self.todo.pop(0)
            step = self.order[place]
            row = lax.rem(self.spot.row + 4 - step, 4)
            self.along(flow, step, row, self.spot.row, 0).wait_recv()
            if place == 0:
                self.hand_over(flow)
            piece = self.flows[flow][0]
            if piece != self.late:
                self.launch(None, functools.partial(self.beside, piece, step, row))
            if place == 2:
                if flow + self.AHEAD < len(self.flows):
                    self.send_rows(flow + self.AHEAD)
                for own in self.own_at.get(flow, ()):
                    self.send_own(own)

    def arrived(self, piece):
        while self.todo and self.flows[self.todo[0][0]][0] <= piece:
            self.forward(1)
        if piece != self.late:
            for step in range(4):
                self.beside_arrival(piece, step, lax.rem(self.spot.row + 4 - step, 4)).wait_recv()

    def finish(self):
        for condition, copy in self.sent:
            if condition is None:
                copy().wait_send()
            else:
                pl.when(condition)(lambda copy=copy: copy().wait_send())


class TensorGather:
    def __init__(self, spot, own, full, rows, send, recv):
        self.spot, self.full, self.rows, self.send, self.recv = spot, full, rows, send, recv
        place = self.at(spot.tensor)
        self.to_x = remote(own, place, send.at[0], recv.at[0], spot.dp, spot.x_peer)
        self.to_core = remote(own, place, send.at[1], recv.at[1], spot.dp, spot.core_peer)
        self.to_x.start()
        self.to_core.start()

    def at(self, index):
        return self.full.at[block_of(index, self.rows)]

    def pass_on(self):
        self.to_x.wait_recv()
        place = self.at(self.spot.x_peer)
        self.on = remote(place, place, self.send.at[2], self.recv.at[2], self.spot.dp, self.spot.core_peer)
        self.on.start()

    def finish(self):
        self.to_core.wait_recv()
        self.on.wait_recv()
        for copy in (self.to_x, self.to_core, self.on):
            copy.wait_send()


def tensor_sum(spot, product, core_send, core_recv, x_send, x_recv, send, recv, finish, between=None):
    width = core_send.shape[2]
    chunk = 512
    count = width // chunk

    def fill(rank, target):
        def body(index, carry):
            target[:, block_of(index, chunk)] = product(rank, index).astype(BF16)
            return carry

        lax.fori_loop(0, count, body, 0)

    copies = []
    for slot, rank in enumerate((spot.far_peer, spot.core_peer)):
        fill(rank, core_send.at[slot])
        copy = remote(core_send.at[slot], core_recv.at[slot], send.at[slot], recv.at[slot], spot.dp, spot.core_peer)
        copy.start()
        copies.append(copy)
    if between is not None:
        between()
    copies[0].wait_recv()

    def join(index, carry):
        where = block_of(index, chunk)
        x_send[:, where] = (product(spot.x_peer, index) + core_recv[0, :, where].astype(F32)).astype(BF16)
        return carry

    lax.fori_loop(0, count, join, 0)
    over = remote(x_send, x_recv, send.at[2], recv.at[2], spot.dp, spot.x_peer)
    over.start()
    copies[1].wait_recv()

    def end():
        over.wait_recv()

        def last(index, carry):
            where = block_of(index, chunk)
            total = product(spot.tensor, index) + core_recv[1, :, where].astype(F32) + x_recv[:, where].astype(F32)
            finish(index, total)
            return carry

        lax.fori_loop(0, count, last, 0)
        for copy in copies + [over]:
            copy.wait_send()

    return end


def normal_parts(rows):
    center = rows - jnp.mean(rows, axis=-1, keepdims=True)
    spread = jnp.mean(center * center, axis=-1, keepdims=True)
    return center, lax.rsqrt(spread + 1e-05)


def forward_kernel(
    heads,
    count,
    prefix,
    tokens,
    cotangent,
    small,
    qkv_shard,
    out_shard,
    up_shard,
    down_shard,
    wqkv,
    wo,
    w1,
    w2,
    h1_all,
    d_rows,
    qkv_all,
    mixed_all,
    lse_all,
    second,
    h2_all,
    gated_all,
    slope_all,
    sums,
    smalls,
    h1v,
    wqkv_v,
    qkv_v,
    mixed_v,
    lse_v,
    wo_v,
    core_send,
    core_recv,
    x_send,
    x_recv,
    h2v,
    w1_v,
    gated_v,
    slope_v,
    small_send,
    small_recv,
    z_send,
    z_recv,
    y_send,
    y_recv,
    g_send,
    g_recv,
    s_send,
    s_recv,
    local_sem,
):
    spot = Spot(count)
    rows, features = tokens.shape
    length = h1v.shape[0]
    depth = qkv_shard.shape[0]
    width = wo_v.shape[0]
    hidden = up_shard.shape[1]
    half = depth // 2
    tall = hidden // 2
    pieces = [
        (qkv_shard.at[pl.ds(part * half, half)],
         lambda owner, part=part: wqkv.at[block_of(owner * 2 + part, half)])
        for part in range(2)
    ]
    pieces.append((out_shard, lambda owner: wo.at[:, block_of(owner, depth)]))
    pieces += [
        (up_shard.at[:, pl.ds(part * tall, tall)],
         lambda owner, part=part: w1.at[block_of(owner, depth), pl.ds(part * tall, tall)])
        for part in range(2)
    ]
    pieces += [
        (down_shard.at[pl.ds(part * tall, tall)],
         lambda owner, part=part: w2.at[pl.ds(part * tall, tall), block_of(owner, depth)])
        for part in range(2)
    ]
    locals_ = []

    def keep(source, target):
        copy = pltpu.make_async_copy(source, target, local_sem.at[len(locals_)])
        copy.start()
        locals_.append(copy)

    spot.meet()
    small_copies = []
    for step in range(1, count):
        copy = remote(
            small, smalls.at[spot.dp], small_send.at[step], small_recv.at[step],
            lax.rem(spot.dp + step, count), spot.tensor,
        )
        copy.start()
        small_copies.append(copy)
    spread = Spread(
        spot, pieces, 6, {None: (0, 1, 2, 3), 0: (4,), 1: (6,), 2: (5,)}, (z_send, z_recv, y_send, y_recv)
    )
    for source, target in pieces:
        keep(source, target(spot.dp))
    smalls[spot.dp] = small[...]
    for step in range(1, count):
        owner = lax.rem(spot.dp + count - step, count)
        remote(
            small, smalls.at[owner], small_send.at[step], small_recv.at[step], spot.dp, spot.core_peer
        ).wait_recv()
    sums[...] = jnp.zeros_like(sums)
    joint = smalls[0, 0:24, :]
    for index in range(1, count):
        joint = joint + smalls[index, 0:24, :]
    lanes = 128
    for head in range(heads):
        sums[6:7, head * lanes : (head + 1) * lanes] = joint[head : head + 1, :]
        start = 2 * width + head * lanes
        sums[6:7, start : start + lanes] = joint[4 + head : 5 + head, :]
    for line in range(hidden // lanes):
        sums[7:8, line * lanes : (line + 1) * lanes] = joint[8 + line : 9 + line, :]
    for owner in range(count):
        for part in range(2):
            start = owner * depth + part * lanes
            sums[0:6, start : start + lanes] = smalls[owner, 24 + 8 * part : 30 + 8 * part, :]

    strip = 32
    base = spot.tensor * rows

    def norm1(index, carry):
        where = block_of(index, strip)
        center, scale = normal_parts(tokens[where, :].astype(F32))
        h1v[pl.ds(pl.multiple_of(base + index * strip, strip), strip), :] = (
            center * scale * sums[0:1, :] + sums[1:2, :]
        ).astype(BF16)
        return carry

    lax.fori_loop(0, rows // strip, norm1, 0)
    gather1 = TensorGather(spot, h1v.at[block_of(spot.tensor, rows)], h1v, rows, g_send.at[0], g_recv.at[0])
    gather_d = TensorGather(spot, cotangent, d_rows, rows, g_send.at[1], g_recv.at[1])
    keep(cotangent, d_rows.at[block_of(spot.tensor, rows)])
    spread.forward(1)
    gather1.pass_on()
    spread.forward(2)
    gather_d.pass_on()
    gather1.finish()
    keep(h1v, h1_all)
    spread.forward(6)
    spread.arrived(0)
    spread.arrived(1)
    for copy in locals_[:2]:
        copy.wait()
    load = pltpu.make_async_copy(wqkv, wqkv_v, local_sem.at[14])
    load.start()
    load.wait()

    def project(index, carry):
        where = block_of(index, rows)
        for part in range(3):
            lanes = slice(part * width, (part + 1) * width)
            value = jnp.dot(h1v[where, :], wqkv_v[:, lanes], preferred_element_type=F32) + sums[6:7, lanes]
            if part == 0:
                value = value * (width // heads) ** -0.5
            qkv_v[where, lanes] = value.astype(BF16)
        return carry

    lax.fori_loop(0, length // rows, project, 0)
    keep(qkv_v, qkv_all)
    spread.forward(3)
    size = width // heads
    limit = prefix[0]
    bench = 256

    for block in range(length // bench):
        reach = min(length, max((block + 1) * bench, PREFIX_TOP))
        span = slice(block * bench, (block + 1) * bench)

        def attend(head, carry, block=block, span=span, reach=reach):
            line = block * bench + lax.broadcasted_iota(jnp.int32, (bench, reach), 0)
            place = lax.broadcasted_iota(jnp.int32, (bench, reach), 1)
            seen = (place <= line) | (place < limit)
            q = qkv_v[span, block_of(head, size)]
            k = qkv_v[0:reach, pl.ds(pl.multiple_of(width + head * size, size), size)]
            v = qkv_v[0:reach, pl.ds(pl.multiple_of(2 * width + head * size, size), size)]
            scores = lax.dot_general(q, k, (((1,), (1,)), ((), ())), preferred_element_type=F32)
            scores = jnp.where(seen, scores, -1e30)
            top = jnp.max(scores, axis=-1, keepdims=True)
            expd = jnp.exp(scores - top)
            total = jnp.sum(expd, axis=-1, keepdims=True)
            probs = (expd * (1.0 / total)).astype(BF16)
            mixed_v[span, block_of(head, size)] = jnp.dot(probs, v, preferred_element_type=F32).astype(BF16)
            lse_v[head, span, :] = jnp.broadcast_to(top + jnp.log(total), (bench, 128))
            return carry

        lax.fori_loop(0, heads, attend, 0)
        if block == 2:
            spread.forward(2)
    keep(mixed_v, mixed_all)
    keep(lse_v, lse_all)
    spread.forward(1)
    spread.arrived(2)
    locals_[2].wait()
    load = pltpu.make_async_copy(wo, wo_v, local_sem.at[14])
    load.start()
    load.wait()

    def out_part(rank, index):
        return jnp.dot(mixed_v[block_of(rank, rows), :], wo_v[:, block_of(index, 512)], preferred_element_type=F32)

    def take_second(index, total):
        where = block_of(index, 512)
        second[:, where] = tokens[:, where].astype(F32) + total + sums[4:5, where]

    end = tensor_sum(
        spot, out_part, core_send, core_recv, x_send, x_recv, s_send.at[0], s_recv.at[0], take_second
    )
    end()

    def norm2(index, carry):
        where = block_of(index, strip)
        center, scale = normal_parts(second[where, :])
        h2v[pl.ds(pl.multiple_of(base + index * strip, strip), strip), :] = (
            center * scale * sums[2:3, :] + sums[3:4, :]
        ).astype(BF16)
        return carry

    lax.fori_loop(0, rows // strip, norm2, 0)
    gather2 = TensorGather(spot, h2v.at[block_of(spot.tensor, rows)], h2v, rows, g_send.at[2], g_recv.at[2])
    gather2.pass_on()
    spread.forward(3)
    gather2.finish()
    gather_d.finish()
    keep(h2v, h2_all)
    stored = []
    for part in range(2):
        spread.arrived(3 + part)
        locals_[3 + part].wait()
        lanes_of = pl.ds(part * tall, tall)
        load = pltpu.make_async_copy(w1.at[:, lanes_of], w1_v.at[:, lanes_of], local_sem.at[14])
        load.start()
        load.wait()
        for block in range(length // rows):
            slot = block % 2
            if len(stored) >= 2:
                stored[-2].wait()

            def lift(index, carry, block=block, slot=slot, part=part):
                where = block_of(part * (tall // 512) + index, 512)
                u = jnp.dot(
                    h2v[block * rows : (block + 1) * rows, :], w1_v[:, where], preferred_element_type=F32
                ) + sums[7:8, where]
                below = 0.5 * (1.0 + lax.erf(u * 0.7071067811865476))
                gated_v[block * rows : (block + 1) * rows, where] = (u * below).astype(BF16)
                slope_v[slot, :, block_of(index, 512)] = below + u * (0.3989422804014327 * jnp.exp(-0.5 * u * u))
                return carry

            lax.fori_loop(0, tall // 512, lift, 0)
            copy = pltpu.make_async_copy(
                slope_v.at[slot], slope_all.at[pl.ds(block * rows, rows), lanes_of], local_sem.at[15 + slot]
            )
            copy.start()
            stored.append(copy)
        if part == 0:
            spread.forward(3)
    keep(gated_v, gated_all)
    spread.arrived(6)
    spread.arrived(5)
    spread.finish()
    for copy in small_copies:
        copy.wait_send()
    for copy in locals_[5:] + stored[-2:]:
        copy.wait()


def forward_call(heads, count, prefix, tokens, cotangent, small, qkv_shard, out_shard, up_shard, down_shard):
    rows, features = tokens.shape
    length = rows * 4
    depth, triple = qkv_shard.shape
    width = out_shard.shape[0]
    hidden = up_shard.shape[1]
    outer, inner = split_of(count)
    shape = jax.ShapeDtypeStruct
    hbm = pl.BlockSpec(memory_space=pl.ANY)
    vmem = pl.BlockSpec(memory_space=pltpu.VMEM)
    dma = pltpu.SemaphoreType.DMA
    pieces = 7
    return pl.pallas_call(
        functools.partial(forward_kernel, heads, count),
        out_shape=[
            shape((features, triple), BF16),
            shape((width, features), BF16),
            shape((features, hidden), BF16),
            shape((hidden, features), BF16),
            shape((length, features), BF16),
            shape((length, features), BF16),
            shape((length, triple), BF16),
            shape((length, width), BF16),
            shape((heads, length, 128), F32),
            shape((rows, features), F32),
            shape((length, features), BF16),
            shape((length, hidden), BF16),
            shape((length, hidden), F32),
            shape((8, features), F32),
        ],
        in_specs=[pl.BlockSpec(memory_space=pltpu.SMEM)] + [vmem] * 7,
        out_specs=[hbm] * 9 + [vmem] + [hbm] * 3 + [vmem],
        scratch_shapes=[
            pltpu.VMEM((count, 40, 128), F32),
            pltpu.VMEM((length, features), BF16),
            pltpu.VMEM((features, triple), BF16),
            pltpu.VMEM((length, triple), BF16),
            pltpu.VMEM((length, width), BF16),
            pltpu.VMEM((heads, length, 128), F32),
            pltpu.VMEM((width, features), BF16),
            pltpu.VMEM((2, rows, features), BF16),
            pltpu.VMEM((2, rows, features), BF16),
            pltpu.VMEM((rows, features), BF16),
            pltpu.VMEM((rows, features), BF16),
            pltpu.VMEM((length, features), BF16),
            pltpu.VMEM((features, hidden), BF16),
            pltpu.VMEM((length, hidden), BF16),
            pltpu.VMEM((2, rows, hidden // 2), F32),
            dma((count,)),
            dma((count,)),
            dma((pieces + 1, outer)),
            dma((pieces + 1, outer)),
            dma((pieces, outer)),
            dma((pieces, outer)),
            dma((3, 3)),
            dma((3, 3)),
            dma((1, 3)),
            dma((1, 3)),
            dma((17,)),
        ],
        compiler_params=pltpu.CompilerParams(
            collective_id=0, has_side_effects=True, vmem_limit_bytes=VMEM_BYTES
        ),
    )(prefix, tokens, cotangent, small, qkv_shard, out_shard, up_shard, down_shard)
class Reduce:
    def __init__(self, spot, left, right, lanes, landing, target, shared, index, last):
        self.spot, self.left, self.right, self.lanes = spot, left, right, lanes
        self.landing, self.target, self.shared, self.index, self.last = landing, target, shared, index, last
        self.width = lanes.stop - lanes.start
        self.share = target.shape[0]
        self.stepped = {}
        self.held = ()

    def block(self, owner, take):
        turned = jnp.transpose(self.left[:, block_of(owner, self.share)])
        for start in range(0, self.width, 512):
            source = self.right[:, self.lanes.start + start : self.lanes.start + start + 512]
            take(slice(start, start + 512), jnp.dot(turned, source, preferred_element_type=F32))

    def y_copy(self, step):
        shared = self.shared
        area = pl.ds(0, self.width)
        return remote(
            shared["y_out"].at[step, :, area], shared["y_in"].at[step, :, area], shared["y_send"].at[step],
            shared["y_recv"].at[step], self.spot.beside(1), self.spot.tensor,
        )

    def z_copy(self, step):
        shared = self.shared
        return remote(
            shared["z_out"].at[step, :, pl.ds(0, self.width)], self.landing.at[step - 1],
            shared["z_send"].at[step], shared["z_recv"].at[self.index, step], self.spot.across(step),
            self.spot.tensor,
        )

    def produce(self, step):
        shared, spot = self.shared, self.spot
        row = lax.rem(spot.row + step, spot.outer)
        if step in shared["y_busy"]:
            shared["y_busy"].pop(step).wait_send()

        def take(where, value):
            shared["y_out"][step, :, where] = value.astype(BF16)

        self.block(spot.beside(1, row), take)
        if self.index > 0:
            pl.semaphore_wait(shared["credit"], 1)
        copy = self.y_copy(step)
        copy.start()
        shared["y_busy"][step] = copy

    def hold(self, steps):
        self.held = steps
        for step in steps:

            def take(where, value, step=step):
                self.shared["z_out"][step, :, where] = value.astype(BF16)

            self.block(self.spot.across(step), take)

    def serve(self, step):
        shared, spot = self.shared, self.spot
        self.y_copy(step).wait_recv()
        if step in shared["z_busy"]:
            shared["z_busy"].pop(step).wait_send()
        y_in, z_out = shared["y_in"], shared["z_out"]
        if step in self.held:
            for start in range(0, self.width, 512):
                where = slice(start, start + 512)
                z_out[step, :, where] = (z_out[step, :, where].astype(F32) + y_in[step, :, where].astype(F32)).astype(BF16)
        else:

            def take(where, value):
                z_out[step, :, where] = (value + y_in[step, :, where].astype(F32)).astype(BF16)

            self.block(spot.across(step), take)
        if not self.last:
            pl.semaphore_signal(
                shared["credit"], inc=1, device_id=(spot.beside(1), spot.tensor), device_id_type=MESH
            )
        if step:
            copy = self.z_copy(step)
            copy.start()
            shared["z_busy"][step] = copy

    def settle(self):
        shared, spot = self.shared, self.spot
        for step in range(1, spot.outer):
            self.z_copy(step).wait_recv()
        loads, stores = [], []
        chunks = self.width // 128
        for chunk in range(chunks):
            slot = chunk % 4
            loads.append(pltpu.make_async_copy(
                self.landing.at[:, :, pl.ds(chunk * 128, 128)], shared["z_stage"].at[slot], shared["stage_sem"].at[slot]
            ))
            stores.append(pltpu.make_async_copy(
                shared["o_stage"].at[slot], self.target.at[:, pl.ds(chunk * 128, 128)], shared["stage_sem"].at[4 + slot]
            ))
        for load in loads[:3]:
            load.start()
        for chunk in range(chunks):
            loads[chunk].wait()
            if chunk + 3 < chunks:
                loads[chunk + 3].start()
            if chunk >= 4:
                stores[chunk - 4].wait()
            total = shared["z_out"][0, :, chunk * 128 : (chunk + 1) * 128].astype(F32)
            for step in range(spot.outer - 1):
                total = total + shared["z_stage"][chunk % 4, step].astype(F32)
            shared["o_stage"][chunk % 4] = total
            stores[chunk].start()
        for store in stores[-4:]:
            store.wait()


def row_dot(left, right):
    return lax.dot_general(left, right, (((1,), (1,)), ((), ())), preferred_element_type=F32)


def backward_kernel(
    heads,
    count,
    prefix,
    sums,
    tokens,
    cotangent,
    wqkv,
    wo,
    w1,
    w2,
    h1_all,
    d_rows,
    qkv_all,
    mixed_all,
    lse_v,
    second,
    h2_all,
    gated_all,
    slope_all,
    layer_out,
    input_grad,
    grad_down,
    grad_up,
    grad_out,
    grad_qkv,
    vector_sums,
    bias_sums,
    land_down,
    land_up,
    land_out,
    land_qkv,
    weight_v,
    buf1,
    buf2,
    buf3,
    buf4,
    buf5,
    buf6,
    core_send,
    core_recv,
    x_send,
    x_recv,
    y_in,
    y_out,
    z_out,
    z_stage,
    o_stage,
    spare,
    line,
    dk_sum,
    dv_sum,
    vectors,
    biases,
    vector_in,
    bias_in,
    part_sum,
    part_in,
    y_send,
    y_recv,
    z_send,
    z_recv,
    g_send,
    g_recv,
    s_send,
    s_recv,
    v_send,
    v_recv,
    b_send,
    b_recv,
    t_send,
    t_recv,
    stage_sem,
    load_sem,
    credit,
    ready,
):
    spot = Spot(count)
    rows, features = line.shape
    length = buf1.shape[0]
    width = wo.shape[0]
    hidden = w1.shape[1]
    triple = 3 * width
    size = width // heads
    scale = size ** -0.5
    tail = slice(triple, triple + width)
    shared = {
        "y_in": y_in, "y_out": y_out, "z_out": z_out, "z_stage": z_stage, "o_stage": o_stage, "y_send": y_send,
        "y_recv": y_recv, "z_send": z_send, "z_recv": z_recv, "credit": credit, "stage_sem": stage_sem,
        "y_busy": {}, "z_busy": {},
    }
    down = Reduce(spot, buf1, buf2, slice(0, hidden), land_down, grad_down, shared, 0, False)
    up = Reduce(spot, buf4, buf3, slice(0, hidden), land_up, grad_up, shared, 1, False)
    qkv = Reduce(spot, buf6, buf5, slice(0, triple), land_qkv, grad_qkv, shared, 2, False)
    out = Reduce(spot, buf1, buf2, tail, land_out, grad_out, shared, 3, True)

    def fetch(source, target, slot):
        copy = pltpu.make_async_copy(source, target, load_sem.at[slot])
        copy.start()
        return copy

    load_a = fetch(d_rows, buf1, 0)
    load_b = fetch(gated_all, buf2, 1)
    load_w = fetch(w2, weight_v, 2)
    slopes = [fetch(slope_all.at[pl.ds(part * rows, rows)], (spare, input_grad)[part % 2], 3 + part % 2) for part in range(2)]
    load_h = fetch(h2_all, buf4, 5)
    load_c = fetch(cotangent, line, 6)
    load_n = fetch(h1_all, buf6, 7)
    spot.meet(True)
    vectors[...] = jnp.zeros_like(vectors)
    biases[...] = jnp.zeros_like(biases)
    load_a.wait()
    load_b.wait()
    order = list(range(1, spot.outer)) + [0]
    for step in order:
        down.produce(step)
    load_w.wait()
    tensor = (core_send, core_recv, x_send, x_recv)

    def down_part(rank, index):
        return jnp.dot(buf2[block_of(rank, rows), :], weight_v[:, block_of(index, 512)], preferred_element_type=F32)

    def take_out(index, total):
        where = block_of(index, 512)
        layer_out[:, where] = (spare[:, where] + total + sums[5:6, where]).astype(BF16)

    end = tensor_sum(
        spot, down_part, *tensor, s_send, s_recv, take_out, between=lambda: down.serve(1)
    )
    for part in range(length // rows):
        held = (spare, input_grad)[part % 2]
        slopes[part].wait()

        def lower(index, carry, part=part, held=held):
            where = block_of(index, 512)
            span = slice(part * rows, (part + 1) * rows)
            du = row_dot(buf1[span, :], weight_v[where, :]) * held[:, where]
            biases[pl.ds(index, 1), :] += jnp.sum(du, axis=0, keepdims=True)
            buf3[span, where] = du.astype(BF16)
            return carry

        lax.fori_loop(0, hidden // 512, lower, 0)
        if part + 2 < length // rows:
            slopes.append(fetch(slope_all.at[pl.ds((part + 2) * rows, rows)], held, 3 + part % 2))
        if part == 1:
            down.serve(2)
    load_s = fetch(second, spare, 3)
    load_s.wait()
    end()
    spot.release(ready)
    load_w = fetch(w1, weight_v, 2)
    load_h.wait()
    down.serve(3)
    down.hold((0,))
    load_q = fetch(qkv_all, buf2.at[:, pl.ds(0, triple)], 0)
    load_m = fetch(mixed_all, buf2.at[:, pl.ds(triple, width)], 1)
    up.produce(1)
    up.produce(2)
    up.produce(3)
    load_w.wait()

    def h2_part(rank, index):
        return row_dot(buf3[block_of(rank, rows), :], weight_v[block_of(index, 512), :])

    def take_h2(index, total):
        input_grad[:, block_of(index, 512)] = total

    pl.semaphore_wait(ready, 2)
    end = tensor_sum(spot, h2_part, *tensor, s_send, s_recv, take_h2)
    down.serve(0)
    up.produce(0)
    up.serve(1)
    end()
    spot.release(ready)
    load_o = fetch(wo, weight_v.at[pl.ds(0, width)], 2)
    load_c.wait()
    strip = 32
    base = spot.tensor * rows

    def norm_back(rows_of, gain, grads, keep, first):
        center, inverse = normal_parts(rows_of)
        normal = center * inverse
        vectors[first : first + 1, :] += jnp.sum(grads * normal, axis=0, keepdims=True)
        vectors[first + 1 : first + 2, :] += jnp.sum(grads, axis=0, keepdims=True)
        scaled = grads * gain
        mean = jnp.mean(scaled, axis=-1, keepdims=True)
        slope = jnp.mean(scaled * normal, axis=-1, keepdims=True)
        return keep + inverse * (scaled - mean - normal * slope)

    def back2(index, carry):
        where = block_of(index, strip)
        dy = line[where, :].astype(F32)
        dx = norm_back(spare[where, :], sums[2:3, :], input_grad[where, :], dy, 2)
        vectors[4:5, :] += jnp.sum(dx, axis=0, keepdims=True)
        vectors[5:6, :] += jnp.sum(dy, axis=0, keepdims=True)
        input_grad[where, :] = dx
        buf1[pl.ds(pl.multiple_of(base + index * strip, strip), strip), :] = dx.astype(BF16)
        return carry

    lax.fori_loop(0, rows // strip, back2, 0)
    gather = TensorGather(spot, buf1.at[block_of(spot.tensor, rows)], buf1, rows, g_send, g_recv)
    load_t = fetch(tokens, line, 6)
    up.serve(2)
    down.settle()
    gather.pass_on()
    load_o.wait()
    gather.finish()
    load_q.wait()
    load_m.wait()

    def mix_back(index, carry):
        where = block_of(index, rows)
        buf5[where, tail] = row_dot(buf1[where, :], weight_v[0:width, :]).astype(BF16)
        return carry

    lax.fori_loop(0, length // rows, mix_back, 0)
    load_w = fetch(wqkv, weight_v.at[:, pl.ds(0, triple)], 2)
    limit = prefix[0]
    bench = 256

    def attend(head, carry):
        q_at = block_of(head, size)
        k_at = pl.ds(pl.multiple_of(width + head * size, size), size)
        v_at = pl.ds(pl.multiple_of(2 * width + head * size, size), size)
        o_at = pl.ds(pl.multiple_of(triple + head * size, size), size)
        dk_sum[...] = jnp.zeros_like(dk_sum)
        dv_sum[...] = jnp.zeros_like(dv_sum)
        for block in range(length // bench):
            reach = min(length, max((block + 1) * bench, PREFIX_TOP))
            span = slice(block * bench, (block + 1) * bench)
            row_of = block * bench + lax.broadcasted_iota(jnp.int32, (bench, reach), 0)
            place = lax.broadcasted_iota(jnp.int32, (bench, reach), 1)
            seen = (place <= row_of) | (place < limit)
            q = buf2[span, q_at]
            k = buf2[0:reach, k_at]
            v = buf2[0:reach, v_at]
            do = buf5[span, o_at]
            scores = jnp.where(seen, row_dot(q, k), -1e30)
            probs = jnp.exp(scores - lse_v[head, span, 0:1])
            d_probs = row_dot(do, v)
            inner = jnp.sum(probs * d_probs, axis=-1, keepdims=True)
            d_scores = (probs * (d_probs - inner)).astype(BF16)
            flip = (((0,), (0,)), ((), ()))
            dv_sum[0:reach, :] += lax.dot_general(probs.astype(BF16), do, flip, preferred_element_type=F32)
            dk_sum[0:reach, :] += lax.dot_general(d_scores, q, flip, preferred_element_type=F32)
            dq = jnp.dot(d_scores, k, preferred_element_type=F32) * scale
            biases[4:5, q_at] += jnp.sum(dq, axis=0, keepdims=True)
            buf5[span, q_at] = dq.astype(BF16)
        buf5[:, k_at] = dk_sum[...].astype(BF16)
        buf5[:, v_at] = dv_sum[...].astype(BF16)
        biases[5:6, q_at] += jnp.sum(dv_sum[...], axis=0, keepdims=True)
        return carry

    lax.fori_loop(0, heads, attend, 0)
    load_n.wait()
    qkv.produce(1)
    qkv.produce(2)
    up.serve(3)
    qkv.produce(3)
    load_w.wait()

    def h1_part(rank, index):
        return row_dot(buf5[block_of(rank, rows), 0:triple], weight_v[block_of(index, 512), 0:triple])

    def take_h1(index, total):
        spare[:, block_of(index, 512)] = total

    pl.semaphore_wait(ready, 2)
    end = tensor_sum(spot, h1_part, *tensor, s_send, s_recv, take_h1)
    up.serve(0)
    qkv.produce(0)
    qkv.serve(1)
    out.produce(1)
    end()
    load_t.wait()

    def back1(index, carry):
        where = block_of(index, strip)
        dx = norm_back(line[where, :].astype(F32), sums[0:1, :], spare[where, :], input_grad[where, :], 0)
        input_grad[where, :] = dx
        return carry

    lax.fori_loop(0, rows // strip, back1, 0)
    share = grad_up.shape[0]
    vector_copies, bias_copies = [], []
    for step in range(1, count):
        peer = lax.rem(spot.dp + step, count)
        vector_copies.append(remote(
            vectors.at[:, block_of(peer, share)], vector_in.at[spot.dp], v_send.at[step], v_recv.at[step], peer,
            spot.tensor,
        ))
        bias_copies.append(remote(biases, bias_in.at[spot.dp], b_send.at[step], b_recv.at[step], peer, spot.tensor))
    for copy in vector_copies + bias_copies:
        copy.start()
    vector_in[spot.dp] = vectors[:, block_of(spot.dp, share)]
    bias_in[spot.dp] = biases[...]
    up.settle()
    qkv.serve(2)
    out.produce(2)
    for copy in vector_copies + bias_copies:
        copy.wait_recv()
    total, bias_total = vector_in[0], bias_in[0]
    for index in range(1, count):
        total = total + vector_in[index]
        bias_total = bias_total + bias_in[index]
    part_sum[...] = total
    bias_sums[...] = bias_total
    part_copies = [
        remote(part_sum, part_in.at[spot.tensor], t_send.at[slot], t_recv.at[slot], spot.dp, peer)
        for slot, peer in enumerate((spot.x_peer, spot.core_peer, spot.far_peer))
    ]
    for copy in part_copies:
        copy.start()
    part_in[spot.tensor] = part_sum[...]
    qkv.serve(3)
    out.produce(3)
    for copy in part_copies:
        copy.wait_recv()
    vector_sums[...] = part_in[0] + part_in[1] + part_in[2] + part_in[3]
    qkv.serve(0)
    out.produce(0)
    out.serve(1)
    out.serve(2)
    out.serve(3)
    for copy in vector_copies + bias_copies + part_copies:
        copy.wait_send()
    qkv.settle()
    out.serve(0)
    out.settle()
    for copy in list(shared["y_busy"].values()) + list(shared["z_busy"].values()):
        copy.wait_send()


def backward_call(heads, count, prefix, sums, tokens, cotangent, weights, saved):
    rows, features = tokens.shape
    length = rows * 4
    share = features // count
    wqkv, wo, w1, w2 = weights
    width, hidden, triple = wo.shape[0], w1.shape[1], wqkv.shape[1]
    outer, inner = split_of(count)
    shape = jax.ShapeDtypeStruct
    hbm = pl.BlockSpec(memory_space=pl.ANY)
    vmem = pl.BlockSpec(memory_space=pltpu.VMEM)
    dma = pltpu.SemaphoreType.DMA
    regular = pltpu.SemaphoreType.REGULAR
    wide = (length, features)
    return pl.pallas_call(
        functools.partial(backward_kernel, heads, count),
        out_shape=[
            shape((rows, features), BF16),
            shape((rows, features), F32),
            shape((share, hidden), F32),
            shape((share, hidden), F32),
            shape((share, width), F32),
            shape((share, triple), F32),
            shape((8, share), F32),
            shape((8, 512), F32),
            shape((outer - 1, share, hidden), BF16),
            shape((outer - 1, share, hidden), BF16),
            shape((outer - 1, share, width), BF16),
            shape((outer - 1, share, triple), BF16),
        ],
        in_specs=[pl.BlockSpec(memory_space=pltpu.SMEM), vmem] + [hbm] * 10 + [vmem] + [hbm] * 4,
        out_specs=[vmem] * 2 + [hbm] * 4 + [vmem] * 2 + [hbm] * 4,
        scratch_shapes=[
            pltpu.VMEM((hidden, features), BF16),
            pltpu.VMEM(wide, BF16),
            pltpu.VMEM(wide, BF16),
            pltpu.VMEM(wide, BF16),
            pltpu.VMEM(wide, BF16),
            pltpu.VMEM(wide, BF16),
            pltpu.VMEM(wide, BF16),
            pltpu.VMEM((2, rows, features), BF16),
            pltpu.VMEM((2, rows, features), BF16),
            pltpu.VMEM((rows, features), BF16),
            pltpu.VMEM((rows, features), BF16),
            pltpu.VMEM((outer, share, hidden), BF16),
            pltpu.VMEM((outer, share, hidden), BF16),
            pltpu.VMEM((outer, share, hidden), BF16),
            pltpu.VMEM((4, outer - 1, share, 128), BF16),
            pltpu.VMEM((4, share, 128), F32),
            pltpu.VMEM((rows, features), F32),
            pltpu.VMEM((rows, features), BF16),
            pltpu.VMEM((length, width // heads), F32),
            pltpu.VMEM((length, width // heads), F32),
            pltpu.VMEM((8, features), F32),
            pltpu.VMEM((8, 512), F32),
            pltpu.VMEM((count, 8, share), F32),
            pltpu.VMEM((count, 8, 512), F32),
            pltpu.VMEM((8, share), F32),
            pltpu.VMEM((4, 8, share), F32),
            dma((outer,)),
            dma((outer,)),
            dma((outer,)),
            dma((4, outer)),
            dma((3,)),
            dma((3,)),
            dma((3,)),
            dma((3,)),
            dma((count,)),
            dma((count,)),
            dma((count,)),
            dma((count,)),
            dma((3,)),
            dma((3,)),
            dma((8,)),
            dma((8,)),
            regular,
            regular,
        ],
        compiler_params=pltpu.CompilerParams(
            collective_id=1, has_side_effects=True, vmem_limit_bytes=VMEM_BYTES
        ),
    )(prefix, sums, tokens, cotangent, wqkv, wo, w1, w2, *saved)


def pack_small(biases, vectors):
    devices = lax.axis_size("dp")
    parts = jnp.concatenate(biases, axis=0)
    lane = lax.broadcasted_iota(jnp.int32, (parts.shape[0], parts.shape[1] * devices), 1)
    wide = jnp.where(lane // parts.shape[1] == lax.axis_index("dp"), jnp.tile(parts, (1, devices)), 0)
    halves = jnp.pad(jnp.stack(vectors), ((0, 2), (0, 0)))
    return jnp.concatenate([wide, halves[:, :128], halves[:, 128:]], axis=0).astype(F32)


def layer_norm(rows, gain, shift):
    center = rows - jnp.mean(rows, axis=-1, keepdims=True)
    spread = jnp.mean(center * center, axis=-1, keepdims=True)
    return center * lax.rsqrt(spread + 1e-05) * gain + shift


def gelu_exact(values):
    return jax.nn.gelu(values, approximate=False)


def head_major(matrix, heads):
    return matrix.reshape(matrix.shape[0], heads, -1).transpose(1, 0, 2)


def row_major(stacked):
    return stacked.transpose(1, 0, 2).reshape(stacked.shape[1], -1)


def masked_scores(q_block, keys, start, prefix_len):
    scores = jnp.einsum("hqd,hkd->hqk", q_block, keys, preferred_element_type=jnp.float32)
    rows = start + lax.broadcasted_iota(jnp.int32, scores.shape[1:], 0)
    cols = lax.broadcasted_iota(jnp.int32, scores.shape[1:], 1)
    seen = (cols <= rows) | (cols < prefix_len)
    return jnp.where(seen[None], scores, -1e30)


def to_blocks(stacked, count):
    heads, length = (stacked.shape[0], stacked.shape[1])
    return stacked.reshape((heads, count, length // count) + stacked.shape[2:]).swapaxes(0, 1)


def from_blocks(blocked):
    count, heads, block = (blocked.shape[0], blocked.shape[1], blocked.shape[2])
    return blocked.swapaxes(0, 1).reshape((heads, count * block) + blocked.shape[3:])


def contract_rows(left, right):
    return jnp.einsum("ld,le->de", left, right, preferred_element_type=jnp.float32)


def times_transpose(left, right):
    return jnp.einsum("le,de->ld", left, right, preferred_element_type=jnp.float32)


def plain(
    tokens,
    prefix,
    query_weight,
    key_weight,
    value_weight,
    out_weight,
    query_bias,
    value_bias,
    up_weight,
    down_weight,
    up_bias,
    norm1_gain,
    norm1_bias,
    norm2_gain,
    norm2_bias,
    out_bias,
    down_bias,
    cotangent,
):
    f32 = jnp.float32
    bf16 = jnp.bfloat16
    devices = lax.axis_size("dp")
    small = (query_bias, value_bias, up_bias, norm1_gain, norm1_bias, norm2_gain, norm2_bias, out_bias, down_bias)
    packed = jnp.concatenate([part.reshape(-1) for part in small])
    packed = lax.all_gather(packed, "dp", axis=0, tiled=False)
    pieces = []
    offset = 0
    for part in small:
        piece = packed[:, offset : offset + part.size].reshape((devices,) + part.shape)
        offset += part.size
        pieces.append(jnp.moveaxis(piece, 0, -2).reshape(part.shape[:-1] + (-1,)))
    bq, bv, b1, g1, n1, g2, n2, bo, b2 = pieces
    wq, wk, wv, wo = (
        lax.all_gather(query_weight, "dp", axis=0, tiled=True),
        lax.all_gather(key_weight, "dp", axis=0, tiled=True),
        lax.all_gather(value_weight, "dp", axis=0, tiled=True),
        lax.all_gather(out_weight, "dp", axis=1, tiled=True),
    )
    w1, w2 = (
        lax.all_gather(up_weight, "dp", axis=0, tiled=True),
        lax.all_gather(down_weight, "dp", axis=1, tiled=True),
    )
    g1f, n1f, g2f, n2f = (g1.astype(f32), n1.astype(f32), g2.astype(f32), n2.astype(f32))
    bof, b2f = (bo.astype(f32), b2.astype(f32))
    heads = bq.shape[0]
    head_size = bq.shape[1]
    scale = head_size ** (-0.5)
    prefix_len = prefix[0]
    xf = tokens.astype(f32)
    h1 = layer_norm(xf, g1f, n1f).astype(bf16)
    rows1 = lax.all_gather(h1, "tensor", axis=0, tiled=True)
    length = rows1.shape[0]
    block = min(512, length)
    count = length // block
    query = (
        (jnp.dot(rows1, wq, preferred_element_type=f32) + bq.astype(f32).reshape(-1)) * scale
    ).astype(bf16)
    keyed = jnp.dot(rows1, wk, preferred_element_type=f32).astype(bf16)
    valued = (jnp.dot(rows1, wv, preferred_element_type=f32) + bv.astype(f32).reshape(-1)).astype(
        bf16
    )
    q_heads = head_major(query, heads)
    k_heads = head_major(keyed, heads)
    v_heads = head_major(valued, heads)
    q_blocks = to_blocks(q_heads, count)
    starts = jnp.arange(count, dtype=jnp.int32) * block

    def forward_block(item):
        q_block, start = item
        scores = masked_scores(q_block, k_heads, start, prefix_len)
        top = jnp.max(scores, axis=-1, keepdims=True)
        expd = jnp.exp(scores - top)
        total = jnp.sum(expd, axis=-1, keepdims=True)
        probs = (expd / total).astype(bf16)
        outv = jnp.einsum("hqk,hkd->hqd", probs, v_heads, preferred_element_type=f32)
        return (outv.astype(bf16), (top + jnp.log(total))[..., 0])

    o_blocks, lse_blocks = lax.map(forward_block, (q_blocks, starts))
    mixed = row_major(from_blocks(o_blocks))
    attn_part = jnp.dot(mixed, wo, preferred_element_type=f32)
    attn_total = lax.psum_scatter(attn_part.astype(bf16), "tensor", scatter_dimension=0, tiled=True).astype(f32)
    second = xf + attn_total + bof
    h2 = layer_norm(second, g2f, n2f).astype(bf16)
    rows2 = lax.all_gather(h2, "tensor", axis=0, tiled=True)
    hidden = jnp.dot(rows2, w1, preferred_element_type=f32) + b1.astype(f32).reshape(-1)
    gated = gelu_exact(hidden).astype(bf16)
    mlp_part = jnp.dot(gated, w2, preferred_element_type=f32)
    mlp_total = lax.psum_scatter(
        mlp_part.astype(jnp.bfloat16), "tensor", scatter_dimension=0, tiled=True
    ).astype(jnp.float32)
    layer_out = (second + mlp_total + b2f).astype(bf16)
    d_out = cotangent.astype(f32)
    g_b2 = jnp.sum(d_out, axis=0)
    d_rows = lax.all_gather(cotangent, "tensor", axis=0, tiled=True)
    d_gated = times_transpose(d_rows, w2)
    d_hidden = jax.vjp(gelu_exact, hidden)[1](d_gated)[0]
    g_b1 = jnp.sum(d_hidden, axis=0).reshape(b1.shape)
    d_hidden_low = d_hidden.astype(bf16)
    d_h2_part = times_transpose(d_hidden_low, w1)
    g_w2 = contract_rows(gated, d_rows)
    g_w1 = contract_rows(rows2, d_hidden_low)
    d_h2 = lax.psum_scatter(d_h2_part.astype(bf16), "tensor", scatter_dimension=0, tiled=True).astype(f32)
    norm2_back = jax.vjp(layer_norm, second, g2f, n2f)[1]
    d_second_ln, g_g2, g_n2 = norm2_back(d_h2)
    d_second = d_out + d_second_ln
    g_bo = jnp.sum(d_second, axis=0)
    d_second_low = d_second.astype(bf16)
    back_rows = lax.all_gather(d_second_low, "tensor", axis=0, tiled=True)
    g_wo = contract_rows(mixed, back_rows)
    d_mixed = times_transpose(back_rows, wo).astype(bf16)
    do_blocks = to_blocks(head_major(d_mixed, heads), count)

    def backward_block(carry, item):
        d_keys, d_vals = carry
        q_block, do_block, lse_block, start = item
        scores = masked_scores(q_block, k_heads, start, prefix_len)
        probs = jnp.exp(scores - lse_block[..., None])
        d_probs = jnp.einsum("hqd,hkd->hqk", do_block, v_heads, preferred_element_type=f32)
        d_vals = d_vals + jnp.einsum(
            "hqk,hqd->hkd", probs.astype(bf16), do_block, preferred_element_type=f32
        )
        inner = jnp.sum(probs * d_probs, axis=-1, keepdims=True)
        d_scores = (probs * (d_probs - inner)).astype(bf16)
        d_query = jnp.einsum("hqk,hkd->hqd", d_scores, k_heads, preferred_element_type=f32)
        d_keys = d_keys + jnp.einsum("hqk,hqd->hkd", d_scores, q_block, preferred_element_type=f32)
        return ((d_keys, d_vals), d_query)

    empty = jnp.zeros(k_heads.shape, f32)
    (d_keys, d_vals), dq_blocks = lax.scan(
        backward_block, (empty, empty), (q_blocks, do_blocks, lse_blocks, starts)
    )
    d_query = row_major(from_blocks(dq_blocks)) * scale
    d_keys = row_major(d_keys)
    d_vals = row_major(d_vals)
    g_bq = jnp.sum(d_query, axis=0).reshape(bq.shape)
    g_bv = jnp.sum(d_vals, axis=0).reshape(bv.shape)
    dq_low, dk_low, dv_low = (d_query.astype(bf16), d_keys.astype(bf16), d_vals.astype(bf16))
    g_wq = contract_rows(rows1, dq_low)
    g_wk = contract_rows(rows1, dk_low)
    g_wv = contract_rows(rows1, dv_low)
    d_h1_part = (
        times_transpose(dq_low, wq) + times_transpose(dk_low, wk) + times_transpose(dv_low, wv)
    )
    d_h1 = lax.psum_scatter(d_h1_part.astype(bf16), "tensor", scatter_dimension=0, tiled=True).astype(f32)
    norm1_back = jax.vjp(layer_norm, xf, g1f, n1f)[1]
    d_input_ln, g_g1, g_n1 = norm1_back(d_h1)
    input_grad = d_second + d_input_ln
    def scatter(part, dim):
        return lax.psum_scatter(part.astype(bf16), "dp", scatter_dimension=dim, tiled=True).astype(f32)

    s_w2, s_w1, s_wo = scatter(g_w2, 1), scatter(g_w1, 0), scatter(g_wo, 1)
    s_wq, s_wk, s_wv = scatter(g_wq, 0), scatter(g_wk, 0), scatter(g_wv, 0)

    def by_device(part):
        return jnp.moveaxis(part.reshape(part.shape[:-1] + (devices, -1)), -2, 0).reshape(devices, -1)

    rows = [by_device(part) for part in (g_bq, g_bv, g_b1, g_g1, g_n1, g_g2, g_n2, g_bo, g_b2)]
    total = lax.psum_scatter(jnp.concatenate(rows, axis=1), "dp", scatter_dimension=0, tiled=True)[0]
    offset = 0
    outs = []
    for part in (query_bias, value_bias, up_bias):
        outs.append(total[offset : offset + part.size].reshape(part.shape))
        offset += part.size
    s_bq, s_bv, s_b1 = outs
    vectors = lax.psum_scatter(
        total[offset:].reshape(6, lax.axis_size("tensor"), -1), "tensor", scatter_dimension=1, tiled=True
    ).reshape(6, -1)
    s_g1, s_n1, s_g2, s_n2, s_bo, s_b2 = (vectors[index] for index in range(6))
    return (
        layer_out,
        input_grad,
        s_wq,
        s_wk,
        s_wv,
        s_wo,
        s_bq,
        s_bv,
        s_w1,
        s_w2,
        s_b1,
        s_g1,
        s_n1,
        s_g2,
        s_n2,
        s_bo,
        s_b2,
    )


def fast(
    tokens,
    prefix,
    query_weight,
    key_weight,
    value_weight,
    out_weight,
    query_bias,
    value_bias,
    up_weight,
    down_weight,
    up_bias,
    norm1_gain,
    norm1_bias,
    norm2_gain,
    norm2_bias,
    out_bias,
    down_bias,
    cotangent,
):
    devices = lax.axis_size("dp")
    me = lax.axis_index("dp")
    heads = query_bias.shape[0]
    small = pack_small(
        (query_bias, value_bias, up_bias), (norm1_gain, norm1_bias, norm2_gain, norm2_bias, out_bias, down_bias)
    )
    results = forward_call(
        heads, devices, prefix, tokens, cotangent, small,
        jnp.concatenate([query_weight, key_weight, value_weight], axis=1), out_weight, up_weight, down_weight,
    )
    layer_out, input_grad, g_w2, g_w1, g_wo, g_qkv, vectors, biases, *_ = backward_call(
        heads, devices, prefix, results[-1], tokens, cotangent, results[:4], results[4:-1]
    )
    g_wq, g_wk, g_wv = jnp.split(g_qkv, 3, axis=1)
    vectors = vectors.reshape(8, lax.axis_size("tensor"), -1)
    vectors = lax.dynamic_index_in_dim(vectors, lax.axis_index("tensor"), axis=1, keepdims=False)

    def own(flat, part):
        whole = flat.reshape(part.shape[0], -1)
        return lax.dynamic_slice_in_dim(whole, me * part.shape[1], part.shape[1], axis=1)

    width = out_weight.shape[0]
    up_size = up_bias.size * devices
    g_b1 = own(biases[: up_size // 512].reshape(-1), up_bias)
    g_bq = own(biases[4, :width], query_bias)
    g_bv = own(biases[5, :width], value_bias)
    return (
        layer_out, input_grad, g_wq, g_wk, g_wv, g_wo.T, g_bq, g_bv, g_w1, g_w2.T, g_b1,
        vectors[0], vectors[1], vectors[2], vectors[3], vectors[4], vectors[5],
    )


def local(*args):
    tokens, query_weight, up_weight = args[0], args[2], args[8]
    devices = lax.axis_size("dp")
    features = tokens.shape[1]
    share = features // devices
    fits = (
        lax.axis_size("tensor") == 4
        and devices == 8
        and share % 128 == 0
        and tokens.shape[0] == 256
        and query_weight.shape[1] == 512
        and args[6].shape[0] == 4
        and features == 2048
        and up_weight.shape[1] == 2048
    )
    return fast(*args) if fits else plain(*args)


def solution(mesh):
    in_specs = (
        P(("dp", "tensor"), None),
        P("dp"),
        P("dp", "tensor"),
        P("dp", "tensor"),
        P("dp", "tensor"),
        P("tensor", "dp"),
        P("tensor", "dp"),
        P("tensor", "dp"),
        P("dp", "tensor"),
        P("tensor", "dp"),
        P("tensor", "dp"),
        P("dp"),
        P("dp"),
        P("dp"),
        P("dp"),
        P("dp"),
        P("dp"),
        P(("dp", "tensor"), None),
    )
    out_specs = (
        P(("dp", "tensor"), None),
        P(("dp", "tensor"), None),
        P("dp", "tensor"),
        P("dp", "tensor"),
        P("dp", "tensor"),
        P("tensor", "dp"),
        P("tensor", "dp"),
        P("tensor", "dp"),
        P("dp", "tensor"),
        P("tensor", "dp"),
        P("tensor", "dp"),
        P(("dp", "tensor")),
        P(("dp", "tensor")),
        P(("dp", "tensor")),
        P(("dp", "tensor")),
        P(("dp", "tensor")),
        P(("dp", "tensor")),
    )
    return jax.shard_map(local, mesh=mesh, in_specs=in_specs, out_specs=out_specs, check_vma=False)
```

```python
import functools

import jax
import jax.numpy as jnp
from jax import lax
from jax.experimental import pallas as pl
from jax.experimental.pallas import tpu as pltpu
from jax.sharding import PartitionSpec as P

MESH = pl.DeviceIdType.MESH
F32 = jnp.float32
BF16 = jnp.bfloat16
PREFIX_TOP = 512
VMEM_BYTES = 67043328


def split_of(count):
    inner = 1
    for size in range(1, count + 1):
        if size * size <= count and count % size == 0:
            inner = size
    return count // inner, inner


def remote(source, target, send_sem, recv_sem, dp, tensor):
    return pltpu.make_async_remote_copy(
        src_ref=source,
        dst_ref=target,
        send_sem=send_sem,
        recv_sem=recv_sem,
        device_id=(dp, tensor),
        device_id_type=MESH,
    )


def block_of(index, size):
    return pl.ds(pl.multiple_of(index * size, size), size)


class Spot:
    def __init__(self, count):
        self.outer, self.inner = split_of(count)
        self.count = count
        self.dp = lax.axis_index("dp")
        self.tensor = lax.axis_index("tensor")
        self.row = lax.div(self.dp, self.inner)
        self.column = lax.rem(self.dp, self.inner)
        self.core_peer = self.tensor + 1 - 2 * lax.rem(self.tensor, 2)
        self.x_peer = lax.rem(self.tensor + 2, 4)
        self.far_peer = lax.rem(self.core_peer + 2, 4)

    def across(self, step):
        return lax.rem(self.row + step, self.outer) * self.inner + self.column

    def beside(self, step, row=None):
        return (self.row if row is None else row) * self.inner + lax.rem(self.column + step, self.inner)

    def meet(self, far=False):
        barrier = pltpu.get_barrier_semaphore()
        for step in range(1, self.count):
            pl.semaphore_signal(
                barrier, inc=1, device_id=(lax.rem(self.dp + step, self.count), self.tensor), device_id_type=MESH
            )
        for peer in (self.core_peer, self.x_peer) + ((self.far_peer,) if far else ()):
            pl.semaphore_signal(barrier, inc=1, device_id=(self.dp, peer), device_id_type=MESH)
        pl.semaphore_wait(barrier, self.count + 1 + far)

    def release(self, ready):
        for peer in (self.core_peer, self.x_peer):
            pl.semaphore_signal(ready, inc=1, device_id=(self.dp, peer), device_id_type=MESH)


class Spread:
    AHEAD = 3

    def __init__(self, spot, pieces, late, own_at, sems):
        self.spot, self.pieces, self.late, self.sems = spot, pieces, late, sems
        self.flows = [(piece, 0) for piece in range(len(pieces)) if piece != late] + [(late, 0), (late, 1)]
        self.own_at = own_at
        self.order = (2, jnp.where(spot.row == 0, 3, 1), jnp.where(spot.row == 0, 1, 3))
        self.sent = []
        self.todo = [(flow, place) for flow in range(len(self.flows)) for place in range(3)]
        for piece in own_at[None]:
            self.send_own(piece)
        for flow in range(self.AHEAD):
            self.send_rows(flow)

    def owner(self, row, side):
        return row * 2 + lax.rem(self.spot.column + side, 2)

    def launch(self, condition, copy):
        if condition is None:
            copy().start()
        else:
            pl.when(condition)(lambda: copy().start())
        self.sent.append((condition, copy))

    def along(self, flow, step, source_row, target_row, send_slot):
        piece, side = self.flows[flow]
        source, target = self.pieces[piece]
        place = target(self.owner(source_row, side))
        if source_row is not self.spot.row or side:
            source = place
        return remote(
            source, place, self.sems[0].at[flow, send_slot], self.sems[1].at[flow, step],
            target_row * 2 + self.spot.column, self.spot.tensor,
        )

    def send_rows(self, flow):
        row = self.spot.row
        if self.flows[flow][1]:
            self.beside(self.late, 0, row).wait_recv()
        for step, condition in ((2, None), (1, row != 3), (3, row != 0)):
            self.launch(
                condition,
                functools.partial(self.along, flow, step, row, lax.rem(row + step, 4), step),
            )

    def hand_over(self, flow):
        row = self.spot.row
        self.launch(
            (row == 1) | (row == 2),
            lambda: self.along(flow, 2 * row - 1, lax.rem(row + 2, 4), (row - 1) * 3, 0),
        )

    def beside(self, piece, step, source_row):
        spot = self.spot
        source, target = self.pieces[piece]
        place = target(self.owner(source_row, 0))
        if source_row is not spot.row:
            source = place
        return remote(
            source, place, self.sems[2].at[piece, step], self.sems[3].at[piece, step], spot.beside(1), spot.tensor
        )

    def beside_arrival(self, piece, step, source_row):
        source, target = self.pieces[piece]
        return remote(
            source, target(self.owner(source_row, 1)), self.sems[2].at[piece, step], self.sems[3].at[piece, step],
            self.spot.beside(1), self.spot.tensor,
        )

    def send_own(self, piece):
        self.launch(None, functools.partial(self.beside, piece, 0, self.spot.row))

    def forward(self, count):
        for _ in range(count):
            if not self.todo:
                return
            flow, place = self.todo.pop(0)
            step = self.order[place]
            row = lax.rem(self.spot.row + 4 - step, 4)
            self.along(flow, step, row, self.spot.row, 0).wait_recv()
            if place == 0:
                self.hand_over(flow)
            piece = self.flows[flow][0]
            if piece != self.late:
                self.launch(None, functools.partial(self.beside, piece, step, row))
            if place == 2:
                if flow + self.AHEAD < len(self.flows):
                    self.send_rows(flow + self.AHEAD)
                for own in self.own_at.get(flow, ()):
                    self.send_own(own)

    def arrived(self, piece):
        while self.todo and self.flows[self.todo[0][0]][0] <= piece:
            self.forward(1)
        if piece != self.late:
            for step in range(4):
                self.beside_arrival(piece, step, lax.rem(self.spot.row + 4 - step, 4)).wait_recv()

    def finish(self):
        for condition, copy in self.sent:
            if condition is None:
                copy().wait_send()
            else:
                pl.when(condition)(lambda copy=copy: copy().wait_send())


class TensorGather:
    def __init__(self, spot, own, full, rows, send, recv):
        self.spot, self.full, self.rows, self.send, self.recv = spot, full, rows, send, recv
        place = self.at(spot.tensor)
        self.to_x = remote(own, place, send.at[0], recv.at[0], spot.dp, spot.x_peer)
        self.to_core = remote(own, place, send.at[1], recv.at[1], spot.dp, spot.core_peer)
        self.to_x.start()
        self.to_core.start()

    def at(self, index):
        return self.full.at[block_of(index, self.rows)]

    def pass_on(self):
        self.to_x.wait_recv()
        place = self.at(self.spot.x_peer)
        self.on = remote(place, place, self.send.at[2], self.recv.at[2], self.spot.dp, self.spot.core_peer)
        self.on.start()

    def finish(self):
        self.to_core.wait_recv()
        self.on.wait_recv()
        for copy in (self.to_x, self.to_core, self.on):
            copy.wait_send()


def tensor_sum(spot, product, core_send, core_recv, x_send, x_recv, send, recv, finish, between=None):
    width = core_send.shape[2]
    chunk = 512
    count = width // chunk

    def fill(rank, target):
        def body(index, carry):
            target[:, block_of(index, chunk)] = product(rank, index).astype(BF16)
            return carry

        lax.fori_loop(0, count, body, 0)

    copies = []
    for slot, rank in enumerate((spot.far_peer, spot.core_peer)):
        fill(rank, core_send.at[slot])
        copy = remote(core_send.at[slot], core_recv.at[slot], send.at[slot], recv.at[slot], spot.dp, spot.core_peer)
        copy.start()
        copies.append(copy)
    if between is not None:
        between()
    copies[0].wait_recv()

    def join(index, carry):
        where = block_of(index, chunk)
        x_send[:, where] = (product(spot.x_peer, index) + core_recv[0, :, where].astype(F32)).astype(BF16)
        return carry

    lax.fori_loop(0, count, join, 0)
    over = remote(x_send, x_recv, send.at[2], recv.at[2], spot.dp, spot.x_peer)
    over.start()
    copies[1].wait_recv()

    def end():
        over.wait_recv()

        def last(index, carry):
            where = block_of(index, chunk)
            total = product(spot.tensor, index) + core_recv[1, :, where].astype(F32) + x_recv[:, where].astype(F32)
            finish(index, total)
            return carry

        lax.fori_loop(0, count, last, 0)
        for copy in copies + [over]:
            copy.wait_send()

    return end


def normal_parts(rows):
    center = rows - jnp.mean(rows, axis=-1, keepdims=True)
    spread = jnp.mean(center * center, axis=-1, keepdims=True)
    return center, lax.rsqrt(spread + 1e-05)


def forward_kernel(
    heads,
    count,
    prefix,
    tokens,
    cotangent,
    small,
    qkv_shard,
    out_shard,
    up_shard,
    down_shard,
    wqkv,
    wo,
    w1,
    w2,
    h1_all,
    d_rows,
    qkv_all,
    mixed_all,
    lse_all,
    second,
    h2_all,
    gated_all,
    slope_all,
    sums,
    smalls,
    h1v,
    wqkv_v,
    qkv_v,
    mixed_v,
    lse_v,
    wo_v,
    core_send,
    core_recv,
    x_send,
    x_recv,
    h2v,
    w1_v,
    gated_v,
    slope_v,
    small_send,
    small_recv,
    z_send,
    z_recv,
    y_send,
    y_recv,
    g_send,
    g_recv,
    s_send,
    s_recv,
    local_sem,
):
    spot = Spot(count)
    rows, features = tokens.shape
    length = h1v.shape[0]
    depth = qkv_shard.shape[0]
    width = wo_v.shape[0]
    hidden = up_shard.shape[1]
    half = depth // 2
    tall = hidden // 2
    pieces = [
        (qkv_shard.at[pl.ds(part * half, half)],
         lambda owner, part=part: wqkv.at[block_of(owner * 2 + part, half)])
        for part in range(2)
    ]
    pieces.append((out_shard, lambda owner: wo.at[:, block_of(owner, depth)]))
    pieces += [
        (up_shard.at[:, pl.ds(part * tall, tall)],
         lambda owner, part=part: w1.at[block_of(owner, depth), pl.ds(part * tall, tall)])
        for part in range(2)
    ]
    pieces += [
        (down_shard.at[pl.ds(part * tall, tall)],
         lambda owner, part=part: w2.at[pl.ds(part * tall, tall), block_of(owner, depth)])
        for part in range(2)
    ]
    locals_ = []

    def keep(source, target):
        copy = pltpu.make_async_copy(source, target, local_sem.at[len(locals_)])
        copy.start()
        locals_.append(copy)

    spot.meet()
    small_copies = []
    for step in range(1, count):
        copy = remote(
            small, smalls.at[spot.dp], small_send.at[step], small_recv.at[step],
            lax.rem(spot.dp + step, count), spot.tensor,
        )
        copy.start()
        small_copies.append(copy)
    spread = Spread(
        spot, pieces, 6, {None: (0, 1, 2, 3), 0: (4,), 1: (6,), 2: (5,)}, (z_send, z_recv, y_send, y_recv)
    )
    for source, target in pieces:
        keep(source, target(spot.dp))
    smalls[spot.dp] = small[...]
    for step in range(1, count):
        owner = lax.rem(spot.dp + count - step, count)
        remote(
            small, smalls.at[owner], small_send.at[step], small_recv.at[step], spot.dp, spot.core_peer
        ).wait_recv()
    sums[...] = jnp.zeros_like(sums)
    joint = smalls[0, 0:24, :]
    for index in range(1, count):
        joint = joint + smalls[index, 0:24, :]
    lanes = 128
    for head in range(heads):
        sums[6:7, head * lanes : (head + 1) * lanes] = joint[head : head + 1, :]
        start = 2 * width + head * lanes
        sums[6:7, start : start + lanes] = joint[4 + head : 5 + head, :]
    for line in range(hidden // lanes):
        sums[7:8, line * lanes : (line + 1) * lanes] = joint[8 + line : 9 + line, :]
    for owner in range(count):
        for part in range(2):
            start = owner * depth + part * lanes
            sums[0:6, start : start + lanes] = smalls[owner, 24 + 8 * part : 30 + 8 * part, :]

    strip = 32
    base = spot.tensor * rows

    def norm1(index, carry):
        where = block_of(index, strip)
        center, scale = normal_parts(tokens[where, :].astype(F32))
        h1v[pl.ds(pl.multiple_of(base + index * strip, strip), strip), :] = (
            center * scale * sums[0:1, :] + sums[1:2, :]
        ).astype(BF16)
        return carry

    lax.fori_loop(0, rows // strip, norm1, 0)
    gather1 = TensorGather(spot, h1v.at[block_of(spot.tensor, rows)], h1v, rows, g_send.at[0], g_recv.at[0])
    gather_d = TensorGather(spot, cotangent, d_rows, rows, g_send.at[1], g_recv.at[1])
    keep(cotangent, d_rows.at[block_of(spot.tensor, rows)])
    spread.forward(1)
    gather1.pass_on()
    spread.forward(2)
    gather_d.pass_on()
    gather1.finish()
    keep(h1v, h1_all)
    spread.forward(6)
    spread.arrived(0)
    spread.arrived(1)
    for copy in locals_[:2]:
        copy.wait()
    load = pltpu.make_async_copy(wqkv, wqkv_v, local_sem.at[14])
    load.start()
    load.wait()

    def project(index, carry):
        where = block_of(index, rows)
        for part in range(3):
            lanes = slice(part * width, (part + 1) * width)
            value = jnp.dot(h1v[where, :], wqkv_v[:, lanes], preferred_element_type=F32) + sums[6:7, lanes]
            if part == 0:
                value = value * (width // heads) ** -0.5
            qkv_v[where, lanes] = value.astype(BF16)
        return carry

    lax.fori_loop(0, length // rows, project, 0)
    keep(qkv_v, qkv_all)
    spread.forward(3)
    size = width // heads
    limit = prefix[0]
    bench = 256

    for block in range(length // bench):
        reach = min(length, max((block + 1) * bench, PREFIX_TOP))
        span = slice(block * bench, (block + 1) * bench)

        def attend(head, carry, block=block, span=span, reach=reach):
            line = block * bench + lax.broadcasted_iota(jnp.int32, (bench, reach), 0)
            place = lax.broadcasted_iota(jnp.int32, (bench, reach), 1)
            seen = (place <= line) | (place < limit)
            q = qkv_v[span, block_of(head, size)]
            k = qkv_v[0:reach, pl.ds(pl.multiple_of(width + head * size, size), size)]
            v = qkv_v[0:reach, pl.ds(pl.multiple_of(2 * width + head * size, size), size)]
            scores = lax.dot_general(q, k, (((1,), (1,)), ((), ())), preferred_element_type=F32)
            scores = jnp.where(seen, scores, -1e30)
            top = jnp.max(scores, axis=-1, keepdims=True)
            expd = jnp.exp(scores - top)
            total = jnp.sum(expd, axis=-1, keepdims=True)
            probs = (expd * (1.0 / total)).astype(BF16)
            mixed_v[span, block_of(head, size)] = jnp.dot(probs, v, preferred_element_type=F32).astype(BF16)
            lse_v[head, span, :] = jnp.broadcast_to(top + jnp.log(total), (bench, 128))
            return carry

        lax.fori_loop(0, heads, attend, 0)
        if block == 2:
            spread.forward(2)
    keep(mixed_v, mixed_all)
    keep(lse_v, lse_all)
    spread.forward(1)
    spread.arrived(2)
    locals_[2].wait()
    load = pltpu.make_async_copy(wo, wo_v, local_sem.at[14])
    load.start()
    load.wait()

    def out_part(rank, index):
        return jnp.dot(mixed_v[block_of(rank, rows), :], wo_v[:, block_of(index, 512)], preferred_element_type=F32)

    def take_second(index, total):
        where = block_of(index, 512)
        second[:, where] = tokens[:, where].astype(F32) + total + sums[4:5, where]

    end = tensor_sum(
        spot, out_part, core_send, core_recv, x_send, x_recv, s_send.at[0], s_recv.at[0], take_second
    )
    end()

    def norm2(index, carry):
        where = block_of(index, strip)
        center, scale = normal_parts(second[where, :])
        h2v[pl.ds(pl.multiple_of(base + index * strip, strip), strip), :] = (
            center * scale * sums[2:3, :] + sums[3:4, :]
        ).astype(BF16)
        return carry

    lax.fori_loop(0, rows // strip, norm2, 0)
    gather2 = TensorGather(spot, h2v.at[block_of(spot.tensor, rows)], h2v, rows, g_send.at[2], g_recv.at[2])
    gather2.pass_on()
    spread.forward(3)
    gather2.finish()
    gather_d.finish()
    keep(h2v, h2_all)
    stored = []
    for part in range(2):
        spread.arrived(3 + part)
        locals_[3 + part].wait()
        lanes_of = pl.ds(part * tall, tall)
        load = pltpu.make_async_copy(w1.at[:, lanes_of], w1_v.at[:, lanes_of], local_sem.at[14])
        load.start()
        load.wait()
        for block in range(length // rows):
            slot = block % 2
            if len(stored) >= 2:
                stored[-2].wait()

            def lift(index, carry, block=block, slot=slot, part=part):
                where = block_of(part * (tall // 512) + index, 512)
                u = jnp.dot(
                    h2v[block * rows : (block + 1) * rows, :], w1_v[:, where], preferred_element_type=F32
                ) + sums[7:8, where]
                below = 0.5 * (1.0 + lax.erf(u * 0.7071067811865476))
                gated_v[block * rows : (block + 1) * rows, where] = (u * below).astype(BF16)
                slope_v[slot, :, block_of(index, 512)] = below + u * (0.3989422804014327 * jnp.exp(-0.5 * u * u))
                return carry

            lax.fori_loop(0, tall // 512, lift, 0)
            copy = pltpu.make_async_copy(
                slope_v.at[slot], slope_all.at[pl.ds(block * rows, rows), lanes_of], local_sem.at[15 + slot]
            )
            copy.start()
            stored.append(copy)
        if part == 0:
            spread.forward(3)
    keep(gated_v, gated_all)
    spread.arrived(6)
    spread.arrived(5)
    spread.finish()
    for copy in small_copies:
        copy.wait_send()
    for copy in locals_[5:] + stored[-2:]:
        copy.wait()


def forward_call(heads, count, prefix, tokens, cotangent, small, qkv_shard, out_shard, up_shard, down_shard):
    rows, features = tokens.shape
    length = rows * 4
    depth, triple = qkv_shard.shape
    width = out_shard.shape[0]
    hidden = up_shard.shape[1]
    outer, inner = split_of(count)
    shape = jax.ShapeDtypeStruct
    hbm = pl.BlockSpec(memory_space=pl.ANY)
    vmem = pl.BlockSpec(memory_space=pltpu.VMEM)
    dma = pltpu.SemaphoreType.DMA
    pieces = 7
    return pl.pallas_call(
        functools.partial(forward_kernel, heads, count),
        out_shape=[
            shape((features, triple), BF16),
            shape((width, features), BF16),
            shape((features, hidden), BF16),
            shape((hidden, features), BF16),
            shape((length, features), BF16),
            shape((length, features), BF16),
            shape((length, triple), BF16),
            shape((length, width), BF16),
            shape((heads, length, 128), F32),
            shape((rows, features), F32),
            shape((length, features), BF16),
            shape((length, hidden), BF16),
            shape((length, hidden), F32),
            shape((8, features), F32),
        ],
        in_specs=[pl.BlockSpec(memory_space=pltpu.SMEM)] + [vmem] * 7,
        out_specs=[hbm] * 9 + [vmem] + [hbm] * 3 + [vmem],
        scratch_shapes=[
            pltpu.VMEM((count, 40, 128), F32),
            pltpu.VMEM((length, features), BF16),
            pltpu.VMEM((features, triple), BF16),
            pltpu.VMEM((length, triple), BF16),
            pltpu.VMEM((length, width), BF16),
            pltpu.VMEM((heads, length, 128), F32),
            pltpu.VMEM((width, features), BF16),
            pltpu.VMEM((2, rows, features), BF16),
            pltpu.VMEM((2, rows, features), BF16),
            pltpu.VMEM((rows, features), BF16),
            pltpu.VMEM((rows, features), BF16),
            pltpu.VMEM((length, features), BF16),
            pltpu.VMEM((features, hidden), BF16),
            pltpu.VMEM((length, hidden), BF16),
            pltpu.VMEM((2, rows, hidden // 2), F32),
            dma((count,)),
            dma((count,)),
            dma((pieces + 1, outer)),
            dma((pieces + 1, outer)),
            dma((pieces, outer)),
            dma((pieces, outer)),
            dma((3, 3)),
            dma((3, 3)),
            dma((1, 3)),
            dma((1, 3)),
            dma((17,)),
        ],
        compiler_params=pltpu.CompilerParams(
            collective_id=0, has_side_effects=True, vmem_limit_bytes=VMEM_BYTES
        ),
    )(prefix, tokens, cotangent, small, qkv_shard, out_shard, up_shard, down_shard)
class Reduce:
    def __init__(self, spot, left, right, lanes, landing, target, shared, index, last):
        self.spot, self.left, self.right, self.lanes = spot, left, right, lanes
        self.landing, self.target, self.shared, self.index, self.last = landing, target, shared, index, last
        self.width = lanes.stop - lanes.start
        self.share = target.shape[0]
        self.stepped = {}
        self.held = ()
        row = spot.row
        self.inner = (row == 1) | (row == 2)
        self.steps = (
            jnp.where(row == 0, 3, 1), jnp.where(self.inner, 3, 2), jnp.where(row == 0, 1, jnp.where(row == 3, 3, 2)), 0
        )

    def block(self, owner, take):
        turned = jnp.transpose(self.left[:, block_of(owner, self.share)])
        for start in range(0, self.width, 512):
            source = self.right[:, self.lanes.start + start : self.lanes.start + start + 512]
            take(slice(start, start + 512), jnp.dot(turned, source, preferred_element_type=F32))

    def y_copy(self, step):
        shared = self.shared
        area = pl.ds(0, self.width)
        return remote(
            shared["y_out"].at[step, :, area], shared["y_in"].at[step, :, area], shared["y_send"].at[step],
            shared["y_recv"].at[step], self.spot.beside(1), self.spot.tensor,
        )

    def z_copy(self, place):
        shared, step = self.shared, self.steps[place]
        return remote(
            shared["z_out"].at[place, :, pl.ds(0, self.width)], self.landing.at[step - 1],
            shared["z_send"].at[place], shared["z_recv"].at[self.index, step], self.spot.across(step),
            self.spot.tensor,
        )

    def near_copy(self):
        shared, spot = self.shared, self.spot
        area = pl.ds(0, self.width)
        return remote(
            shared["z_out"].at[0, :, area], shared["near"].at[:, area], shared["z_send"].at[0], shared["near_recv"].at[0],
            jnp.where(spot.row == 0, 1, 2) * spot.inner + spot.column, spot.tensor,
        )

    def produce(self, place):
        shared, spot = self.shared, self.spot
        row = lax.rem(spot.row + self.steps[place], spot.outer)
        if place in shared["y_busy"]:
            shared["y_busy"].pop(place).wait_send()

        def take(where, value):
            shared["y_out"][place, :, where] = value.astype(BF16)

        self.block(spot.beside(1, row), take)
        if self.index > 0:
            pl.semaphore_wait(shared["credit"], 1)
        copy = self.y_copy(place)
        copy.start()
        shared["y_busy"][place] = copy

    def hold(self, places):
        self.held = places
        for place in places:

            def take(where, value, place=place):
                self.shared["z_out"][place, :, where] = value.astype(BF16)

            self.block(self.spot.across(self.steps[place]), take)

    def serve(self, place):
        shared, spot = self.shared, self.spot
        self.y_copy(place).wait_recv()
        if place in shared["z_busy"]:
            shared["z_busy"].pop(place).wait_send()
        y_in, z_out = shared["y_in"], shared["z_out"]
        if place in self.held:
            for start in range(0, self.width, 512):
                where = slice(start, start + 512)
                z_out[place, :, where] = (
                    z_out[place, :, where].astype(F32) + y_in[place, :, where].astype(F32)
                ).astype(BF16)
        else:

            def take(where, value):
                z_out[place, :, where] = (value + y_in[place, :, where].astype(F32)).astype(BF16)

            self.block(spot.across(self.steps[place]), take)
        if not self.last:
            pl.semaphore_signal(
                shared["credit"], inc=1, device_id=(spot.beside(1), spot.tensor), device_id_type=MESH
            )
        if place == 3:
            return
        if place == 0:

            @pl.when(jnp.logical_not(self.inner))
            def _():
                if self.index > 0:
                    pl.semaphore_wait(shared["near_free"], 1)
                self.near_copy().start()

            @pl.when(self.inner)
            def _():
                self.z_copy(0).start()

        else:
            if place == 2:

                @pl.when(self.inner)
                def _():
                    self.near_copy().wait_recv()
                    for start in range(0, self.width, 512):
                        where = slice(start, start + 512)
                        z_out[2, :, where] = (
                            z_out[2, :, where].astype(F32) + shared["near"][:, where].astype(F32)
                        ).astype(BF16)
                    if not self.last:
                        pl.semaphore_signal(
                            shared["near_free"], inc=1,
                            device_id=(jnp.where(spot.row == 1, 0, 3) * spot.inner + spot.column, spot.tensor),
                            device_id_type=MESH,
                        )

            self.z_copy(place).start()
        shared["z_busy"][place] = self.z_copy(place)

    def landed(self, step):
        shared = self.shared
        remote(
            shared["z_out"].at[0, :, pl.ds(0, self.width)], self.landing.at[step - 1], shared["z_send"].at[0],
            shared["z_recv"].at[self.index, step], self.spot.across(1), self.spot.tensor,
        ).wait_recv()

    def settle(self):
        shared, spot = self.shared, self.spot
        pl.when(spot.row != 0)(lambda: self.landed(1))
        self.landed(2)
        pl.when(spot.row != 3)(lambda: self.landed(3))
        loads, stores = [], []
        chunks = self.width // 128
        for chunk in range(chunks):
            slot = chunk % 4
            loads.append(pltpu.make_async_copy(
                self.landing.at[:, :, pl.ds(chunk * 128, 128)], shared["z_stage"].at[slot], shared["stage_sem"].at[slot]
            ))
            stores.append(pltpu.make_async_copy(
                shared["o_stage"].at[slot], self.target.at[:, pl.ds(chunk * 128, 128)], shared["stage_sem"].at[4 + slot]
            ))
        for load in loads[:3]:
            load.start()
        for chunk in range(chunks):
            loads[chunk].wait()
            if chunk + 3 < chunks:
                loads[chunk + 3].start()
            if chunk >= 4:
                stores[chunk - 4].wait()
            total = shared["z_out"][3, :, chunk * 128 : (chunk + 1) * 128].astype(F32)
            for step in range(spot.outer - 1):
                part = shared["z_stage"][chunk % 4, step].astype(F32)
                if step != 1:
                    part = jnp.where(spot.row == (0 if step == 0 else 3), 0.0, part)
                total = total + part
            shared["o_stage"][chunk % 4] = total
            stores[chunk].start()
        for store in stores[-4:]:
            store.wait()


def row_dot(left, right):
    return lax.dot_general(left, right, (((1,), (1,)), ((), ())), preferred_element_type=F32)


def backward_kernel(
    heads,
    count,
    prefix,
    sums,
    tokens,
    cotangent,
    wqkv,
    wo,
    w1,
    w2,
    h1_all,
    d_rows,
    qkv_all,
    mixed_all,
    lse_v,
    second,
    h2_all,
    gated_all,
    slope_all,
    layer_out,
    input_grad,
    grad_down,
    grad_up,
    grad_out,
    grad_qkv,
    vector_sums,
    bias_sums,
    land_down,
    land_up,
    land_out,
    land_qkv,
    weight_v,
    buf1,
    buf2,
    buf3,
    buf4,
    buf5,
    buf6,
    near,
    core_send,
    core_recv,
    x_send,
    x_recv,
    y_in,
    y_out,
    z_out,
    z_stage,
    o_stage,
    spare,
    line,
    dk_sum,
    dv_sum,
    vectors,
    biases,
    vector_in,
    bias_in,
    part_sum,
    part_in,
    y_send,
    y_recv,
    z_send,
    z_recv,
    g_send,
    g_recv,
    s_send,
    s_recv,
    v_send,
    v_recv,
    b_send,
    b_recv,
    t_send,
    t_recv,
    stage_sem,
    load_sem,
    near_recv,
    credit,
    ready,
    near_free,
):
    spot = Spot(count)
    rows, features = line.shape
    length = buf1.shape[0]
    width = wo.shape[0]
    hidden = w1.shape[1]
    triple = 3 * width
    size = width // heads
    scale = size ** -0.5
    tail = slice(triple, triple + width)
    shared = {
        "y_in": y_in, "y_out": y_out, "z_out": z_out, "z_stage": z_stage, "o_stage": o_stage, "y_send": y_send,
        "y_recv": y_recv, "z_send": z_send, "z_recv": z_recv, "credit": credit, "stage_sem": stage_sem,
        "y_busy": {}, "z_busy": {}, "near": near, "near_recv": near_recv, "near_free": near_free,
    }
    down = Reduce(spot, buf1, buf2, slice(0, hidden), land_down, grad_down, shared, 0, False)
    up = Reduce(spot, buf4, buf3, slice(0, hidden), land_up, grad_up, shared, 1, False)
    qkv = Reduce(spot, buf6, buf5, slice(0, triple), land_qkv, grad_qkv, shared, 2, False)
    out = Reduce(spot, buf1, buf2, tail, land_out, grad_out, shared, 3, True)

    def fetch(source, target, slot):
        copy = pltpu.make_async_copy(source, target, load_sem.at[slot])
        copy.start()
        return copy

    load_a = fetch(d_rows, buf1, 0)
    load_b = fetch(gated_all, buf2, 1)
    load_w = fetch(w2, weight_v, 2)
    slopes = [fetch(slope_all.at[pl.ds(part * rows, rows)], (spare, input_grad)[part % 2], 3 + part % 2) for part in range(2)]
    load_h = fetch(h2_all, buf4, 5)
    load_c = fetch(cotangent, line, 6)
    spot.meet(True)
    vectors[...] = jnp.zeros_like(vectors)
    biases[...] = jnp.zeros_like(biases)
    load_a.wait()
    load_b.wait()
    for place in range(spot.outer):
        down.produce(place)
    load_w.wait()
    tensor = (core_send, core_recv, x_send, x_recv)

    def down_part(rank, index):
        return jnp.dot(buf2[block_of(rank, rows), :], weight_v[:, block_of(index, 512)], preferred_element_type=F32)

    def take_out(index, total):
        where = block_of(index, 512)
        buf6[0:rows, where] = (spare[:, where] + total + sums[5:6, where]).astype(BF16)

    end = tensor_sum(
        spot, down_part, *tensor, s_send, s_recv, take_out, between=lambda: down.serve(0)
    )
    for part in range(length // rows):
        held = (spare, input_grad)[part % 2]
        slopes[part].wait()

        def lower(index, carry, part=part, held=held):
            where = block_of(index, 512)
            span = slice(part * rows, (part + 1) * rows)
            du = row_dot(buf1[span, :], weight_v[where, :]) * held[:, where]
            biases[pl.ds(index, 1), :] += jnp.sum(du, axis=0, keepdims=True)
            buf3[span, where] = du.astype(BF16)
            return carry

        lax.fori_loop(0, hidden // 512, lower, 0)
        if part + 2 < length // rows:
            slopes.append(fetch(slope_all.at[pl.ds((part + 2) * rows, rows)], held, 3 + part % 2))
        if part == 1:
            down.serve(1)
    load_s = fetch(second, spare, 3)
    load_s.wait()
    end()
    spot.release(ready)
    store_l = fetch(buf6.at[pl.ds(0, rows)], layer_out, 7)
    load_w = fetch(w1, weight_v, 2)
    load_h.wait()
    down.serve(2)
    down.hold((3,))
    load_q = fetch(qkv_all, buf2.at[:, pl.ds(0, triple)], 0)
    load_m = fetch(mixed_all, buf2.at[:, pl.ds(triple, width)], 1)
    up.produce(0)
    up.produce(1)
    up.produce(2)
    load_w.wait()

    def h2_part(rank, index):
        return row_dot(buf3[block_of(rank, rows), :], weight_v[block_of(index, 512), :])

    def take_h2(index, total):
        input_grad[:, block_of(index, 512)] = total

    pl.semaphore_wait(ready, 2)
    end = tensor_sum(spot, h2_part, *tensor, s_send, s_recv, take_h2)
    down.serve(3)
    up.produce(3)
    up.serve(0)
    end()
    spot.release(ready)
    store_l.wait()
    load_n = fetch(h1_all, buf6, 7)
    load_o = fetch(wo, weight_v.at[pl.ds(0, width)], 2)
    load_c.wait()
    strip = 32
    base = spot.tensor * rows

    def norm_back(rows_of, gain, grads, keep, first):
        center, inverse = normal_parts(rows_of)
        normal = center * inverse
        vectors[first : first + 1, :] += jnp.sum(grads * normal, axis=0, keepdims=True)
        vectors[first + 1 : first + 2, :] += jnp.sum(grads, axis=0, keepdims=True)
        scaled = grads * gain
        mean = jnp.mean(scaled, axis=-1, keepdims=True)
        slope = jnp.mean(scaled * normal, axis=-1, keepdims=True)
        return keep + inverse * (scaled - mean - normal * slope)

    def back2(index, carry):
        where = block_of(index, strip)
        dy = line[where, :].astype(F32)
        dx = norm_back(spare[where, :], sums[2:3, :], input_grad[where, :], dy, 2)
        vectors[4:5, :] += jnp.sum(dx, axis=0, keepdims=True)
        vectors[5:6, :] += jnp.sum(dy, axis=0, keepdims=True)
        input_grad[where, :] = dx
        buf1[pl.ds(pl.multiple_of(base + index * strip, strip), strip), :] = dx.astype(BF16)
        return carry

    lax.fori_loop(0, rows // strip, back2, 0)
    gather = TensorGather(spot, buf1.at[block_of(spot.tensor, rows)], buf1, rows, g_send, g_recv)
    load_t = fetch(tokens, line, 6)
    up.serve(1)
    down.settle()
    gather.pass_on()
    load_o.wait()
    gather.finish()
    load_q.wait()
    load_m.wait()

    def mix_back(index, carry):
        where = block_of(index, rows)
        buf5[where, tail] = row_dot(buf1[where, :], weight_v[0:width, :]).astype(BF16)
        return carry

    lax.fori_loop(0, length // rows, mix_back, 0)
    load_w = fetch(wqkv, weight_v.at[:, pl.ds(0, triple)], 2)
    limit = prefix[0]
    bench = 256

    def attend(head, carry):
        q_at = block_of(head, size)
        k_at = pl.ds(pl.multiple_of(width + head * size, size), size)
        v_at = pl.ds(pl.multiple_of(2 * width + head * size, size), size)
        o_at = pl.ds(pl.multiple_of(triple + head * size, size), size)
        dk_sum[...] = jnp.zeros_like(dk_sum)
        dv_sum[...] = jnp.zeros_like(dv_sum)
        for block in range(length // bench):
            reach = min(length, max((block + 1) * bench, PREFIX_TOP))
            span = slice(block * bench, (block + 1) * bench)
            row_of = block * bench + lax.broadcasted_iota(jnp.int32, (bench, reach), 0)
            place = lax.broadcasted_iota(jnp.int32, (bench, reach), 1)
            seen = (place <= row_of) | (place < limit)
            q = buf2[span, q_at]
            k = buf2[0:reach, k_at]
            v = buf2[0:reach, v_at]
            do = buf5[span, o_at]
            scores = jnp.where(seen, row_dot(q, k), -1e30)
            probs = jnp.exp(scores - lse_v[head, span, 0:1])
            d_probs = row_dot(do, v)
            inner = jnp.sum(probs * d_probs, axis=-1, keepdims=True)
            d_scores = (probs * (d_probs - inner)).astype(BF16)
            flip = (((0,), (0,)), ((), ()))
            dv_sum[0:reach, :] += lax.dot_general(probs.astype(BF16), do, flip, preferred_element_type=F32)
            dk_sum[0:reach, :] += lax.dot_general(d_scores, q, flip, preferred_element_type=F32)
            dq = jnp.dot(d_scores, k, preferred_element_type=F32) * scale
            biases[4:5, q_at] += jnp.sum(dq, axis=0, keepdims=True)
            buf5[span, q_at] = dq.astype(BF16)
        buf5[:, k_at] = dk_sum[...].astype(BF16)
        buf5[:, v_at] = dv_sum[...].astype(BF16)
        biases[5:6, q_at] += jnp.sum(dv_sum[...], axis=0, keepdims=True)
        return carry

    lax.fori_loop(0, heads, attend, 0)
    load_n.wait()
    qkv.produce(0)
    qkv.produce(1)
    up.serve(2)
    qkv.produce(2)
    load_w.wait()

    def h1_part(rank, index):
        return row_dot(buf5[block_of(rank, rows), 0:triple], weight_v[block_of(index, 512), 0:triple])

    def take_h1(index, total):
        spare[:, block_of(index, 512)] = total

    pl.semaphore_wait(ready, 2)
    end = tensor_sum(spot, h1_part, *tensor, s_send, s_recv, take_h1)
    up.serve(3)
    qkv.produce(3)
    qkv.serve(0)
    out.produce(0)
    end()
    load_t.wait()

    def back1(index, carry):
        where = block_of(index, strip)
        dx = norm_back(line[where, :].astype(F32), sums[0:1, :], spare[where, :], input_grad[where, :], 0)
        input_grad[where, :] = dx
        return carry

    lax.fori_loop(0, rows // strip, back1, 0)
    share = grad_up.shape[0]
    vector_copies, bias_copies = [], []
    for step in range(1, count):
        peer = lax.rem(spot.dp + step, count)
        vector_copies.append(remote(
            vectors.at[:, block_of(peer, share)], vector_in.at[spot.dp], v_send.at[step], v_recv.at[step], peer,
            spot.tensor,
        ))
        bias_copies.append(remote(biases, bias_in.at[spot.dp], b_send.at[step], b_recv.at[step], peer, spot.tensor))
    for copy in vector_copies + bias_copies:
        copy.start()
    vector_in[spot.dp] = vectors[:, block_of(spot.dp, share)]
    bias_in[spot.dp] = biases[...]
    up.settle()
    qkv.serve(1)
    out.produce(1)
    for copy in vector_copies + bias_copies:
        copy.wait_recv()
    total, bias_total = vector_in[0], bias_in[0]
    for index in range(1, count):
        total = total + vector_in[index]
        bias_total = bias_total + bias_in[index]
    part_sum[...] = total
    bias_sums[...] = bias_total
    part_copies = [
        remote(part_sum, part_in.at[spot.tensor], t_send.at[slot], t_recv.at[slot], spot.dp, peer)
        for slot, peer in enumerate((spot.x_peer, spot.core_peer, spot.far_peer))
    ]
    for copy in part_copies:
        copy.start()
    part_in[spot.tensor] = part_sum[...]
    qkv.serve(2)
    out.produce(2)
    for copy in part_copies:
        copy.wait_recv()
    vector_sums[...] = part_in[0] + part_in[1] + part_in[2] + part_in[3]
    qkv.serve(3)
    out.produce(3)
    out.serve(0)
    out.serve(1)
    out.serve(2)
    for copy in vector_copies + bias_copies + part_copies:
        copy.wait_send()
    qkv.settle()
    out.serve(3)
    out.settle()
    for copy in list(shared["y_busy"].values()) + list(shared["z_busy"].values()):
        copy.wait_send()


def backward_call(heads, count, prefix, sums, tokens, cotangent, weights, saved):
    rows, features = tokens.shape
    length = rows * 4
    share = features // count
    wqkv, wo, w1, w2 = weights
    width, hidden, triple = wo.shape[0], w1.shape[1], wqkv.shape[1]
    outer, inner = split_of(count)
    shape = jax.ShapeDtypeStruct
    hbm = pl.BlockSpec(memory_space=pl.ANY)
    vmem = pl.BlockSpec(memory_space=pltpu.VMEM)
    dma = pltpu.SemaphoreType.DMA
    regular = pltpu.SemaphoreType.REGULAR
    wide = (length, features)
    return pl.pallas_call(
        functools.partial(backward_kernel, heads, count),
        out_shape=[
            shape((rows, features), BF16),
            shape((rows, features), F32),
            shape((share, hidden), F32),
            shape((share, hidden), F32),
            shape((share, width), F32),
            shape((share, triple), F32),
            shape((8, share), F32),
            shape((8, 512), F32),
            shape((outer - 1, share, hidden), BF16),
            shape((outer - 1, share, hidden), BF16),
            shape((outer - 1, share, width), BF16),
            shape((outer - 1, share, triple), BF16),
        ],
        in_specs=[pl.BlockSpec(memory_space=pltpu.SMEM), vmem] + [hbm] * 10 + [vmem] + [hbm] * 4,
        out_specs=[hbm, vmem] + [hbm] * 4 + [vmem] * 2 + [hbm] * 4,
        scratch_shapes=[
            pltpu.VMEM((hidden, features), BF16),
            pltpu.VMEM(wide, BF16),
            pltpu.VMEM(wide, BF16),
            pltpu.VMEM(wide, BF16),
            pltpu.VMEM(wide, BF16),
            pltpu.VMEM(wide, BF16),
            pltpu.VMEM(wide, BF16),
            pltpu.VMEM((share, hidden), BF16),
            pltpu.VMEM((2, rows, features), BF16),
            pltpu.VMEM((2, rows, features), BF16),
            pltpu.VMEM((rows, features), BF16),
            pltpu.VMEM((rows, features), BF16),
            pltpu.VMEM((outer, share, hidden), BF16),
            pltpu.VMEM((outer, share, hidden), BF16),
            pltpu.VMEM((outer, share, hidden), BF16),
            pltpu.VMEM((4, outer - 1, share, 128), BF16),
            pltpu.VMEM((4, share, 128), F32),
            pltpu.VMEM((rows, features), F32),
            pltpu.VMEM((rows, features), BF16),
            pltpu.VMEM((length, width // heads), F32),
            pltpu.VMEM((length, width // heads), F32),
            pltpu.VMEM((8, features), F32),
            pltpu.VMEM((8, 512), F32),
            pltpu.VMEM((count, 8, share), F32),
            pltpu.VMEM((count, 8, 512), F32),
            pltpu.VMEM((8, share), F32),
            pltpu.VMEM((4, 8, share), F32),
            dma((outer,)),
            dma((outer,)),
            dma((outer,)),
            dma((4, outer)),
            dma((3,)),
            dma((3,)),
            dma((3,)),
            dma((3,)),
            dma((count,)),
            dma((count,)),
            dma((count,)),
            dma((count,)),
            dma((3,)),
            dma((3,)),
            dma((8,)),
            dma((8,)),
            dma((1,)),
            regular,
            regular,
            regular,
        ],
        compiler_params=pltpu.CompilerParams(
            collective_id=1, has_side_effects=True, vmem_limit_bytes=VMEM_BYTES
        ),
    )(prefix, sums, tokens, cotangent, wqkv, wo, w1, w2, *saved)


def pack_small(biases, vectors):
    devices = lax.axis_size("dp")
    parts = jnp.concatenate(biases, axis=0)
    lane = lax.broadcasted_iota(jnp.int32, (parts.shape[0], parts.shape[1] * devices), 1)
    wide = jnp.where(lane // parts.shape[1] == lax.axis_index("dp"), jnp.tile(parts, (1, devices)), 0)
    halves = jnp.pad(jnp.stack(vectors), ((0, 2), (0, 0)))
    return jnp.concatenate([wide, halves[:, :128], halves[:, 128:]], axis=0).astype(F32)


def layer_norm(rows, gain, shift):
    center = rows - jnp.mean(rows, axis=-1, keepdims=True)
    spread = jnp.mean(center * center, axis=-1, keepdims=True)
    return center * lax.rsqrt(spread + 1e-05) * gain + shift


def gelu_exact(values):
    return jax.nn.gelu(values, approximate=False)


def head_major(matrix, heads):
    return matrix.reshape(matrix.shape[0], heads, -1).transpose(1, 0, 2)


def row_major(stacked):
    return stacked.transpose(1, 0, 2).reshape(stacked.shape[1], -1)


def masked_scores(q_block, keys, start, prefix_len):
    scores = jnp.einsum("hqd,hkd->hqk", q_block, keys, preferred_element_type=jnp.float32)
    rows = start + lax.broadcasted_iota(jnp.int32, scores.shape[1:], 0)
    cols = lax.broadcasted_iota(jnp.int32, scores.shape[1:], 1)
    seen = (cols <= rows) | (cols < prefix_len)
    return jnp.where(seen[None], scores, -1e30)


def to_blocks(stacked, count):
    heads, length = (stacked.shape[0], stacked.shape[1])
    return stacked.reshape((heads, count, length // count) + stacked.shape[2:]).swapaxes(0, 1)


def from_blocks(blocked):
    count, heads, block = (blocked.shape[0], blocked.shape[1], blocked.shape[2])
    return blocked.swapaxes(0, 1).reshape((heads, count * block) + blocked.shape[3:])


def contract_rows(left, right):
    return jnp.einsum("ld,le->de", left, right, preferred_element_type=jnp.float32)


def times_transpose(left, right):
    return jnp.einsum("le,de->ld", left, right, preferred_element_type=jnp.float32)


def plain(
    tokens,
    prefix,
    query_weight,
    key_weight,
    value_weight,
    out_weight,
    query_bias,
    value_bias,
    up_weight,
    down_weight,
    up_bias,
    norm1_gain,
    norm1_bias,
    norm2_gain,
    norm2_bias,
    out_bias,
    down_bias,
    cotangent,
):
    f32 = jnp.float32
    bf16 = jnp.bfloat16
    devices = lax.axis_size("dp")
    small = (query_bias, value_bias, up_bias, norm1_gain, norm1_bias, norm2_gain, norm2_bias, out_bias, down_bias)
    packed = jnp.concatenate([part.reshape(-1) for part in small])
    packed = lax.all_gather(packed, "dp", axis=0, tiled=False)
    pieces = []
    offset = 0
    for part in small:
        piece = packed[:, offset : offset + part.size].reshape((devices,) + part.shape)
        offset += part.size
        pieces.append(jnp.moveaxis(piece, 0, -2).reshape(part.shape[:-1] + (-1,)))
    bq, bv, b1, g1, n1, g2, n2, bo, b2 = pieces
    wq, wk, wv, wo = (
        lax.all_gather(query_weight, "dp", axis=0, tiled=True),
        lax.all_gather(key_weight, "dp", axis=0, tiled=True),
        lax.all_gather(value_weight, "dp", axis=0, tiled=True),
        lax.all_gather(out_weight, "dp", axis=1, tiled=True),
    )
    w1, w2 = (
        lax.all_gather(up_weight, "dp", axis=0, tiled=True),
        lax.all_gather(down_weight, "dp", axis=1, tiled=True),
    )
    g1f, n1f, g2f, n2f = (g1.astype(f32), n1.astype(f32), g2.astype(f32), n2.astype(f32))
    bof, b2f = (bo.astype(f32), b2.astype(f32))
    heads = bq.shape[0]
    head_size = bq.shape[1]
    scale = head_size ** (-0.5)
    prefix_len = prefix[0]
    xf = tokens.astype(f32)
    h1 = layer_norm(xf, g1f, n1f).astype(bf16)
    rows1 = lax.all_gather(h1, "tensor", axis=0, tiled=True)
    length = rows1.shape[0]
    block = min(512, length)
    count = length // block
    query = (
        (jnp.dot(rows1, wq, preferred_element_type=f32) + bq.astype(f32).reshape(-1)) * scale
    ).astype(bf16)
    keyed = jnp.dot(rows1, wk, preferred_element_type=f32).astype(bf16)
    valued = (jnp.dot(rows1, wv, preferred_element_type=f32) + bv.astype(f32).reshape(-1)).astype(
        bf16
    )
    q_heads = head_major(query, heads)
    k_heads = head_major(keyed, heads)
    v_heads = head_major(valued, heads)
    q_blocks = to_blocks(q_heads, count)
    starts = jnp.arange(count, dtype=jnp.int32) * block

    def forward_block(item):
        q_block, start = item
        scores = masked_scores(q_block, k_heads, start, prefix_len)
        top = jnp.max(scores, axis=-1, keepdims=True)
        expd = jnp.exp(scores - top)
        total = jnp.sum(expd, axis=-1, keepdims=True)
        probs = (expd / total).astype(bf16)
        outv = jnp.einsum("hqk,hkd->hqd", probs, v_heads, preferred_element_type=f32)
        return (outv.astype(bf16), (top + jnp.log(total))[..., 0])

    o_blocks, lse_blocks = lax.map(forward_block, (q_blocks, starts))
    mixed = row_major(from_blocks(o_blocks))
    attn_part = jnp.dot(mixed, wo, preferred_element_type=f32)
    attn_total = lax.psum_scatter(attn_part.astype(bf16), "tensor", scatter_dimension=0, tiled=True).astype(f32)
    second = xf + attn_total + bof
    h2 = layer_norm(second, g2f, n2f).astype(bf16)
    rows2 = lax.all_gather(h2, "tensor", axis=0, tiled=True)
    hidden = jnp.dot(rows2, w1, preferred_element_type=f32) + b1.astype(f32).reshape(-1)
    gated = gelu_exact(hidden).astype(bf16)
    mlp_part = jnp.dot(gated, w2, preferred_element_type=f32)
    mlp_total = lax.psum_scatter(
        mlp_part.astype(jnp.bfloat16), "tensor", scatter_dimension=0, tiled=True
    ).astype(jnp.float32)
    layer_out = (second + mlp_total + b2f).astype(bf16)
    d_out = cotangent.astype(f32)
    g_b2 = jnp.sum(d_out, axis=0)
    d_rows = lax.all_gather(cotangent, "tensor", axis=0, tiled=True)
    d_gated = times_transpose(d_rows, w2)
    d_hidden = jax.vjp(gelu_exact, hidden)[1](d_gated)[0]
    g_b1 = jnp.sum(d_hidden, axis=0).reshape(b1.shape)
    d_hidden_low = d_hidden.astype(bf16)
    d_h2_part = times_transpose(d_hidden_low, w1)
    g_w2 = contract_rows(gated, d_rows)
    g_w1 = contract_rows(rows2, d_hidden_low)
    d_h2 = lax.psum_scatter(d_h2_part.astype(bf16), "tensor", scatter_dimension=0, tiled=True).astype(f32)
    norm2_back = jax.vjp(layer_norm, second, g2f, n2f)[1]
    d_second_ln, g_g2, g_n2 = norm2_back(d_h2)
    d_second = d_out + d_second_ln
    g_bo = jnp.sum(d_second, axis=0)
    d_second_low = d_second.astype(bf16)
    back_rows = lax.all_gather(d_second_low, "tensor", axis=0, tiled=True)
    g_wo = contract_rows(mixed, back_rows)
    d_mixed = times_transpose(back_rows, wo).astype(bf16)
    do_blocks = to_blocks(head_major(d_mixed, heads), count)

    def backward_block(carry, item):
        d_keys, d_vals = carry
        q_block, do_block, lse_block, start = item
        scores = masked_scores(q_block, k_heads, start, prefix_len)
        probs = jnp.exp(scores - lse_block[..., None])
        d_probs = jnp.einsum("hqd,hkd->hqk", do_block, v_heads, preferred_element_type=f32)
        d_vals = d_vals + jnp.einsum(
            "hqk,hqd->hkd", probs.astype(bf16), do_block, preferred_element_type=f32
        )
        inner = jnp.sum(probs * d_probs, axis=-1, keepdims=True)
        d_scores = (probs * (d_probs - inner)).astype(bf16)
        d_query = jnp.einsum("hqk,hkd->hqd", d_scores, k_heads, preferred_element_type=f32)
        d_keys = d_keys + jnp.einsum("hqk,hqd->hkd", d_scores, q_block, preferred_element_type=f32)
        return ((d_keys, d_vals), d_query)

    empty = jnp.zeros(k_heads.shape, f32)
    (d_keys, d_vals), dq_blocks = lax.scan(
        backward_block, (empty, empty), (q_blocks, do_blocks, lse_blocks, starts)
    )
    d_query = row_major(from_blocks(dq_blocks)) * scale
    d_keys = row_major(d_keys)
    d_vals = row_major(d_vals)
    g_bq = jnp.sum(d_query, axis=0).reshape(bq.shape)
    g_bv = jnp.sum(d_vals, axis=0).reshape(bv.shape)
    dq_low, dk_low, dv_low = (d_query.astype(bf16), d_keys.astype(bf16), d_vals.astype(bf16))
    g_wq = contract_rows(rows1, dq_low)
    g_wk = contract_rows(rows1, dk_low)
    g_wv = contract_rows(rows1, dv_low)
    d_h1_part = (
        times_transpose(dq_low, wq) + times_transpose(dk_low, wk) + times_transpose(dv_low, wv)
    )
    d_h1 = lax.psum_scatter(d_h1_part.astype(bf16), "tensor", scatter_dimension=0, tiled=True).astype(f32)
    norm1_back = jax.vjp(layer_norm, xf, g1f, n1f)[1]
    d_input_ln, g_g1, g_n1 = norm1_back(d_h1)
    input_grad = d_second + d_input_ln
    def scatter(part, dim):
        return lax.psum_scatter(part.astype(bf16), "dp", scatter_dimension=dim, tiled=True).astype(f32)

    s_w2, s_w1, s_wo = scatter(g_w2, 1), scatter(g_w1, 0), scatter(g_wo, 1)
    s_wq, s_wk, s_wv = scatter(g_wq, 0), scatter(g_wk, 0), scatter(g_wv, 0)

    def by_device(part):
        return jnp.moveaxis(part.reshape(part.shape[:-1] + (devices, -1)), -2, 0).reshape(devices, -1)

    rows = [by_device(part) for part in (g_bq, g_bv, g_b1, g_g1, g_n1, g_g2, g_n2, g_bo, g_b2)]
    total = lax.psum_scatter(jnp.concatenate(rows, axis=1), "dp", scatter_dimension=0, tiled=True)[0]
    offset = 0
    outs = []
    for part in (query_bias, value_bias, up_bias):
        outs.append(total[offset : offset + part.size].reshape(part.shape))
        offset += part.size
    s_bq, s_bv, s_b1 = outs
    vectors = lax.psum_scatter(
        total[offset:].reshape(6, lax.axis_size("tensor"), -1), "tensor", scatter_dimension=1, tiled=True
    ).reshape(6, -1)
    s_g1, s_n1, s_g2, s_n2, s_bo, s_b2 = (vectors[index] for index in range(6))
    return (
        layer_out,
        input_grad,
        s_wq,
        s_wk,
        s_wv,
        s_wo,
        s_bq,
        s_bv,
        s_w1,
        s_w2,
        s_b1,
        s_g1,
        s_n1,
        s_g2,
        s_n2,
        s_bo,
        s_b2,
    )


def fast(
    tokens,
    prefix,
    query_weight,
    key_weight,
    value_weight,
    out_weight,
    query_bias,
    value_bias,
    up_weight,
    down_weight,
    up_bias,
    norm1_gain,
    norm1_bias,
    norm2_gain,
    norm2_bias,
    out_bias,
    down_bias,
    cotangent,
):
    devices = lax.axis_size("dp")
    me = lax.axis_index("dp")
    heads = query_bias.shape[0]
    small = pack_small(
        (query_bias, value_bias, up_bias), (norm1_gain, norm1_bias, norm2_gain, norm2_bias, out_bias, down_bias)
    )
    results = forward_call(
        heads, devices, prefix, tokens, cotangent, small,
        jnp.concatenate([query_weight, key_weight, value_weight], axis=1), out_weight, up_weight, down_weight,
    )
    layer_out, input_grad, g_w2, g_w1, g_wo, g_qkv, vectors, biases, *_ = backward_call(
        heads, devices, prefix, results[-1], tokens, cotangent, results[:4], results[4:-1]
    )
    g_wq, g_wk, g_wv = jnp.split(g_qkv, 3, axis=1)
    vectors = vectors.reshape(8, lax.axis_size("tensor"), -1)
    vectors = lax.dynamic_index_in_dim(vectors, lax.axis_index("tensor"), axis=1, keepdims=False)

    def own(flat, part):
        whole = flat.reshape(part.shape[0], -1)
        return lax.dynamic_slice_in_dim(whole, me * part.shape[1], part.shape[1], axis=1)

    width = out_weight.shape[0]
    up_size = up_bias.size * devices
    g_b1 = own(biases[: up_size // 512].reshape(-1), up_bias)
    g_bq = own(biases[4, :width], query_bias)
    g_bv = own(biases[5, :width], value_bias)
    return (
        layer_out, input_grad, g_wq, g_wk, g_wv, g_wo.T, g_bq, g_bv, g_w1, g_w2.T, g_b1,
        vectors[0], vectors[1], vectors[2], vectors[3], vectors[4], vectors[5],
    )


def local(*args):
    tokens, query_weight, up_weight = args[0], args[2], args[8]
    devices = lax.axis_size("dp")
    features = tokens.shape[1]
    share = features // devices
    fits = (
        lax.axis_size("tensor") == 4
        and devices == 8
        and share % 128 == 0
        and tokens.shape[0] == 256
        and query_weight.shape[1] == 512
        and args[6].shape[0] == 4
        and features == 2048
        and up_weight.shape[1] == 2048
    )
    return fast(*args) if fits else plain(*args)


def solution(mesh):
    in_specs = (
        P(("dp", "tensor"), None),
        P("dp"),
        P("dp", "tensor"),
        P("dp", "tensor"),
        P("dp", "tensor"),
        P("tensor", "dp"),
        P("tensor", "dp"),
        P("tensor", "dp"),
        P("dp", "tensor"),
        P("tensor", "dp"),
        P("tensor", "dp"),
        P("dp"),
        P("dp"),
        P("dp"),
        P("dp"),
        P("dp"),
        P("dp"),
        P(("dp", "tensor"), None),
    )
    out_specs = (
        P(("dp", "tensor"), None),
        P(("dp", "tensor"), None),
        P("dp", "tensor"),
        P("dp", "tensor"),
        P("dp", "tensor"),
        P("tensor", "dp"),
        P("tensor", "dp"),
        P("tensor", "dp"),
        P("dp", "tensor"),
        P("tensor", "dp"),
        P("tensor", "dp"),
        P(("dp", "tensor")),
        P(("dp", "tensor")),
        P(("dp", "tensor")),
        P(("dp", "tensor")),
        P(("dp", "tensor")),
        P(("dp", "tensor")),
    )
    return jax.shard_map(local, mesh=mesh, in_specs=in_specs, out_specs=out_specs, check_vma=False)
```

```python
import functools

import jax
import jax.numpy as jnp
from jax import lax
from jax.experimental import pallas as pl
from jax.experimental.pallas import tpu as pltpu
from jax.sharding import PartitionSpec as P

MESH = pl.DeviceIdType.MESH
F32 = jnp.float32
BF16 = jnp.bfloat16
PREFIX_TOP = 512
VMEM_BYTES = 67043328


def split_of(count):
    inner = 1
    for size in range(1, count + 1):
        if size * size <= count and count % size == 0:
            inner = size
    return count // inner, inner


def remote(source, target, send_sem, recv_sem, dp, tensor):
    return pltpu.make_async_remote_copy(
        src_ref=source,
        dst_ref=target,
        send_sem=send_sem,
        recv_sem=recv_sem,
        device_id=(dp, tensor),
        device_id_type=MESH,
    )


def block_of(index, size):
    return pl.ds(pl.multiple_of(index * size, size), size)


class Spot:
    def __init__(self, count):
        self.outer, self.inner = split_of(count)
        self.count = count
        self.dp = lax.axis_index("dp")
        self.tensor = lax.axis_index("tensor")
        self.row = lax.div(self.dp, self.inner)
        self.column = lax.rem(self.dp, self.inner)
        self.core_peer = self.tensor + 1 - 2 * lax.rem(self.tensor, 2)
        self.x_peer = lax.rem(self.tensor + 2, 4)
        self.far_peer = lax.rem(self.core_peer + 2, 4)

    def across(self, step):
        return lax.rem(self.row + step, self.outer) * self.inner + self.column

    def beside(self, step, row=None):
        return (self.row if row is None else row) * self.inner + lax.rem(self.column + step, self.inner)

    def meet(self, far=False):
        barrier = pltpu.get_barrier_semaphore()
        for step in range(1, self.count):
            pl.semaphore_signal(
                barrier, inc=1, device_id=(lax.rem(self.dp + step, self.count), self.tensor), device_id_type=MESH
            )
        for peer in (self.core_peer, self.x_peer) + ((self.far_peer,) if far else ()):
            pl.semaphore_signal(barrier, inc=1, device_id=(self.dp, peer), device_id_type=MESH)
        pl.semaphore_wait(barrier, self.count + 1 + far)

    def release(self, ready):
        for peer in (self.core_peer, self.x_peer):
            pl.semaphore_signal(ready, inc=1, device_id=(self.dp, peer), device_id_type=MESH)


class Spread:
    AHEAD = 3

    def __init__(self, spot, pieces, late, own_at, sems):
        self.spot, self.pieces, self.late, self.sems = spot, pieces, late, sems
        self.flows = [(piece, 0) for piece in range(len(pieces)) if piece != late] + [(late, 0), (late, 1)]
        self.own_at = own_at
        self.order = (2, jnp.where(spot.row == 0, 3, 1), jnp.where(spot.row == 0, 1, 3))
        self.sent = []
        self.todo = [(flow, place) for flow in range(len(self.flows)) for place in range(3)]
        for piece in own_at[None]:
            self.send_own(piece)
        for flow in range(self.AHEAD):
            self.send_rows(flow)

    def owner(self, row, side):
        return row * 2 + lax.rem(self.spot.column + side, 2)

    def launch(self, condition, copy):
        if condition is None:
            copy().start()
        else:
            pl.when(condition)(lambda: copy().start())
        self.sent.append((condition, copy))

    def along(self, flow, step, source_row, target_row, send_slot):
        piece, side = self.flows[flow]
        source, target = self.pieces[piece]
        place = target(self.owner(source_row, side))
        if source_row is not self.spot.row or side:
            source = place
        return remote(
            source, place, self.sems[0].at[flow, send_slot], self.sems[1].at[flow, step],
            target_row * 2 + self.spot.column, self.spot.tensor,
        )

    def send_rows(self, flow):
        row = self.spot.row
        if self.flows[flow][1]:
            self.beside(self.late, 0, row).wait_recv()
        for step, condition in ((2, None), (1, row != 3), (3, row != 0)):
            self.launch(
                condition,
                functools.partial(self.along, flow, step, row, lax.rem(row + step, 4), step),
            )

    def hand_over(self, flow):
        row = self.spot.row
        self.launch(
            (row == 1) | (row == 2),
            lambda: self.along(flow, 2 * row - 1, lax.rem(row + 2, 4), (row - 1) * 3, 0),
        )

    def beside(self, piece, step, source_row):
        spot = self.spot
        source, target = self.pieces[piece]
        place = target(self.owner(source_row, 0))
        if source_row is not spot.row:
            source = place
        return remote(
            source, place, self.sems[2].at[piece, step], self.sems[3].at[piece, step], spot.beside(1), spot.tensor
        )

    def beside_arrival(self, piece, step, source_row):
        source, target = self.pieces[piece]
        return remote(
            source, target(self.owner(source_row, 1)), self.sems[2].at[piece, step], self.sems[3].at[piece, step],
            self.spot.beside(1), self.spot.tensor,
        )

    def send_own(self, piece):
        self.launch(None, functools.partial(self.beside, piece, 0, self.spot.row))

    def forward(self, count):
        for _ in range(count):
            if not self.todo:
                return
            flow, place = self.todo.pop(0)
            step = self.order[place]
            row = lax.rem(self.spot.row + 4 - step, 4)
            self.along(flow, step, row, self.spot.row, 0).wait_recv()
            if place == 0:
                self.hand_over(flow)
            piece = self.flows[flow][0]
            if piece != self.late:
                self.launch(None, functools.partial(self.beside, piece, step, row))
            if place == 2:
                if flow + self.AHEAD < len(self.flows):
                    self.send_rows(flow + self.AHEAD)
                for own in self.own_at.get(flow, ()):
                    self.send_own(own)

    def arrived(self, piece):
        while self.todo and self.flows[self.todo[0][0]][0] <= piece:
            self.forward(1)
        if piece != self.late:
            for step in range(4):
                self.beside_arrival(piece, step, lax.rem(self.spot.row + 4 - step, 4)).wait_recv()

    def finish(self):
        for condition, copy in self.sent:
            if condition is None:
                copy().wait_send()
            else:
                pl.when(condition)(lambda copy=copy: copy().wait_send())


class TensorGather:
    def __init__(self, spot, own, full, rows, send, recv):
        self.spot, self.full, self.rows, self.send, self.recv = spot, full, rows, send, recv
        place = self.at(spot.tensor)
        self.to_x = remote(own, place, send.at[0], recv.at[0], spot.dp, spot.x_peer)
        self.to_core = remote(own, place, send.at[1], recv.at[1], spot.dp, spot.core_peer)
        self.to_x.start()
        self.to_core.start()

    def at(self, index):
        return self.full.at[block_of(index, self.rows)]

    def pass_on(self):
        self.to_x.wait_recv()
        place = self.at(self.spot.x_peer)
        self.on = remote(place, place, self.send.at[2], self.recv.at[2], self.spot.dp, self.spot.core_peer)
        self.on.start()

    def finish(self):
        self.to_core.wait_recv()
        self.on.wait_recv()
        for copy in (self.to_x, self.to_core, self.on):
            copy.wait_send()


def tensor_sum(spot, product, core_send, core_recv, x_send, x_recv, send, recv, finish, between=None):
    width = core_send.shape[2]
    chunk = 512
    count = width // chunk

    def fill(rank, target):
        def body(index, carry):
            target[:, block_of(index, chunk)] = product(rank, index).astype(BF16)
            return carry

        lax.fori_loop(0, count, body, 0)

    copies = []
    for slot, rank in enumerate((spot.far_peer, spot.core_peer)):
        fill(rank, core_send.at[slot])
        copy = remote(core_send.at[slot], core_recv.at[slot], send.at[slot], recv.at[slot], spot.dp, spot.core_peer)
        copy.start()
        copies.append(copy)
    if between is not None:
        between()
    copies[0].wait_recv()

    def join(index, carry):
        where = block_of(index, chunk)
        x_send[:, where] = (product(spot.x_peer, index) + core_recv[0, :, where].astype(F32)).astype(BF16)
        return carry

    lax.fori_loop(0, count, join, 0)
    over = remote(x_send, x_recv, send.at[2], recv.at[2], spot.dp, spot.x_peer)
    over.start()
    copies[1].wait_recv()

    def end():
        over.wait_recv()

        def last(index, carry):
            where = block_of(index, chunk)
            total = product(spot.tensor, index) + core_recv[1, :, where].astype(F32) + x_recv[:, where].astype(F32)
            finish(index, total)
            return carry

        lax.fori_loop(0, count, last, 0)
        for copy in copies + [over]:
            copy.wait_send()

    return end


def normal_parts(rows):
    center = rows - jnp.mean(rows, axis=-1, keepdims=True)
    spread = jnp.mean(center * center, axis=-1, keepdims=True)
    return center, lax.rsqrt(spread + 1e-05)


def forward_kernel(
    heads,
    count,
    prefix,
    tokens,
    cotangent,
    small,
    qkv_shard,
    out_shard,
    up_shard,
    down_shard,
    wqkv,
    wo,
    w1,
    w2,
    h1_all,
    d_rows,
    qkv_all,
    mixed_all,
    lse_all,
    second,
    h2_all,
    gated_all,
    slope_all,
    sums,
    smalls,
    h1v,
    wqkv_v,
    qkv_v,
    mixed_v,
    lse_v,
    wo_v,
    core_send,
    core_recv,
    x_send,
    x_recv,
    h2v,
    w1_v,
    gated_v,
    slope_v,
    small_send,
    small_recv,
    z_send,
    z_recv,
    y_send,
    y_recv,
    g_send,
    g_recv,
    s_send,
    s_recv,
    local_sem,
):
    spot = Spot(count)
    rows, features = tokens.shape
    length = h1v.shape[0]
    depth = qkv_shard.shape[0]
    width = wo_v.shape[0]
    hidden = up_shard.shape[1]
    half = depth // 2
    tall = hidden // 2
    pieces = [
        (qkv_shard.at[pl.ds(part * half, half)],
         lambda owner, part=part: wqkv.at[block_of(owner * 2 + part, half)])
        for part in range(2)
    ]
    pieces.append((out_shard, lambda owner: wo.at[:, block_of(owner, depth)]))
    pieces += [
        (up_shard.at[:, pl.ds(part * tall, tall)],
         lambda owner, part=part: w1.at[block_of(owner, depth), pl.ds(part * tall, tall)])
        for part in range(2)
    ]
    pieces += [
        (down_shard.at[pl.ds(part * tall, tall)],
         lambda owner, part=part: w2.at[pl.ds(part * tall, tall), block_of(owner, depth)])
        for part in range(2)
    ]
    locals_ = []

    def keep(source, target):
        copy = pltpu.make_async_copy(source, target, local_sem.at[len(locals_)])
        copy.start()
        locals_.append(copy)

    spot.meet()
    small_copies = []
    for step in range(1, count):
        copy = remote(
            small, smalls.at[spot.dp], small_send.at[step], small_recv.at[step],
            lax.rem(spot.dp + step, count), spot.tensor,
        )
        copy.start()
        small_copies.append(copy)
    spread = Spread(
        spot, pieces, 6, {None: (0, 1, 2, 3), 0: (4,), 1: (6,), 2: (5,)}, (z_send, z_recv, y_send, y_recv)
    )
    for source, target in pieces:
        keep(source, target(spot.dp))
    smalls[spot.dp] = small[...]
    for step in range(1, count):
        owner = lax.rem(spot.dp + count - step, count)
        remote(
            small, smalls.at[owner], small_send.at[step], small_recv.at[step], spot.dp, spot.core_peer
        ).wait_recv()
    sums[...] = jnp.zeros_like(sums)
    joint = smalls[0, 0:24, :]
    for index in range(1, count):
        joint = joint + smalls[index, 0:24, :]
    lanes = 128
    for head in range(heads):
        sums[6:7, head * lanes : (head + 1) * lanes] = joint[head : head + 1, :]
        start = 2 * width + head * lanes
        sums[6:7, start : start + lanes] = joint[4 + head : 5 + head, :]
    for line in range(hidden // lanes):
        sums[7:8, line * lanes : (line + 1) * lanes] = joint[8 + line : 9 + line, :]
    for owner in range(count):
        for part in range(2):
            start = owner * depth + part * lanes
            sums[0:6, start : start + lanes] = smalls[owner, 24 + 8 * part : 30 + 8 * part, :]

    strip = 32
    base = spot.tensor * rows

    def norm1(index, carry):
        where = block_of(index, strip)
        center, scale = normal_parts(tokens[where, :].astype(F32))
        h1v[pl.ds(pl.multiple_of(base + index * strip, strip), strip), :] = (
            center * scale * sums[0:1, :] + sums[1:2, :]
        ).astype(BF16)
        return carry

    lax.fori_loop(0, rows // strip, norm1, 0)
    gather1 = TensorGather(spot, h1v.at[block_of(spot.tensor, rows)], h1v, rows, g_send.at[0], g_recv.at[0])
    gather_d = TensorGather(spot, cotangent, d_rows, rows, g_send.at[1], g_recv.at[1])
    keep(cotangent, d_rows.at[block_of(spot.tensor, rows)])
    spread.forward(1)
    gather1.pass_on()
    spread.forward(2)
    gather_d.pass_on()
    gather1.finish()
    keep(h1v, h1_all)
    spread.forward(6)
    spread.arrived(0)
    spread.arrived(1)
    for copy in locals_[:2]:
        copy.wait()
    load = pltpu.make_async_copy(wqkv, wqkv_v, local_sem.at[14])
    load.start()
    load.wait()

    def project(index, carry):
        where = block_of(index, rows)
        for part in range(3):
            lanes = slice(part * width, (part + 1) * width)
            value = jnp.dot(h1v[where, :], wqkv_v[:, lanes], preferred_element_type=F32) + sums[6:7, lanes]
            if part == 0:
                value = value * (width // heads) ** -0.5
            qkv_v[where, lanes] = value.astype(BF16)
        return carry

    lax.fori_loop(0, length // rows, project, 0)
    keep(qkv_v, qkv_all)
    spread.forward(3)
    size = width // heads
    limit = prefix[0]
    bench = 256

    for block in range(length // bench):
        reach = min(length, max((block + 1) * bench, PREFIX_TOP))
        span = slice(block * bench, (block + 1) * bench)

        def attend(head, carry, block=block, span=span, reach=reach):
            line = block * bench + lax.broadcasted_iota(jnp.int32, (bench, reach), 0)
            place = lax.broadcasted_iota(jnp.int32, (bench, reach), 1)
            seen = (place <= line) | (place < limit)
            q = qkv_v[span, block_of(head, size)]
            k = qkv_v[0:reach, pl.ds(pl.multiple_of(width + head * size, size), size)]
            v = qkv_v[0:reach, pl.ds(pl.multiple_of(2 * width + head * size, size), size)]
            scores = lax.dot_general(q, k, (((1,), (1,)), ((), ())), preferred_element_type=F32)
            scores = jnp.where(seen, scores, -1e30)
            top = jnp.max(scores, axis=-1, keepdims=True)
            expd = jnp.exp(scores - top)
            total = jnp.sum(expd, axis=-1, keepdims=True)
            probs = (expd * (1.0 / total)).astype(BF16)
            mixed_v[span, block_of(head, size)] = jnp.dot(probs, v, preferred_element_type=F32).astype(BF16)
            lse_v[head, span, :] = jnp.broadcast_to(top + jnp.log(total), (bench, 128))
            return carry

        lax.fori_loop(0, heads, attend, 0)
        if block == 2:
            spread.forward(2)
    keep(mixed_v, mixed_all)
    keep(lse_v, lse_all)
    spread.forward(1)
    spread.arrived(2)
    locals_[2].wait()
    load = pltpu.make_async_copy(wo, wo_v, local_sem.at[14])
    load.start()
    load.wait()

    def out_part(rank, index):
        return jnp.dot(mixed_v[block_of(rank, rows), :], wo_v[:, block_of(index, 512)], preferred_element_type=F32)

    def take_second(index, total):
        where = block_of(index, 512)
        second[:, where] = tokens[:, where].astype(F32) + total + sums[4:5, where]

    end = tensor_sum(
        spot, out_part, core_send, core_recv, x_send, x_recv, s_send.at[0], s_recv.at[0], take_second
    )
    end()

    def norm2(index, carry):
        where = block_of(index, strip)
        center, scale = normal_parts(second[where, :])
        h2v[pl.ds(pl.multiple_of(base + index * strip, strip), strip), :] = (
            center * scale * sums[2:3, :] + sums[3:4, :]
        ).astype(BF16)
        return carry

    lax.fori_loop(0, rows // strip, norm2, 0)
    gather2 = TensorGather(spot, h2v.at[block_of(spot.tensor, rows)], h2v, rows, g_send.at[2], g_recv.at[2])
    gather2.pass_on()
    spread.forward(3)
    gather2.finish()
    gather_d.finish()
    keep(h2v, h2_all)
    for part in range(2):
        spread.arrived(3 + part)
        locals_[3 + part].wait()
        lanes_of = pl.ds(part * tall, tall)
        load = pltpu.make_async_copy(w1.at[:, lanes_of], w1_v.at[:, lanes_of], local_sem.at[14])
        load.start()
        load.wait()

        def stored(block, lanes_of=lanes_of):
            slot = lax.rem(block, 2)
            return pltpu.make_async_copy(
                slope_v.at[slot], slope_all.at[block_of(block, rows), lanes_of], local_sem.at[15 + slot]
            )

        def lift_rows(block, carry, part=part, stored=stored):
            where_rows = block_of(block, rows)
            if part == 0:
                pl.when(block >= 2)(lambda: stored(block).wait())
            else:
                stored(block).wait()

            def lift(index, carry):
                where = block_of(part * (tall // 512) + index, 512)
                u = jnp.dot(h2v[where_rows, :], w1_v[:, where], preferred_element_type=F32) + sums[7:8, where]
                below = 0.5 * (1.0 + lax.erf(u * 0.7071067811865476))
                gated_v[where_rows, where] = (u * below).astype(BF16)
                slope_v[lax.rem(block, 2), :, block_of(index, 512)] = (
                    below + u * (0.3989422804014327 * jnp.exp(-0.5 * u * u))
                )
                return carry

            lax.fori_loop(0, tall // 512, lift, 0)
            stored(block).start()
            return carry

        lax.fori_loop(0, length // rows, lift_rows, 0)
        if part == 0:
            spread.forward(3)
    keep(gated_v, gated_all)
    spread.arrived(6)
    spread.arrived(5)
    spread.finish()
    for copy in small_copies:
        copy.wait_send()
    for copy in locals_[5:] + [stored(jnp.int32(block)) for block in range(2)]:
        copy.wait()


def forward_call(heads, count, prefix, tokens, cotangent, small, qkv_shard, out_shard, up_shard, down_shard):
    rows, features = tokens.shape
    length = rows * 4
    depth, triple = qkv_shard.shape
    width = out_shard.shape[0]
    hidden = up_shard.shape[1]
    outer, inner = split_of(count)
    shape = jax.ShapeDtypeStruct
    hbm = pl.BlockSpec(memory_space=pl.ANY)
    vmem = pl.BlockSpec(memory_space=pltpu.VMEM)
    dma = pltpu.SemaphoreType.DMA
    pieces = 7
    return pl.pallas_call(
        functools.partial(forward_kernel, heads, count),
        out_shape=[
            shape((features, triple), BF16),
            shape((width, features), BF16),
            shape((features, hidden), BF16),
            shape((hidden, features), BF16),
            shape((length, features), BF16),
            shape((length, features), BF16),
            shape((length, triple), BF16),
            shape((length, width), BF16),
            shape((heads, length, 128), F32),
            shape((rows, features), F32),
            shape((length, features), BF16),
            shape((length, hidden), BF16),
            shape((length, hidden), F32),
            shape((8, features), F32),
        ],
        in_specs=[pl.BlockSpec(memory_space=pltpu.SMEM)] + [vmem] * 7,
        out_specs=[hbm] * 9 + [vmem] + [hbm] * 3 + [vmem],
        scratch_shapes=[
            pltpu.VMEM((count, 40, 128), F32),
            pltpu.VMEM((length, features), BF16),
            pltpu.VMEM((features, triple), BF16),
            pltpu.VMEM((length, triple), BF16),
            pltpu.VMEM((length, width), BF16),
            pltpu.VMEM((heads, length, 128), F32),
            pltpu.VMEM((width, features), BF16),
            pltpu.VMEM((2, rows, features), BF16),
            pltpu.VMEM((2, rows, features), BF16),
            pltpu.VMEM((rows, features), BF16),
            pltpu.VMEM((rows, features), BF16),
            pltpu.VMEM((length, features), BF16),
            pltpu.VMEM((features, hidden), BF16),
            pltpu.VMEM((length, hidden), BF16),
            pltpu.VMEM((2, rows, hidden // 2), F32),
            dma((count,)),
            dma((count,)),
            dma((pieces + 1, outer)),
            dma((pieces + 1, outer)),
            dma((pieces, outer)),
            dma((pieces, outer)),
            dma((3, 3)),
            dma((3, 3)),
            dma((1, 3)),
            dma((1, 3)),
            dma((17,)),
        ],
        compiler_params=pltpu.CompilerParams(
            collective_id=0, has_side_effects=True, vmem_limit_bytes=VMEM_BYTES
        ),
    )(prefix, tokens, cotangent, small, qkv_shard, out_shard, up_shard, down_shard)
class Reduce:
    def __init__(self, spot, left, right, lanes, landing, target, shared, index, last):
        self.spot, self.left, self.right, self.lanes = spot, left, right, lanes
        self.landing, self.target, self.shared, self.index, self.last = landing, target, shared, index, last
        self.width = lanes.stop - lanes.start
        self.share = target.shape[0]
        self.stepped = {}
        self.held = ()
        row = spot.row
        self.inner = (row == 1) | (row == 2)
        self.steps = (
            jnp.where(row == 0, 3, 1), jnp.where(self.inner, 3, 2), jnp.where(row == 0, 1, jnp.where(row == 3, 3, 2)), 0
        )

    def block(self, owner, take):
        turned = jnp.transpose(self.left[:, block_of(owner, self.share)])

        def body(index, carry):
            source = self.right[:, pl.ds(pl.multiple_of(self.lanes.start + index * 512, 512), 512)]
            take(block_of(index, 512), jnp.dot(turned, source, preferred_element_type=F32))
            return carry

        lax.fori_loop(0, self.width // 512, body, 0)

    def y_copy(self, step):
        shared = self.shared
        area = pl.ds(0, self.width)
        return remote(
            shared["y_out"].at[step, :, area], shared["y_in"].at[step, :, area], shared["y_send"].at[step],
            shared["y_recv"].at[step], self.spot.beside(1), self.spot.tensor,
        )

    def z_copy(self, place):
        shared, step = self.shared, self.steps[place]
        return remote(
            shared["z_out"].at[place, :, pl.ds(0, self.width)], self.landing.at[step - 1],
            shared["z_send"].at[place], shared["z_recv"].at[self.index, step], self.spot.across(step),
            self.spot.tensor,
        )

    def near_copy(self):
        shared, spot = self.shared, self.spot
        area = pl.ds(0, self.width)
        return remote(
            shared["z_out"].at[0, :, area], shared["near"].at[:, area], shared["z_send"].at[0], shared["near_recv"].at[0],
            jnp.where(spot.row == 0, 1, 2) * spot.inner + spot.column, spot.tensor,
        )

    def produce(self, place):
        shared, spot = self.shared, self.spot
        row = lax.rem(spot.row + self.steps[place], spot.outer)
        if place in shared["y_busy"]:
            shared["y_busy"].pop(place).wait_send()

        def take(where, value):
            shared["y_out"][place, :, where] = value.astype(BF16)

        self.block(spot.beside(1, row), take)
        if self.index > 0:
            pl.semaphore_wait(shared["credit"], 1)
        copy = self.y_copy(place)
        copy.start()
        shared["y_busy"][place] = copy

    def hold(self, places):
        self.held = places
        for place in places:

            def take(where, value, place=place):
                self.shared["z_out"][place, :, where] = value.astype(BF16)

            self.block(self.spot.across(self.steps[place]), take)

    def serve(self, place):
        shared, spot = self.shared, self.spot
        self.y_copy(place).wait_recv()
        if place in shared["z_busy"]:
            shared["z_busy"].pop(place).wait_send()
        y_in, z_out = shared["y_in"], shared["z_out"]
        if place in self.held:
            for start in range(0, self.width, 512):
                where = slice(start, start + 512)
                z_out[place, :, where] = (
                    z_out[place, :, where].astype(F32) + y_in[place, :, where].astype(F32)
                ).astype(BF16)
        else:

            def take(where, value):
                z_out[place, :, where] = (value + y_in[place, :, where].astype(F32)).astype(BF16)

            self.block(spot.across(self.steps[place]), take)
        if not self.last:
            pl.semaphore_signal(
                shared["credit"], inc=1, device_id=(spot.beside(1), spot.tensor), device_id_type=MESH
            )
        if place == 3:
            return
        if place == 0:

            @pl.when(jnp.logical_not(self.inner))
            def _():
                if self.index > 0:
                    pl.semaphore_wait(shared["near_free"], 1)
                self.near_copy().start()

            @pl.when(self.inner)
            def _():
                self.z_copy(0).start()

        else:
            if place == 2:

                @pl.when(self.inner)
                def _():
                    self.near_copy().wait_recv()
                    for start in range(0, self.width, 512):
                        where = slice(start, start + 512)
                        z_out[2, :, where] = (
                            z_out[2, :, where].astype(F32) + shared["near"][:, where].astype(F32)
                        ).astype(BF16)
                    if not self.last:
                        pl.semaphore_signal(
                            shared["near_free"], inc=1,
                            device_id=(jnp.where(spot.row == 1, 0, 3) * spot.inner + spot.column, spot.tensor),
                            device_id_type=MESH,
                        )

            self.z_copy(place).start()
        shared["z_busy"][place] = self.z_copy(place)

    def landed(self, step):
        shared = self.shared
        remote(
            shared["z_out"].at[0, :, pl.ds(0, self.width)], self.landing.at[step - 1], shared["z_send"].at[0],
            shared["z_recv"].at[self.index, step], self.spot.across(1), self.spot.tensor,
        ).wait_recv()

    def settle(self):
        shared, spot = self.shared, self.spot
        pl.when(spot.row != 0)(lambda: self.landed(1))
        self.landed(2)
        pl.when(spot.row != 3)(lambda: self.landed(3))
        chunks = self.width // 128

        def load(chunk):
            slot = lax.rem(chunk, 4)
            return pltpu.make_async_copy(
                self.landing.at[:, :, block_of(chunk, 128)], shared["z_stage"].at[slot], shared["stage_sem"].at[slot]
            )

        def store(chunk):
            slot = lax.rem(chunk, 4)
            return pltpu.make_async_copy(
                shared["o_stage"].at[slot], self.target.at[:, block_of(chunk, 128)], shared["stage_sem"].at[4 + slot]
            )

        def add(chunk, carry):
            slot = lax.rem(chunk, 4)
            load(chunk).wait()
            pl.when(chunk + 3 < chunks)(lambda: load(chunk + 3).start())
            pl.when(chunk >= 4)(lambda: store(chunk - 4).wait())
            total = shared["z_out"][3, :, block_of(chunk, 128)].astype(F32)
            for step in range(spot.outer - 1):
                part = shared["z_stage"][slot, step].astype(F32)
                if step != 1:
                    part = jnp.where(spot.row == (0 if step == 0 else 3), 0.0, part)
                total = total + part
            shared["o_stage"][slot] = total
            store(chunk).start()
            return carry

        for chunk in range(3):
            load(jnp.int32(chunk)).start()
        lax.fori_loop(0, chunks, add, 0)
        for chunk in range(chunks - 4, chunks):
            store(jnp.int32(chunk)).wait()


def row_dot(left, right):
    return lax.dot_general(left, right, (((1,), (1,)), ((), ())), preferred_element_type=F32)


def backward_kernel(
    heads,
    count,
    prefix,
    sums,
    tokens,
    cotangent,
    wqkv,
    wo,
    w1,
    w2,
    h1_all,
    d_rows,
    qkv_all,
    mixed_all,
    lse_v,
    second,
    h2_all,
    gated_all,
    slope_all,
    layer_out,
    input_grad,
    grad_down,
    grad_up,
    grad_out,
    grad_qkv,
    vector_sums,
    bias_sums,
    land_down,
    land_up,
    land_out,
    land_qkv,
    weight_v,
    buf1,
    buf2,
    buf3,
    buf4,
    buf5,
    buf6,
    near,
    core_send,
    core_recv,
    x_send,
    x_recv,
    y_in,
    y_out,
    z_out,
    z_stage,
    o_stage,
    spare,
    line,
    dk_sum,
    dv_sum,
    vectors,
    biases,
    vector_in,
    bias_in,
    part_sum,
    part_in,
    y_send,
    y_recv,
    z_send,
    z_recv,
    g_send,
    g_recv,
    s_send,
    s_recv,
    v_send,
    v_recv,
    b_send,
    b_recv,
    t_send,
    t_recv,
    stage_sem,
    load_sem,
    near_recv,
    credit,
    ready,
    near_free,
):
    spot = Spot(count)
    rows, features = line.shape
    length = buf1.shape[0]
    width = wo.shape[0]
    hidden = w1.shape[1]
    triple = 3 * width
    size = width // heads
    scale = size ** -0.5
    tail = slice(triple, triple + width)
    shared = {
        "y_in": y_in, "y_out": y_out, "z_out": z_out, "z_stage": z_stage, "o_stage": o_stage, "y_send": y_send,
        "y_recv": y_recv, "z_send": z_send, "z_recv": z_recv, "credit": credit, "stage_sem": stage_sem,
        "y_busy": {}, "z_busy": {}, "near": near, "near_recv": near_recv, "near_free": near_free,
    }
    down = Reduce(spot, buf1, buf2, slice(0, hidden), land_down, grad_down, shared, 0, False)
    up = Reduce(spot, buf4, buf3, slice(0, hidden), land_up, grad_up, shared, 1, False)
    qkv = Reduce(spot, buf6, buf5, slice(0, triple), land_qkv, grad_qkv, shared, 2, False)
    out = Reduce(spot, buf1, buf2, tail, land_out, grad_out, shared, 3, True)

    def fetch(source, target, slot):
        copy = pltpu.make_async_copy(source, target, load_sem.at[slot])
        copy.start()
        return copy

    load_a = fetch(d_rows, buf1, 0)
    load_b = fetch(gated_all, buf2, 1)
    load_w = fetch(w2, weight_v, 2)
    slopes = [fetch(slope_all.at[pl.ds(part * rows, rows)], (spare, input_grad)[part % 2], 3 + part % 2) for part in range(2)]
    load_h = fetch(h2_all, buf4, 5)
    load_c = fetch(cotangent, line, 6)
    spot.meet(True)
    vectors[...] = jnp.zeros_like(vectors)
    biases[...] = jnp.zeros_like(biases)
    load_a.wait()
    load_b.wait()
    for place in range(spot.outer):
        down.produce(place)
    load_w.wait()
    tensor = (core_send, core_recv, x_send, x_recv)

    def down_part(rank, index):
        return jnp.dot(buf2[block_of(rank, rows), :], weight_v[:, block_of(index, 512)], preferred_element_type=F32)

    def take_out(index, total):
        where = block_of(index, 512)
        buf6[0:rows, where] = (spare[:, where] + total + sums[5:6, where]).astype(BF16)

    end = tensor_sum(
        spot, down_part, *tensor, s_send, s_recv, take_out, between=lambda: down.serve(0)
    )
    for part in range(length // rows):
        held = (spare, input_grad)[part % 2]
        slopes[part].wait()

        def lower(index, carry, part=part, held=held):
            where = block_of(index, 512)
            span = slice(part * rows, (part + 1) * rows)
            du = row_dot(buf1[span, :], weight_v[where, :]) * held[:, where]
            biases[pl.ds(index, 1), :] += jnp.sum(du, axis=0, keepdims=True)
            buf3[span, where] = du.astype(BF16)
            return carry

        lax.fori_loop(0, hidden // 512, lower, 0)
        if part + 2 < length // rows:
            slopes.append(fetch(slope_all.at[pl.ds((part + 2) * rows, rows)], held, 3 + part % 2))
        if part == 1:
            down.serve(1)
    load_s = fetch(second, spare, 3)
    load_s.wait()
    end()
    spot.release(ready)
    store_l = fetch(buf6.at[pl.ds(0, rows)], layer_out, 7)
    load_w = fetch(w1, weight_v, 2)
    load_h.wait()
    down.serve(2)
    down.hold((3,))
    load_q = fetch(qkv_all, buf2.at[:, pl.ds(0, triple)], 0)
    load_m = fetch(mixed_all, buf2.at[:, pl.ds(triple, width)], 1)
    up.produce(0)
    up.produce(1)
    up.produce(2)
    load_w.wait()

    def h2_part(rank, index):
        return row_dot(buf3[block_of(rank, rows), :], weight_v[block_of(index, 512), :])

    def take_h2(index, total):
        input_grad[:, block_of(index, 512)] = total

    pl.semaphore_wait(ready, 2)
    end = tensor_sum(spot, h2_part, *tensor, s_send, s_recv, take_h2)
    down.serve(3)
    up.produce(3)
    up.serve(0)
    end()
    spot.release(ready)
    store_l.wait()
    load_n = fetch(h1_all, buf6, 7)
    load_o = fetch(wo, weight_v.at[pl.ds(0, width)], 2)
    load_c.wait()
    strip = 32
    base = spot.tensor * rows

    def norm_back(rows_of, gain, grads, keep, first):
        center, inverse = normal_parts(rows_of)
        normal = center * inverse
        vectors[first : first + 1, :] += jnp.sum(grads * normal, axis=0, keepdims=True)
        vectors[first + 1 : first + 2, :] += jnp.sum(grads, axis=0, keepdims=True)
        scaled = grads * gain
        mean = jnp.mean(scaled, axis=-1, keepdims=True)
        slope = jnp.mean(scaled * normal, axis=-1, keepdims=True)
        return keep + inverse * (scaled - mean - normal * slope)

    def back2(index, carry):
        where = block_of(index, strip)
        dy = line[where, :].astype(F32)
        dx = norm_back(spare[where, :], sums[2:3, :], input_grad[where, :], dy, 2)
        vectors[4:5, :] += jnp.sum(dx, axis=0, keepdims=True)
        vectors[5:6, :] += jnp.sum(dy, axis=0, keepdims=True)
        input_grad[where, :] = dx
        buf1[pl.ds(pl.multiple_of(base + index * strip, strip), strip), :] = dx.astype(BF16)
        return carry

    lax.fori_loop(0, rows // strip, back2, 0)
    gather = TensorGather(spot, buf1.at[block_of(spot.tensor, rows)], buf1, rows, g_send, g_recv)
    load_t = fetch(tokens, line, 6)
    up.serve(1)
    down.settle()
    gather.pass_on()
    load_o.wait()
    gather.finish()
    load_q.wait()
    load_m.wait()

    def mix_back(index, carry):
        where = block_of(index, rows)
        buf5[where, tail] = row_dot(buf1[where, :], weight_v[0:width, :]).astype(BF16)
        return carry

    lax.fori_loop(0, length // rows, mix_back, 0)
    load_w = fetch(wqkv, weight_v.at[:, pl.ds(0, triple)], 2)
    limit = prefix[0]
    bench = 256

    def attend(head, carry):
        q_at = block_of(head, size)
        k_at = pl.ds(pl.multiple_of(width + head * size, size), size)
        v_at = pl.ds(pl.multiple_of(2 * width + head * size, size), size)
        o_at = pl.ds(pl.multiple_of(triple + head * size, size), size)
        dk_sum[...] = jnp.zeros_like(dk_sum)
        dv_sum[...] = jnp.zeros_like(dv_sum)
        for block in range(length // bench):
            reach = min(length, max((block + 1) * bench, PREFIX_TOP))
            span = slice(block * bench, (block + 1) * bench)
            row_of = block * bench + lax.broadcasted_iota(jnp.int32, (bench, reach), 0)
            place = lax.broadcasted_iota(jnp.int32, (bench, reach), 1)
            seen = (place <= row_of) | (place < limit)
            q = buf2[span, q_at]
            k = buf2[0:reach, k_at]
            v = buf2[0:reach, v_at]
            do = buf5[span, o_at]
            scores = jnp.where(seen, row_dot(q, k), -1e30)
            probs = jnp.exp(scores - lse_v[head, span, 0:1])
            d_probs = row_dot(do, v)
            inner = jnp.sum(probs * d_probs, axis=-1, keepdims=True)
            d_scores = (probs * (d_probs - inner)).astype(BF16)
            flip = (((0,), (0,)), ((), ()))
            dv_sum[0:reach, :] += lax.dot_general(probs.astype(BF16), do, flip, preferred_element_type=F32)
            dk_sum[0:reach, :] += lax.dot_general(d_scores, q, flip, preferred_element_type=F32)
            dq = jnp.dot(d_scores, k, preferred_element_type=F32) * scale
            biases[4:5, q_at] += jnp.sum(dq, axis=0, keepdims=True)
            buf5[span, q_at] = dq.astype(BF16)
        buf5[:, k_at] = dk_sum[...].astype(BF16)
        buf5[:, v_at] = dv_sum[...].astype(BF16)
        biases[5:6, q_at] += jnp.sum(dv_sum[...], axis=0, keepdims=True)
        return carry

    lax.fori_loop(0, heads, attend, 0)
    load_n.wait()
    qkv.produce(0)
    qkv.produce(1)
    up.serve(2)
    qkv.produce(2)
    load_w.wait()

    def h1_part(rank, index):
        return row_dot(buf5[block_of(rank, rows), 0:triple], weight_v[block_of(index, 512), 0:triple])

    def take_h1(index, total):
        spare[:, block_of(index, 512)] = total

    pl.semaphore_wait(ready, 2)
    end = tensor_sum(spot, h1_part, *tensor, s_send, s_recv, take_h1)
    up.serve(3)
    qkv.produce(3)
    qkv.serve(0)
    out.produce(0)
    end()
    load_t.wait()

    def back1(index, carry):
        where = block_of(index, strip)
        dx = norm_back(line[where, :].astype(F32), sums[0:1, :], spare[where, :], input_grad[where, :], 0)
        input_grad[where, :] = dx
        return carry

    lax.fori_loop(0, rows // strip, back1, 0)
    share = grad_up.shape[0]
    vector_copies, bias_copies = [], []
    for step in range(1, count):
        peer = lax.rem(spot.dp + step, count)
        vector_copies.append(remote(
            vectors.at[:, block_of(peer, share)], vector_in.at[spot.dp], v_send.at[step], v_recv.at[step], peer,
            spot.tensor,
        ))
        bias_copies.append(remote(biases, bias_in.at[spot.dp], b_send.at[step], b_recv.at[step], peer, spot.tensor))
    for copy in vector_copies + bias_copies:
        copy.start()
    vector_in[spot.dp] = vectors[:, block_of(spot.dp, share)]
    bias_in[spot.dp] = biases[...]
    up.settle()
    qkv.serve(1)
    out.produce(1)
    for copy in vector_copies + bias_copies:
        copy.wait_recv()
    total, bias_total = vector_in[0], bias_in[0]
    for index in range(1, count):
        total = total + vector_in[index]
        bias_total = bias_total + bias_in[index]
    part_sum[...] = total
    bias_sums[...] = bias_total
    part_copies = [
        remote(part_sum, part_in.at[spot.tensor], t_send.at[slot], t_recv.at[slot], spot.dp, peer)
        for slot, peer in enumerate((spot.x_peer, spot.core_peer, spot.far_peer))
    ]
    for copy in part_copies:
        copy.start()
    part_in[spot.tensor] = part_sum[...]
    qkv.serve(2)
    out.produce(2)
    for copy in part_copies:
        copy.wait_recv()
    vector_sums[...] = part_in[0] + part_in[1] + part_in[2] + part_in[3]
    qkv.serve(3)
    out.produce(3)
    out.serve(0)
    out.serve(1)
    out.serve(2)
    for copy in vector_copies + bias_copies + part_copies:
        copy.wait_send()
    qkv.settle()
    out.serve(3)
    out.settle()
    for copy in list(shared["y_busy"].values()) + list(shared["z_busy"].values()):
        copy.wait_send()


def backward_call(heads, count, prefix, sums, tokens, cotangent, weights, saved):
    rows, features = tokens.shape
    length = rows * 4
    share = features // count
    wqkv, wo, w1, w2 = weights
    width, hidden, triple = wo.shape[0], w1.shape[1], wqkv.shape[1]
    outer, inner = split_of(count)
    shape = jax.ShapeDtypeStruct
    hbm = pl.BlockSpec(memory_space=pl.ANY)
    vmem = pl.BlockSpec(memory_space=pltpu.VMEM)
    dma = pltpu.SemaphoreType.DMA
    regular = pltpu.SemaphoreType.REGULAR
    wide = (length, features)
    return pl.pallas_call(
        functools.partial(backward_kernel, heads, count),
        out_shape=[
            shape((rows, features), BF16),
            shape((rows, features), F32),
            shape((share, hidden), F32),
            shape((share, hidden), F32),
            shape((share, width), F32),
            shape((share, triple), F32),
            shape((8, share), F32),
            shape((8, 512), F32),
            shape((outer - 1, share, hidden), BF16),
            shape((outer - 1, share, hidden), BF16),
            shape((outer - 1, share, width), BF16),
            shape((outer - 1, share, triple), BF16),
        ],
        in_specs=[pl.BlockSpec(memory_space=pltpu.SMEM), vmem] + [hbm] * 10 + [vmem] + [hbm] * 4,
        out_specs=[hbm, vmem] + [hbm] * 4 + [vmem] * 2 + [hbm] * 4,
        scratch_shapes=[
            pltpu.VMEM((hidden, features), BF16),
            pltpu.VMEM(wide, BF16),
            pltpu.VMEM(wide, BF16),
            pltpu.VMEM(wide, BF16),
            pltpu.VMEM(wide, BF16),
            pltpu.VMEM(wide, BF16),
            pltpu.VMEM(wide, BF16),
            pltpu.VMEM((share, hidden), BF16),
            pltpu.VMEM((2, rows, features), BF16),
            pltpu.VMEM((2, rows, features), BF16),
            pltpu.VMEM((rows, features), BF16),
            pltpu.VMEM((rows, features), BF16),
            pltpu.VMEM((outer, share, hidden), BF16),
            pltpu.VMEM((outer, share, hidden), BF16),
            pltpu.VMEM((outer, share, hidden), BF16),
            pltpu.VMEM((4, outer - 1, share, 128), BF16),
            pltpu.VMEM((4, share, 128), F32),
            pltpu.VMEM((rows, features), F32),
            pltpu.VMEM((rows, features), BF16),
            pltpu.VMEM((length, width // heads), F32),
            pltpu.VMEM((length, width // heads), F32),
            pltpu.VMEM((8, features), F32),
            pltpu.VMEM((8, 512), F32),
            pltpu.VMEM((count, 8, share), F32),
            pltpu.VMEM((count, 8, 512), F32),
            pltpu.VMEM((8, share), F32),
            pltpu.VMEM((4, 8, share), F32),
            dma((outer,)),
            dma((outer,)),
            dma((outer,)),
            dma((4, outer)),
            dma((3,)),
            dma((3,)),
            dma((3,)),
            dma((3,)),
            dma((count,)),
            dma((count,)),
            dma((count,)),
            dma((count,)),
            dma((3,)),
            dma((3,)),
            dma((8,)),
            dma((8,)),
            dma((1,)),
            regular,
            regular,
            regular,
        ],
        compiler_params=pltpu.CompilerParams(
            collective_id=1, has_side_effects=True, vmem_limit_bytes=VMEM_BYTES
        ),
    )(prefix, sums, tokens, cotangent, wqkv, wo, w1, w2, *saved)


def pack_small(biases, vectors):
    devices = lax.axis_size("dp")
    parts = jnp.concatenate(biases, axis=0)
    lane = lax.broadcasted_iota(jnp.int32, (parts.shape[0], parts.shape[1] * devices), 1)
    wide = jnp.where(lane // parts.shape[1] == lax.axis_index("dp"), jnp.tile(parts, (1, devices)), 0)
    halves = jnp.pad(jnp.stack(vectors), ((0, 2), (0, 0)))
    return jnp.concatenate([wide, halves[:, :128], halves[:, 128:]], axis=0).astype(F32)


def layer_norm(rows, gain, shift):
    center = rows - jnp.mean(rows, axis=-1, keepdims=True)
    spread = jnp.mean(center * center, axis=-1, keepdims=True)
    return center * lax.rsqrt(spread + 1e-05) * gain + shift


def gelu_exact(values):
    return jax.nn.gelu(values, approximate=False)


def head_major(matrix, heads):
    return matrix.reshape(matrix.shape[0], heads, -1).transpose(1, 0, 2)


def row_major(stacked):
    return stacked.transpose(1, 0, 2).reshape(stacked.shape[1], -1)


def masked_scores(q_block, keys, start, prefix_len):
    scores = jnp.einsum("hqd,hkd->hqk", q_block, keys, preferred_element_type=jnp.float32)
    rows = start + lax.broadcasted_iota(jnp.int32, scores.shape[1:], 0)
    cols = lax.broadcasted_iota(jnp.int32, scores.shape[1:], 1)
    seen = (cols <= rows) | (cols < prefix_len)
    return jnp.where(seen[None], scores, -1e30)


def to_blocks(stacked, count):
    heads, length = (stacked.shape[0], stacked.shape[1])
    return stacked.reshape((heads, count, length // count) + stacked.shape[2:]).swapaxes(0, 1)


def from_blocks(blocked):
    count, heads, block = (blocked.shape[0], blocked.shape[1], blocked.shape[2])
    return blocked.swapaxes(0, 1).reshape((heads, count * block) + blocked.shape[3:])


def contract_rows(left, right):
    return jnp.einsum("ld,le->de", left, right, preferred_element_type=jnp.float32)


def times_transpose(left, right):
    return jnp.einsum("le,de->ld", left, right, preferred_element_type=jnp.float32)


def plain(
    tokens,
    prefix,
    query_weight,
    key_weight,
    value_weight,
    out_weight,
    query_bias,
    value_bias,
    up_weight,
    down_weight,
    up_bias,
    norm1_gain,
    norm1_bias,
    norm2_gain,
    norm2_bias,
    out_bias,
    down_bias,
    cotangent,
):
    f32 = jnp.float32
    bf16 = jnp.bfloat16
    devices = lax.axis_size("dp")
    small = (query_bias, value_bias, up_bias, norm1_gain, norm1_bias, norm2_gain, norm2_bias, out_bias, down_bias)
    packed = jnp.concatenate([part.reshape(-1) for part in small])
    packed = lax.all_gather(packed, "dp", axis=0, tiled=False)
    pieces = []
    offset = 0
    for part in small:
        piece = packed[:, offset : offset + part.size].reshape((devices,) + part.shape)
        offset += part.size
        pieces.append(jnp.moveaxis(piece, 0, -2).reshape(part.shape[:-1] + (-1,)))
    bq, bv, b1, g1, n1, g2, n2, bo, b2 = pieces
    wq, wk, wv, wo = (
        lax.all_gather(query_weight, "dp", axis=0, tiled=True),
        lax.all_gather(key_weight, "dp", axis=0, tiled=True),
        lax.all_gather(value_weight, "dp", axis=0, tiled=True),
        lax.all_gather(out_weight, "dp", axis=1, tiled=True),
    )
    w1, w2 = (
        lax.all_gather(up_weight, "dp", axis=0, tiled=True),
        lax.all_gather(down_weight, "dp", axis=1, tiled=True),
    )
    g1f, n1f, g2f, n2f = (g1.astype(f32), n1.astype(f32), g2.astype(f32), n2.astype(f32))
    bof, b2f = (bo.astype(f32), b2.astype(f32))
    heads = bq.shape[0]
    head_size = bq.shape[1]
    scale = head_size ** (-0.5)
    prefix_len = prefix[0]
    xf = tokens.astype(f32)
    h1 = layer_norm(xf, g1f, n1f).astype(bf16)
    rows1 = lax.all_gather(h1, "tensor", axis=0, tiled=True)
    length = rows1.shape[0]
    block = min(512, length)
    count = length // block
    query = (
        (jnp.dot(rows1, wq, preferred_element_type=f32) + bq.astype(f32).reshape(-1)) * scale
    ).astype(bf16)
    keyed = jnp.dot(rows1, wk, preferred_element_type=f32).astype(bf16)
    valued = (jnp.dot(rows1, wv, preferred_element_type=f32) + bv.astype(f32).reshape(-1)).astype(
        bf16
    )
    q_heads = head_major(query, heads)
    k_heads = head_major(keyed, heads)
    v_heads = head_major(valued, heads)
    q_blocks = to_blocks(q_heads, count)
    starts = jnp.arange(count, dtype=jnp.int32) * block

    def forward_block(item):
        q_block, start = item
        scores = masked_scores(q_block, k_heads, start, prefix_len)
        top = jnp.max(scores, axis=-1, keepdims=True)
        expd = jnp.exp(scores - top)
        total = jnp.sum(expd, axis=-1, keepdims=True)
        probs = (expd / total).astype(bf16)
        outv = jnp.einsum("hqk,hkd->hqd", probs, v_heads, preferred_element_type=f32)
        return (outv.astype(bf16), (top + jnp.log(total))[..., 0])

    o_blocks, lse_blocks = lax.map(forward_block, (q_blocks, starts))
    mixed = row_major(from_blocks(o_blocks))
    attn_part = jnp.dot(mixed, wo, preferred_element_type=f32)
    attn_total = lax.psum_scatter(attn_part.astype(bf16), "tensor", scatter_dimension=0, tiled=True).astype(f32)
    second = xf + attn_total + bof
    h2 = layer_norm(second, g2f, n2f).astype(bf16)
    rows2 = lax.all_gather(h2, "tensor", axis=0, tiled=True)
    hidden = jnp.dot(rows2, w1, preferred_element_type=f32) + b1.astype(f32).reshape(-1)
    gated = gelu_exact(hidden).astype(bf16)
    mlp_part = jnp.dot(gated, w2, preferred_element_type=f32)
    mlp_total = lax.psum_scatter(
        mlp_part.astype(jnp.bfloat16), "tensor", scatter_dimension=0, tiled=True
    ).astype(jnp.float32)
    layer_out = (second + mlp_total + b2f).astype(bf16)
    d_out = cotangent.astype(f32)
    g_b2 = jnp.sum(d_out, axis=0)
    d_rows = lax.all_gather(cotangent, "tensor", axis=0, tiled=True)
    d_gated = times_transpose(d_rows, w2)
    d_hidden = jax.vjp(gelu_exact, hidden)[1](d_gated)[0]
    g_b1 = jnp.sum(d_hidden, axis=0).reshape(b1.shape)
    d_hidden_low = d_hidden.astype(bf16)
    d_h2_part = times_transpose(d_hidden_low, w1)
    g_w2 = contract_rows(gated, d_rows)
    g_w1 = contract_rows(rows2, d_hidden_low)
    d_h2 = lax.psum_scatter(d_h2_part.astype(bf16), "tensor", scatter_dimension=0, tiled=True).astype(f32)
    norm2_back = jax.vjp(layer_norm, second, g2f, n2f)[1]
    d_second_ln, g_g2, g_n2 = norm2_back(d_h2)
    d_second = d_out + d_second_ln
    g_bo = jnp.sum(d_second, axis=0)
    d_second_low = d_second.astype(bf16)
    back_rows = lax.all_gather(d_second_low, "tensor", axis=0, tiled=True)
    g_wo = contract_rows(mixed, back_rows)
    d_mixed = times_transpose(back_rows, wo).astype(bf16)
    do_blocks = to_blocks(head_major(d_mixed, heads), count)

    def backward_block(carry, item):
        d_keys, d_vals = carry
        q_block, do_block, lse_block, start = item
        scores = masked_scores(q_block, k_heads, start, prefix_len)
        probs = jnp.exp(scores - lse_block[..., None])
        d_probs = jnp.einsum("hqd,hkd->hqk", do_block, v_heads, preferred_element_type=f32)
        d_vals = d_vals + jnp.einsum(
            "hqk,hqd->hkd", probs.astype(bf16), do_block, preferred_element_type=f32
        )
        inner = jnp.sum(probs * d_probs, axis=-1, keepdims=True)
        d_scores = (probs * (d_probs - inner)).astype(bf16)
        d_query = jnp.einsum("hqk,hkd->hqd", d_scores, k_heads, preferred_element_type=f32)
        d_keys = d_keys + jnp.einsum("hqk,hqd->hkd", d_scores, q_block, preferred_element_type=f32)
        return ((d_keys, d_vals), d_query)

    empty = jnp.zeros(k_heads.shape, f32)
    (d_keys, d_vals), dq_blocks = lax.scan(
        backward_block, (empty, empty), (q_blocks, do_blocks, lse_blocks, starts)
    )
    d_query = row_major(from_blocks(dq_blocks)) * scale
    d_keys = row_major(d_keys)
    d_vals = row_major(d_vals)
    g_bq = jnp.sum(d_query, axis=0).reshape(bq.shape)
    g_bv = jnp.sum(d_vals, axis=0).reshape(bv.shape)
    dq_low, dk_low, dv_low = (d_query.astype(bf16), d_keys.astype(bf16), d_vals.astype(bf16))
    g_wq = contract_rows(rows1, dq_low)
    g_wk = contract_rows(rows1, dk_low)
    g_wv = contract_rows(rows1, dv_low)
    d_h1_part = (
        times_transpose(dq_low, wq) + times_transpose(dk_low, wk) + times_transpose(dv_low, wv)
    )
    d_h1 = lax.psum_scatter(d_h1_part.astype(bf16), "tensor", scatter_dimension=0, tiled=True).astype(f32)
    norm1_back = jax.vjp(layer_norm, xf, g1f, n1f)[1]
    d_input_ln, g_g1, g_n1 = norm1_back(d_h1)
    input_grad = d_second + d_input_ln
    def scatter(part, dim):
        return lax.psum_scatter(part.astype(bf16), "dp", scatter_dimension=dim, tiled=True).astype(f32)

    s_w2, s_w1, s_wo = scatter(g_w2, 1), scatter(g_w1, 0), scatter(g_wo, 1)
    s_wq, s_wk, s_wv = scatter(g_wq, 0), scatter(g_wk, 0), scatter(g_wv, 0)

    def by_device(part):
        return jnp.moveaxis(part.reshape(part.shape[:-1] + (devices, -1)), -2, 0).reshape(devices, -1)

    rows = [by_device(part) for part in (g_bq, g_bv, g_b1, g_g1, g_n1, g_g2, g_n2, g_bo, g_b2)]
    total = lax.psum_scatter(jnp.concatenate(rows, axis=1), "dp", scatter_dimension=0, tiled=True)[0]
    offset = 0
    outs = []
    for part in (query_bias, value_bias, up_bias):
        outs.append(total[offset : offset + part.size].reshape(part.shape))
        offset += part.size
    s_bq, s_bv, s_b1 = outs
    vectors = lax.psum_scatter(
        total[offset:].reshape(6, lax.axis_size("tensor"), -1), "tensor", scatter_dimension=1, tiled=True
    ).reshape(6, -1)
    s_g1, s_n1, s_g2, s_n2, s_bo, s_b2 = (vectors[index] for index in range(6))
    return (
        layer_out,
        input_grad,
        s_wq,
        s_wk,
        s_wv,
        s_wo,
        s_bq,
        s_bv,
        s_w1,
        s_w2,
        s_b1,
        s_g1,
        s_n1,
        s_g2,
        s_n2,
        s_bo,
        s_b2,
    )


def fast(
    tokens,
    prefix,
    query_weight,
    key_weight,
    value_weight,
    out_weight,
    query_bias,
    value_bias,
    up_weight,
    down_weight,
    up_bias,
    norm1_gain,
    norm1_bias,
    norm2_gain,
    norm2_bias,
    out_bias,
    down_bias,
    cotangent,
):
    devices = lax.axis_size("dp")
    me = lax.axis_index("dp")
    heads = query_bias.shape[0]
    small = pack_small(
        (query_bias, value_bias, up_bias), (norm1_gain, norm1_bias, norm2_gain, norm2_bias, out_bias, down_bias)
    )
    results = forward_call(
        heads, devices, prefix, tokens, cotangent, small,
        jnp.concatenate([query_weight, key_weight, value_weight], axis=1), out_weight, up_weight, down_weight,
    )
    layer_out, input_grad, g_w2, g_w1, g_wo, g_qkv, vectors, biases, *_ = backward_call(
        heads, devices, prefix, results[-1], tokens, cotangent, results[:4], results[4:-1]
    )
    g_wq, g_wk, g_wv = jnp.split(g_qkv, 3, axis=1)
    vectors = vectors.reshape(8, lax.axis_size("tensor"), -1)
    vectors = lax.dynamic_index_in_dim(vectors, lax.axis_index("tensor"), axis=1, keepdims=False)

    def own(flat, part):
        whole = flat.reshape(part.shape[0], -1)
        return lax.dynamic_slice_in_dim(whole, me * part.shape[1], part.shape[1], axis=1)

    width = out_weight.shape[0]
    up_size = up_bias.size * devices
    g_b1 = own(biases[: up_size // 512].reshape(-1), up_bias)
    g_bq = own(biases[4, :width], query_bias)
    g_bv = own(biases[5, :width], value_bias)
    return (
        layer_out, input_grad, g_wq, g_wk, g_wv, g_wo.T, g_bq, g_bv, g_w1, g_w2.T, g_b1,
        vectors[0], vectors[1], vectors[2], vectors[3], vectors[4], vectors[5],
    )


def local(*args):
    tokens, query_weight, up_weight = args[0], args[2], args[8]
    devices = lax.axis_size("dp")
    features = tokens.shape[1]
    share = features // devices
    fits = (
        lax.axis_size("tensor") == 4
        and devices == 8
        and share % 128 == 0
        and tokens.shape[0] == 256
        and query_weight.shape[1] == 512
        and args[6].shape[0] == 4
        and features == 2048
        and up_weight.shape[1] == 2048
    )
    return fast(*args) if fits else plain(*args)


def solution(mesh):
    in_specs = (
        P(("dp", "tensor"), None),
        P("dp"),
        P("dp", "tensor"),
        P("dp", "tensor"),
        P("dp", "tensor"),
        P("tensor", "dp"),
        P("tensor", "dp"),
        P("tensor", "dp"),
        P("dp", "tensor"),
        P("tensor", "dp"),
        P("tensor", "dp"),
        P("dp"),
        P("dp"),
        P("dp"),
        P("dp"),
        P("dp"),
        P("dp"),
        P(("dp", "tensor"), None),
    )
    out_specs = (
        P(("dp", "tensor"), None),
        P(("dp", "tensor"), None),
        P("dp", "tensor"),
        P("dp", "tensor"),
        P("dp", "tensor"),
        P("tensor", "dp"),
        P("tensor", "dp"),
        P("tensor", "dp"),
        P("dp", "tensor"),
        P("tensor", "dp"),
        P("tensor", "dp"),
        P(("dp", "tensor")),
        P(("dp", "tensor")),
        P(("dp", "tensor")),
        P(("dp", "tensor")),
        P(("dp", "tensor")),
        P(("dp", "tensor")),
    )
    return jax.shard_map(local, mesh=mesh, in_specs=in_specs, out_specs=out_specs, check_vma=False)
```

```python
import functools

import jax
import jax.numpy as jnp
from jax import lax
from jax.experimental import pallas as pl
from jax.experimental.pallas import tpu as pltpu
from jax.sharding import PartitionSpec as P

MESH = pl.DeviceIdType.MESH
F32 = jnp.float32
BF16 = jnp.bfloat16
PREFIX_TOP = 512
VMEM_BYTES = 67043328


def split_of(count):
    inner = 1
    for size in range(1, count + 1):
        if size * size <= count and count % size == 0:
            inner = size
    return count // inner, inner


def remote(source, target, send_sem, recv_sem, dp, tensor):
    return pltpu.make_async_remote_copy(
        src_ref=source,
        dst_ref=target,
        send_sem=send_sem,
        recv_sem=recv_sem,
        device_id=(dp, tensor),
        device_id_type=MESH,
    )


def block_of(index, size):
    return pl.ds(pl.multiple_of(index * size, size), size)


class Spot:
    def __init__(self, count):
        self.outer, self.inner = split_of(count)
        self.count = count
        self.dp = lax.axis_index("dp")
        self.tensor = lax.axis_index("tensor")
        self.row = lax.div(self.dp, self.inner)
        self.column = lax.rem(self.dp, self.inner)
        self.core_peer = self.tensor + 1 - 2 * lax.rem(self.tensor, 2)
        self.x_peer = lax.rem(self.tensor + 2, 4)
        self.far_peer = lax.rem(self.core_peer + 2, 4)

    def across(self, step):
        return lax.rem(self.row + step, self.outer) * self.inner + self.column

    def beside(self, step, row=None):
        return (self.row if row is None else row) * self.inner + lax.rem(self.column + step, self.inner)

    def meet(self, far=False):
        barrier = pltpu.get_barrier_semaphore()
        for step in range(1, self.count):
            pl.semaphore_signal(
                barrier, inc=1, device_id=(lax.rem(self.dp + step, self.count), self.tensor), device_id_type=MESH
            )
        for peer in (self.core_peer, self.x_peer) + ((self.far_peer,) if far else ()):
            pl.semaphore_signal(barrier, inc=1, device_id=(self.dp, peer), device_id_type=MESH)
        pl.semaphore_wait(barrier, self.count + 1 + far)

    def release(self, ready):
        for peer in (self.core_peer, self.x_peer):
            pl.semaphore_signal(ready, inc=1, device_id=(self.dp, peer), device_id_type=MESH)


class Spread:
    AHEAD = 2

    def __init__(self, spot, pieces, late, own_at, sems):
        self.spot, self.pieces, self.late, self.sems = spot, pieces, late, sems
        self.flows = [(piece, 0) for piece in range(len(pieces)) if piece != late] + [(late, 0), (late, 1)]
        self.own_at = own_at
        self.order = (2, jnp.where(spot.row == 0, 3, 1), jnp.where(spot.row == 0, 1, 3))
        self.sent = []
        self.todo = [(flow, place) for flow in range(len(self.flows)) for place in range(3)]
        for piece in own_at[None]:
            self.send_own(piece)
        for flow in range(self.AHEAD):
            self.send_rows(flow)

    def owner(self, row, side):
        return row * 2 + lax.rem(self.spot.column + side, 2)

    def launch(self, condition, copy):
        if condition is None:
            copy().start()
        else:
            pl.when(condition)(lambda: copy().start())
        self.sent.append((condition, copy))

    def along(self, flow, step, source_row, target_row, send_slot):
        piece, side = self.flows[flow]
        source, target = self.pieces[piece]
        place = target(self.owner(source_row, side))
        if source_row is not self.spot.row or side:
            source = place
        return remote(
            source, place, self.sems[0].at[flow, send_slot], self.sems[1].at[flow, step],
            target_row * 2 + self.spot.column, self.spot.tensor,
        )

    def send_rows(self, flow):
        row = self.spot.row
        if self.flows[flow][1]:
            self.beside(self.late, 0, row).wait_recv()
        for step, condition in ((2, None), (1, row != 3), (3, row != 0)):
            self.launch(
                condition,
                functools.partial(self.along, flow, step, row, lax.rem(row + step, 4), step),
            )

    def hand_over(self, flow):
        row = self.spot.row
        self.launch(
            (row == 1) | (row == 2),
            lambda: self.along(flow, 2 * row - 1, lax.rem(row + 2, 4), (row - 1) * 3, 0),
        )

    def beside(self, piece, step, source_row):
        spot = self.spot
        source, target = self.pieces[piece]
        place = target(self.owner(source_row, 0))
        if source_row is not spot.row:
            source = place
        return remote(
            source, place, self.sems[2].at[piece, step], self.sems[3].at[piece, step], spot.beside(1), spot.tensor
        )

    def beside_arrival(self, piece, step, source_row):
        source, target = self.pieces[piece]
        return remote(
            source, target(self.owner(source_row, 1)), self.sems[2].at[piece, step], self.sems[3].at[piece, step],
            self.spot.beside(1), self.spot.tensor,
        )

    def send_own(self, piece):
        self.launch(None, functools.partial(self.beside, piece, 0, self.spot.row))

    def forward(self, count):
        for _ in range(count):
            if not self.todo:
                return
            flow, place = self.todo.pop(0)
            step = self.order[place]
            row = lax.rem(self.spot.row + 4 - step, 4)
            self.along(flow, step, row, self.spot.row, 0).wait_recv()
            if place == 0:
                self.hand_over(flow)
            piece = self.flows[flow][0]
            if piece != self.late:
                self.launch(None, functools.partial(self.beside, piece, step, row))
            if place == 2:
                if flow + self.AHEAD < len(self.flows):
                    self.send_rows(flow + self.AHEAD)
                for own in self.own_at.get(flow, ()):
                    self.send_own(own)

    def arrived(self, piece):
        while self.todo and self.flows[self.todo[0][0]][0] <= piece:
            self.forward(1)
        if piece != self.late:
            for step in range(4):
                self.beside_arrival(piece, step, lax.rem(self.spot.row + 4 - step, 4)).wait_recv()

    def finish(self):
        for condition, copy in self.sent:
            if condition is None:
                copy().wait_send()
            else:
                pl.when(condition)(lambda copy=copy: copy().wait_send())


class TensorGather:
    def __init__(self, spot, own, full, rows, send, recv):
        self.spot, self.full, self.rows, self.send, self.recv = spot, full, rows, send, recv
        place = self.at(spot.tensor)
        self.to_x = remote(own, place, send.at[0], recv.at[0], spot.dp, spot.x_peer)
        self.to_core = remote(own, place, send.at[1], recv.at[1], spot.dp, spot.core_peer)
        self.to_x.start()
        self.to_core.start()

    def at(self, index):
        return self.full.at[block_of(index, self.rows)]

    def pass_on(self):
        self.to_x.wait_recv()
        place = self.at(self.spot.x_peer)
        self.on = remote(place, place, self.send.at[2], self.recv.at[2], self.spot.dp, self.spot.core_peer)
        self.on.start()

    def finish(self):
        self.to_core.wait_recv()
        self.on.wait_recv()
        for copy in (self.to_x, self.to_core, self.on):
            copy.wait_send()


def tensor_sum(spot, product, core_send, core_recv, x_send, x_recv, send, recv, finish, between=None):
    width = core_send.shape[2]
    chunk = 512
    count = width // chunk

    def fill(rank, target):
        def body(index, carry):
            target[:, block_of(index, chunk)] = product(rank, index).astype(BF16)
            return carry

        lax.fori_loop(0, count, body, 0)

    copies = []
    for slot, rank in enumerate((spot.far_peer, spot.core_peer)):
        fill(rank, core_send.at[slot])
        copy = remote(core_send.at[slot], core_recv.at[slot], send.at[slot], recv.at[slot], spot.dp, spot.core_peer)
        copy.start()
        copies.append(copy)
    if between is not None:
        between()
    copies[0].wait_recv()

    def join(index, carry):
        where = block_of(index, chunk)
        x_send[:, where] = (product(spot.x_peer, index) + core_recv[0, :, where].astype(F32)).astype(BF16)
        return carry

    lax.fori_loop(0, count, join, 0)
    over = remote(x_send, x_recv, send.at[2], recv.at[2], spot.dp, spot.x_peer)
    over.start()
    copies[1].wait_recv()

    def end():
        over.wait_recv()

        def last(index, carry):
            where = block_of(index, chunk)
            total = product(spot.tensor, index) + core_recv[1, :, where].astype(F32) + x_recv[:, where].astype(F32)
            finish(index, total)
            return carry

        lax.fori_loop(0, count, last, 0)
        for copy in copies + [over]:
            copy.wait_send()

    return end


def normal_parts(rows):
    center = rows - jnp.mean(rows, axis=-1, keepdims=True)
    spread = jnp.mean(center * center, axis=-1, keepdims=True)
    return center, lax.rsqrt(spread + 1e-05)


def forward_kernel(
    heads,
    count,
    prefix,
    tokens,
    cotangent,
    small,
    qkv_shard,
    out_shard,
    up_shard,
    down_shard,
    wqkv,
    wo,
    w1,
    w2,
    h1_all,
    d_rows,
    qkv_all,
    mixed_all,
    lse_all,
    second,
    h2_all,
    gated_all,
    slope_all,
    sums,
    smalls,
    h1v,
    wqkv_v,
    qkv_v,
    mixed_v,
    lse_v,
    wo_v,
    core_send,
    core_recv,
    x_send,
    x_recv,
    h2v,
    w1_v,
    gated_v,
    slope_v,
    small_send,
    small_recv,
    z_send,
    z_recv,
    y_send,
    y_recv,
    g_send,
    g_recv,
    s_send,
    s_recv,
    local_sem,
):
    spot = Spot(count)
    rows, features = tokens.shape
    length = h1v.shape[0]
    depth = qkv_shard.shape[0]
    width = wo_v.shape[0]
    hidden = up_shard.shape[1]
    half = depth // 2
    tall = hidden // 2
    pieces = [
        (qkv_shard.at[pl.ds(part * half, half)],
         lambda owner, part=part: wqkv.at[block_of(owner * 2 + part, half)])
        for part in range(2)
    ]
    pieces.append((out_shard, lambda owner: wo.at[:, block_of(owner, depth)]))
    pieces += [
        (up_shard.at[:, pl.ds(part * tall, tall)],
         lambda owner, part=part: w1.at[block_of(owner, depth), pl.ds(part * tall, tall)])
        for part in range(2)
    ]
    pieces += [
        (down_shard.at[pl.ds(part * tall, tall)],
         lambda owner, part=part: w2.at[pl.ds(part * tall, tall), block_of(owner, depth)])
        for part in range(2)
    ]
    locals_ = []

    def keep(source, target):
        copy = pltpu.make_async_copy(source, target, local_sem.at[len(locals_)])
        copy.start()
        locals_.append(copy)

    spot.meet()
    small_copies = []
    for step in range(1, count):
        copy = remote(
            small, smalls.at[spot.dp], small_send.at[step], small_recv.at[step],
            lax.rem(spot.dp + step, count), spot.tensor,
        )
        copy.start()
        small_copies.append(copy)
    spread = Spread(
        spot, pieces, 6, {None: (0, 1, 2, 3), 0: (4,), 1: (6,), 2: (5,)}, (z_send, z_recv, y_send, y_recv)
    )
    for source, target in pieces:
        keep(source, target(spot.dp))
    smalls[spot.dp] = small[...]
    for step in range(1, count):
        owner = lax.rem(spot.dp + count - step, count)
        remote(
            small, smalls.at[owner], small_send.at[step], small_recv.at[step], spot.dp, spot.core_peer
        ).wait_recv()
    sums[...] = jnp.zeros_like(sums)
    joint = smalls[0, 0:24, :]
    for index in range(1, count):
        joint = joint + smalls[index, 0:24, :]
    lanes = 128
    for head in range(heads):
        sums[6:7, head * lanes : (head + 1) * lanes] = joint[head : head + 1, :]
        start = 2 * width + head * lanes
        sums[6:7, start : start + lanes] = joint[4 + head : 5 + head, :]
    for line in range(hidden // lanes):
        sums[7:8, line * lanes : (line + 1) * lanes] = joint[8 + line : 9 + line, :]
    for owner in range(count):
        for part in range(2):
            start = owner * depth + part * lanes
            sums[0:6, start : start + lanes] = smalls[owner, 24 + 8 * part : 30 + 8 * part, :]

    strip = 32
    base = spot.tensor * rows

    def norm1(index, carry):
        where = block_of(index, strip)
        center, scale = normal_parts(tokens[where, :].astype(F32))
        h1v[pl.ds(pl.multiple_of(base + index * strip, strip), strip), :] = (
            center * scale * sums[0:1, :] + sums[1:2, :]
        ).astype(BF16)
        return carry

    lax.fori_loop(0, rows // strip, norm1, 0)
    gather1 = TensorGather(spot, h1v.at[block_of(spot.tensor, rows)], h1v, rows, g_send.at[0], g_recv.at[0])
    gather_d = TensorGather(spot, cotangent, d_rows, rows, g_send.at[1], g_recv.at[1])
    keep(cotangent, d_rows.at[block_of(spot.tensor, rows)])
    spread.forward(1)
    gather1.pass_on()
    spread.forward(2)
    gather_d.pass_on()
    gather1.finish()
    keep(h1v, h1_all)
    spread.forward(6)
    spread.arrived(0)
    spread.arrived(1)
    for copy in locals_[:2]:
        copy.wait()
    load = pltpu.make_async_copy(wqkv, wqkv_v, local_sem.at[14])
    load.start()
    load.wait()

    def project(index, carry):
        where = block_of(index, rows)
        for part in range(3):
            lanes = slice(part * width, (part + 1) * width)
            value = jnp.dot(h1v[where, :], wqkv_v[:, lanes], preferred_element_type=F32) + sums[6:7, lanes]
            if part == 0:
                value = value * (width // heads) ** -0.5
            qkv_v[where, lanes] = value.astype(BF16)
        return carry

    lax.fori_loop(0, length // rows, project, 0)
    keep(qkv_v, qkv_all)
    spread.forward(3)
    size = width // heads
    limit = prefix[0]
    bench = 256

    for block in range(length // bench):
        reach = min(length, max((block + 1) * bench, PREFIX_TOP))
        span = slice(block * bench, (block + 1) * bench)

        def attend(head, carry, block=block, span=span, reach=reach):
            line = block * bench + lax.broadcasted_iota(jnp.int32, (bench, reach), 0)
            place = lax.broadcasted_iota(jnp.int32, (bench, reach), 1)
            seen = (place <= line) | (place < limit)
            q = qkv_v[span, block_of(head, size)]
            k = qkv_v[0:reach, pl.ds(pl.multiple_of(width + head * size, size), size)]
            v = qkv_v[0:reach, pl.ds(pl.multiple_of(2 * width + head * size, size), size)]
            scores = lax.dot_general(q, k, (((1,), (1,)), ((), ())), preferred_element_type=F32)
            scores = jnp.where(seen, scores, -1e30)
            top = jnp.max(scores, axis=-1, keepdims=True)
            expd = jnp.exp(scores - top)
            total = jnp.sum(expd, axis=-1, keepdims=True)
            probs = (expd * (1.0 / total)).astype(BF16)
            mixed_v[span, block_of(head, size)] = jnp.dot(probs, v, preferred_element_type=F32).astype(BF16)
            lse_v[head, span, :] = jnp.broadcast_to(top + jnp.log(total), (bench, 128))
            return carry

        lax.fori_loop(0, heads, attend, 0)
        if block == 2:
            spread.forward(2)
    keep(mixed_v, mixed_all)
    keep(lse_v, lse_all)
    spread.forward(1)
    spread.arrived(2)
    locals_[2].wait()
    load = pltpu.make_async_copy(wo, wo_v, local_sem.at[14])
    load.start()
    load.wait()

    def out_part(rank, index):
        return jnp.dot(mixed_v[block_of(rank, rows), :], wo_v[:, block_of(index, 512)], preferred_element_type=F32)

    def take_second(index, total):
        where = block_of(index, 512)
        second[:, where] = tokens[:, where].astype(F32) + total + sums[4:5, where]

    end = tensor_sum(
        spot, out_part, core_send, core_recv, x_send, x_recv, s_send.at[0], s_recv.at[0], take_second
    )
    end()

    def norm2(index, carry):
        where = block_of(index, strip)
        center, scale = normal_parts(second[where, :])
        h2v[pl.ds(pl.multiple_of(base + index * strip, strip), strip), :] = (
            center * scale * sums[2:3, :] + sums[3:4, :]
        ).astype(BF16)
        return carry

    lax.fori_loop(0, rows // strip, norm2, 0)
    gather2 = TensorGather(spot, h2v.at[block_of(spot.tensor, rows)], h2v, rows, g_send.at[2], g_recv.at[2])
    gather2.pass_on()
    spread.forward(3)
    gather2.finish()
    gather_d.finish()
    keep(h2v, h2_all)
    for part in range(2):
        spread.arrived(3 + part)
        locals_[3 + part].wait()
        lanes_of = pl.ds(part * tall, tall)
        load = pltpu.make_async_copy(w1.at[:, lanes_of], w1_v.at[:, lanes_of], local_sem.at[14])
        load.start()
        load.wait()

        def stored(block, lanes_of=lanes_of):
            slot = lax.rem(block, 2)
            return pltpu.make_async_copy(
                slope_v.at[slot], slope_all.at[block_of(block, rows), lanes_of], local_sem.at[15 + slot]
            )

        def lift_rows(block, carry, part=part, stored=stored):
            where_rows = block_of(block, rows)
            if part == 0:
                pl.when(block >= 2)(lambda: stored(block).wait())
            else:
                stored(block).wait()

            def lift(index, carry):
                where = block_of(part * (tall // 512) + index, 512)
                u = jnp.dot(h2v[where_rows, :], w1_v[:, where], preferred_element_type=F32) + sums[7:8, where]
                below = 0.5 * (1.0 + lax.erf(u * 0.7071067811865476))
                gated_v[where_rows, where] = (u * below).astype(BF16)
                slope_v[lax.rem(block, 2), :, block_of(index, 512)] = (
                    below + u * (0.3989422804014327 * jnp.exp(-0.5 * u * u))
                )
                return carry

            lax.fori_loop(0, tall // 512, lift, 0)
            stored(block).start()
            return carry

        lax.fori_loop(0, length // rows, lift_rows, 0)
        if part == 0:
            spread.forward(3)
    keep(gated_v, gated_all)
    spread.arrived(6)
    spread.arrived(5)
    spread.finish()
    for copy in small_copies:
        copy.wait_send()
    for copy in locals_[5:] + [stored(jnp.int32(block)) for block in range(2)]:
        copy.wait()


def forward_call(heads, count, prefix, tokens, cotangent, small, qkv_shard, out_shard, up_shard, down_shard):
    rows, features = tokens.shape
    length = rows * 4
    depth, triple = qkv_shard.shape
    width = out_shard.shape[0]
    hidden = up_shard.shape[1]
    outer, inner = split_of(count)
    shape = jax.ShapeDtypeStruct
    hbm = pl.BlockSpec(memory_space=pl.ANY)
    vmem = pl.BlockSpec(memory_space=pltpu.VMEM)
    dma = pltpu.SemaphoreType.DMA
    pieces = 7
    return pl.pallas_call(
        functools.partial(forward_kernel, heads, count),
        out_shape=[
            shape((features, triple), BF16),
            shape((width, features), BF16),
            shape((features, hidden), BF16),
            shape((hidden, features), BF16),
            shape((length, features), BF16),
            shape((length, features), BF16),
            shape((length, triple), BF16),
            shape((length, width), BF16),
            shape((heads, length, 128), F32),
            shape((rows, features), F32),
            shape((length, features), BF16),
            shape((length, hidden), BF16),
            shape((length, hidden), F32),
            shape((8, features), F32),
        ],
        in_specs=[pl.BlockSpec(memory_space=pltpu.SMEM)] + [vmem] * 7,
        out_specs=[hbm] * 9 + [vmem] + [hbm] * 3 + [vmem],
        scratch_shapes=[
            pltpu.VMEM((count, 40, 128), F32),
            pltpu.VMEM((length, features), BF16),
            pltpu.VMEM((features, triple), BF16),
            pltpu.VMEM((length, triple), BF16),
            pltpu.VMEM((length, width), BF16),
            pltpu.VMEM((heads, length, 128), F32),
            pltpu.VMEM((width, features), BF16),
            pltpu.VMEM((2, rows, features), BF16),
            pltpu.VMEM((2, rows, features), BF16),
            pltpu.VMEM((rows, features), BF16),
            pltpu.VMEM((rows, features), BF16),
            pltpu.VMEM((length, features), BF16),
            pltpu.VMEM((features, hidden), BF16),
            pltpu.VMEM((length, hidden), BF16),
            pltpu.VMEM((2, rows, hidden // 2), F32),
            dma((count,)),
            dma((count,)),
            dma((pieces + 1, outer)),
            dma((pieces + 1, outer)),
            dma((pieces, outer)),
            dma((pieces, outer)),
            dma((3, 3)),
            dma((3, 3)),
            dma((1, 3)),
            dma((1, 3)),
            dma((17,)),
        ],
        compiler_params=pltpu.CompilerParams(
            collective_id=0, has_side_effects=True, vmem_limit_bytes=VMEM_BYTES
        ),
    )(prefix, tokens, cotangent, small, qkv_shard, out_shard, up_shard, down_shard)
class Reduce:
    def __init__(self, spot, left, right, lanes, landing, target, shared, index, last):
        self.spot, self.left, self.right, self.lanes = spot, left, right, lanes
        self.landing, self.target, self.shared, self.index, self.last = landing, target, shared, index, last
        self.width = lanes.stop - lanes.start
        self.share = target.shape[0]
        self.stepped = {}
        self.held = ()
        row = spot.row
        self.inner = (row == 1) | (row == 2)
        self.steps = (
            jnp.where(row == 0, 3, 1), jnp.where(self.inner, 3, 2), jnp.where(row == 0, 1, jnp.where(row == 3, 3, 2)), 0
        )

    def block(self, owner, take):
        turned = jnp.transpose(self.left[:, block_of(owner, self.share)])

        def body(index, carry):
            source = self.right[:, pl.ds(pl.multiple_of(self.lanes.start + index * 512, 512), 512)]
            take(block_of(index, 512), jnp.dot(turned, source, preferred_element_type=F32))
            return carry

        lax.fori_loop(0, self.width // 512, body, 0)

    def y_copy(self, step):
        shared = self.shared
        area = pl.ds(0, self.width)
        return remote(
            shared["y_out"].at[step, :, area], shared["y_in"].at[step, :, area], shared["y_send"].at[step],
            shared["y_recv"].at[step], self.spot.beside(1), self.spot.tensor,
        )

    def z_copy(self, place):
        shared, step = self.shared, self.steps[place]
        return remote(
            shared["z_out"].at[place, :, pl.ds(0, self.width)], self.landing.at[step - 1],
            shared["z_send"].at[place], shared["z_recv"].at[self.index, step], self.spot.across(step),
            self.spot.tensor,
        )

    def near_copy(self):
        shared, spot = self.shared, self.spot
        area = pl.ds(0, self.width)
        return remote(
            shared["z_out"].at[0, :, area], shared["near"].at[:, area], shared["z_send"].at[0], shared["near_recv"].at[0],
            jnp.where(spot.row == 0, 1, 2) * spot.inner + spot.column, spot.tensor,
        )

    def produce(self, place):
        shared, spot = self.shared, self.spot
        row = lax.rem(spot.row + self.steps[place], spot.outer)
        if place in shared["y_busy"]:
            shared["y_busy"].pop(place).wait_send()

        def take(where, value):
            shared["y_out"][place, :, where] = value.astype(BF16)

        self.block(spot.beside(1, row), take)
        if self.index > 0:
            pl.semaphore_wait(shared["credit"], 1)
        copy = self.y_copy(place)
        copy.start()
        shared["y_busy"][place] = copy

    def hold(self, places):
        self.held = places
        for place in places:

            def take(where, value, place=place):
                self.shared["z_out"][place, :, where] = value.astype(BF16)

            self.block(self.spot.across(self.steps[place]), take)

    def serve(self, place):
        shared, spot = self.shared, self.spot
        self.y_copy(place).wait_recv()
        if place in shared["z_busy"]:
            shared["z_busy"].pop(place).wait_send()
        y_in, z_out = shared["y_in"], shared["z_out"]
        if place in self.held:
            for start in range(0, self.width, 512):
                where = slice(start, start + 512)
                z_out[place, :, where] = (
                    z_out[place, :, where].astype(F32) + y_in[place, :, where].astype(F32)
                ).astype(BF16)
        else:

            def take(where, value):
                z_out[place, :, where] = (value + y_in[place, :, where].astype(F32)).astype(BF16)

            self.block(spot.across(self.steps[place]), take)
        if not self.last:
            pl.semaphore_signal(
                shared["credit"], inc=1, device_id=(spot.beside(1), spot.tensor), device_id_type=MESH
            )
        if place == 3:
            return
        if place == 0:

            @pl.when(jnp.logical_not(self.inner))
            def _():
                if self.index > 0:
                    pl.semaphore_wait(shared["near_free"], 1)
                self.near_copy().start()

            @pl.when(self.inner)
            def _():
                self.z_copy(0).start()

        else:
            if place == 2:

                @pl.when(self.inner)
                def _():
                    self.near_copy().wait_recv()
                    for start in range(0, self.width, 512):
                        where = slice(start, start + 512)
                        z_out[2, :, where] = (
                            z_out[2, :, where].astype(F32) + shared["near"][:, where].astype(F32)
                        ).astype(BF16)
                    if not self.last:
                        pl.semaphore_signal(
                            shared["near_free"], inc=1,
                            device_id=(jnp.where(spot.row == 1, 0, 3) * spot.inner + spot.column, spot.tensor),
                            device_id_type=MESH,
                        )

            self.z_copy(place).start()
        shared["z_busy"][place] = self.z_copy(place)

    def landed(self, step):
        shared = self.shared
        remote(
            shared["z_out"].at[0, :, pl.ds(0, self.width)], self.landing.at[step - 1], shared["z_send"].at[0],
            shared["z_recv"].at[self.index, step], self.spot.across(1), self.spot.tensor,
        ).wait_recv()

    def settle(self):
        shared, spot = self.shared, self.spot
        pl.when(spot.row != 0)(lambda: self.landed(1))
        self.landed(2)
        pl.when(spot.row != 3)(lambda: self.landed(3))
        chunks = self.width // 128

        def load(chunk):
            slot = lax.rem(chunk, 4)
            return pltpu.make_async_copy(
                self.landing.at[:, :, block_of(chunk, 128)], shared["z_stage"].at[slot], shared["stage_sem"].at[slot]
            )

        def store(chunk):
            slot = lax.rem(chunk, 4)
            return pltpu.make_async_copy(
                shared["o_stage"].at[slot], self.target.at[:, block_of(chunk, 128)], shared["stage_sem"].at[4 + slot]
            )

        def add(chunk, carry):
            slot = lax.rem(chunk, 4)
            load(chunk).wait()
            pl.when(chunk + 3 < chunks)(lambda: load(chunk + 3).start())
            pl.when(chunk >= 4)(lambda: store(chunk - 4).wait())
            total = shared["z_out"][3, :, block_of(chunk, 128)].astype(F32)
            for step in range(spot.outer - 1):
                part = shared["z_stage"][slot, step].astype(F32)
                if step != 1:
                    part = jnp.where(spot.row == (0 if step == 0 else 3), 0.0, part)
                total = total + part
            shared["o_stage"][slot] = total
            store(chunk).start()
            return carry

        for chunk in range(3):
            load(jnp.int32(chunk)).start()
        lax.fori_loop(0, chunks, add, 0)
        for chunk in range(chunks - 4, chunks):
            store(jnp.int32(chunk)).wait()


def row_dot(left, right):
    return lax.dot_general(left, right, (((1,), (1,)), ((), ())), preferred_element_type=F32)


def backward_kernel(
    heads,
    count,
    prefix,
    sums,
    tokens,
    cotangent,
    wqkv,
    wo,
    w1,
    w2,
    h1_all,
    d_rows,
    qkv_all,
    mixed_all,
    lse_v,
    second,
    h2_all,
    gated_all,
    slope_all,
    layer_out,
    input_grad,
    grad_down,
    grad_up,
    grad_out,
    grad_qkv,
    vector_sums,
    bias_sums,
    land_down,
    land_up,
    land_out,
    land_qkv,
    weight_v,
    buf1,
    buf2,
    buf3,
    buf4,
    buf5,
    buf6,
    near,
    core_send,
    core_recv,
    x_send,
    x_recv,
    y_in,
    y_out,
    z_out,
    z_stage,
    o_stage,
    spare,
    line,
    dk_sum,
    dv_sum,
    vectors,
    biases,
    vector_in,
    bias_in,
    part_sum,
    part_in,
    y_send,
    y_recv,
    z_send,
    z_recv,
    g_send,
    g_recv,
    s_send,
    s_recv,
    v_send,
    v_recv,
    b_send,
    b_recv,
    t_send,
    t_recv,
    stage_sem,
    load_sem,
    near_recv,
    credit,
    ready,
    near_free,
):
    spot = Spot(count)
    rows, features = line.shape
    length = buf1.shape[0]
    width = wo.shape[0]
    hidden = w1.shape[1]
    triple = 3 * width
    size = width // heads
    scale = size ** -0.5
    tail = slice(triple, triple + width)
    shared = {
        "y_in": y_in, "y_out": y_out, "z_out": z_out, "z_stage": z_stage, "o_stage": o_stage, "y_send": y_send,
        "y_recv": y_recv, "z_send": z_send, "z_recv": z_recv, "credit": credit, "stage_sem": stage_sem,
        "y_busy": {}, "z_busy": {}, "near": near, "near_recv": near_recv, "near_free": near_free,
    }
    down = Reduce(spot, buf1, buf2, slice(0, hidden), land_down, grad_down, shared, 0, False)
    up = Reduce(spot, buf4, buf3, slice(0, hidden), land_up, grad_up, shared, 1, False)
    qkv = Reduce(spot, buf6, buf5, slice(0, triple), land_qkv, grad_qkv, shared, 2, False)
    out = Reduce(spot, buf1, buf2, tail, land_out, grad_out, shared, 3, True)

    def fetch(source, target, slot):
        copy = pltpu.make_async_copy(source, target, load_sem.at[slot])
        copy.start()
        return copy

    load_a = fetch(d_rows, buf1, 0)
    load_b = fetch(gated_all, buf2, 1)
    load_w = fetch(w2, weight_v, 2)
    slopes = [fetch(slope_all.at[pl.ds(part * rows, rows)], (spare, input_grad)[part % 2], 3 + part % 2) for part in range(2)]
    load_h = fetch(h2_all, buf4, 5)
    load_c = fetch(cotangent, line, 6)
    spot.meet(True)
    vectors[...] = jnp.zeros_like(vectors)
    biases[...] = jnp.zeros_like(biases)
    load_a.wait()
    load_b.wait()
    for place in range(spot.outer):
        down.produce(place)
    load_w.wait()
    tensor = (core_send, core_recv, x_send, x_recv)

    def down_part(rank, index):
        return jnp.dot(buf2[block_of(rank, rows), :], weight_v[:, block_of(index, 512)], preferred_element_type=F32)

    def take_out(index, total):
        where = block_of(index, 512)
        buf6[0:rows, where] = (spare[:, where] + total + sums[5:6, where]).astype(BF16)

    end = tensor_sum(
        spot, down_part, *tensor, s_send, s_recv, take_out, between=lambda: down.serve(0)
    )
    for part in range(length // rows):
        held = (spare, input_grad)[part % 2]
        slopes[part].wait()

        def lower(index, carry, part=part, held=held):
            where = block_of(index, 512)
            span = slice(part * rows, (part + 1) * rows)
            du = row_dot(buf1[span, :], weight_v[where, :]) * held[:, where]
            biases[pl.ds(index, 1), :] += jnp.sum(du, axis=0, keepdims=True)
            buf3[span, where] = du.astype(BF16)
            return carry

        lax.fori_loop(0, hidden // 512, lower, 0)
        if part + 2 < length // rows:
            slopes.append(fetch(slope_all.at[pl.ds((part + 2) * rows, rows)], held, 3 + part % 2))
        if part == 1:
            down.serve(1)
    load_s = fetch(second, spare, 3)
    load_s.wait()
    end()
    spot.release(ready)
    store_l = fetch(buf6.at[pl.ds(0, rows)], layer_out, 7)
    load_w = fetch(w1, weight_v, 2)
    load_h.wait()
    down.serve(2)
    down.hold((3,))
    load_q = fetch(qkv_all, buf2.at[:, pl.ds(0, triple)], 0)
    load_m = fetch(mixed_all, buf2.at[:, pl.ds(triple, width)], 1)
    up.produce(0)
    up.produce(1)
    up.produce(2)
    load_w.wait()

    def h2_part(rank, index):
        return row_dot(buf3[block_of(rank, rows), :], weight_v[block_of(index, 512), :])

    def take_h2(index, total):
        input_grad[:, block_of(index, 512)] = total

    pl.semaphore_wait(ready, 2)
    end = tensor_sum(spot, h2_part, *tensor, s_send, s_recv, take_h2)
    down.serve(3)
    up.produce(3)
    up.serve(0)
    end()
    spot.release(ready)
    store_l.wait()
    load_n = fetch(h1_all, buf6, 7)
    load_o = fetch(wo, weight_v.at[pl.ds(0, width)], 2)
    load_c.wait()
    strip = 32
    base = spot.tensor * rows

    def norm_back(rows_of, gain, grads, keep, first):
        center, inverse = normal_parts(rows_of)
        normal = center * inverse
        vectors[first : first + 1, :] += jnp.sum(grads * normal, axis=0, keepdims=True)
        vectors[first + 1 : first + 2, :] += jnp.sum(grads, axis=0, keepdims=True)
        scaled = grads * gain
        mean = jnp.mean(scaled, axis=-1, keepdims=True)
        slope = jnp.mean(scaled * normal, axis=-1, keepdims=True)
        return keep + inverse * (scaled - mean - normal * slope)

    def back2(index, carry):
        where = block_of(index, strip)
        dy = line[where, :].astype(F32)
        dx = norm_back(spare[where, :], sums[2:3, :], input_grad[where, :], dy, 2)
        vectors[4:5, :] += jnp.sum(dx, axis=0, keepdims=True)
        vectors[5:6, :] += jnp.sum(dy, axis=0, keepdims=True)
        input_grad[where, :] = dx
        buf1[pl.ds(pl.multiple_of(base + index * strip, strip), strip), :] = dx.astype(BF16)
        return carry

    lax.fori_loop(0, rows // strip, back2, 0)
    gather = TensorGather(spot, buf1.at[block_of(spot.tensor, rows)], buf1, rows, g_send, g_recv)
    load_t = fetch(tokens, line, 6)
    up.serve(1)
    down.settle()
    gather.pass_on()
    load_o.wait()
    gather.finish()
    load_q.wait()
    load_m.wait()

    def mix_back(index, carry):
        where = block_of(index, rows)
        buf5[where, tail] = row_dot(buf1[where, :], weight_v[0:width, :]).astype(BF16)
        return carry

    lax.fori_loop(0, length // rows, mix_back, 0)
    load_w = fetch(wqkv, weight_v.at[:, pl.ds(0, triple)], 2)
    limit = prefix[0]
    bench = 256

    def attend(head, carry):
        q_at = block_of(head, size)
        k_at = pl.ds(pl.multiple_of(width + head * size, size), size)
        v_at = pl.ds(pl.multiple_of(2 * width + head * size, size), size)
        o_at = pl.ds(pl.multiple_of(triple + head * size, size), size)
        dk_sum[...] = jnp.zeros_like(dk_sum)
        dv_sum[...] = jnp.zeros_like(dv_sum)
        for block in range(length // bench):
            reach = min(length, max((block + 1) * bench, PREFIX_TOP))
            span = slice(block * bench, (block + 1) * bench)
            row_of = block * bench + lax.broadcasted_iota(jnp.int32, (bench, reach), 0)
            place = lax.broadcasted_iota(jnp.int32, (bench, reach), 1)
            seen = (place <= row_of) | (place < limit)
            q = buf2[span, q_at]
            k = buf2[0:reach, k_at]
            v = buf2[0:reach, v_at]
            do = buf5[span, o_at]
            scores = jnp.where(seen, row_dot(q, k), -1e30)
            probs = jnp.exp(scores - lse_v[head, span, 0:1])
            d_probs = row_dot(do, v)
            inner = jnp.sum(probs * d_probs, axis=-1, keepdims=True)
            d_scores = (probs * (d_probs - inner)).astype(BF16)
            flip = (((0,), (0,)), ((), ()))
            dv_sum[0:reach, :] += lax.dot_general(probs.astype(BF16), do, flip, preferred_element_type=F32)
            dk_sum[0:reach, :] += lax.dot_general(d_scores, q, flip, preferred_element_type=F32)
            dq = jnp.dot(d_scores, k, preferred_element_type=F32) * scale
            biases[4:5, q_at] += jnp.sum(dq, axis=0, keepdims=True)
            buf5[span, q_at] = dq.astype(BF16)
        buf5[:, k_at] = dk_sum[...].astype(BF16)
        buf5[:, v_at] = dv_sum[...].astype(BF16)
        biases[5:6, q_at] += jnp.sum(dv_sum[...], axis=0, keepdims=True)
        return carry

    lax.fori_loop(0, heads, attend, 0)
    load_n.wait()
    qkv.produce(0)
    qkv.produce(1)
    up.serve(2)
    qkv.produce(2)
    load_w.wait()

    def h1_part(rank, index):
        return row_dot(buf5[block_of(rank, rows), 0:triple], weight_v[block_of(index, 512), 0:triple])

    def take_h1(index, total):
        spare[:, block_of(index, 512)] = total

    pl.semaphore_wait(ready, 2)
    end = tensor_sum(spot, h1_part, *tensor, s_send, s_recv, take_h1)
    up.serve(3)
    qkv.produce(3)
    qkv.serve(0)
    out.produce(0)
    end()
    load_t.wait()

    def back1(index, carry):
        where = block_of(index, strip)
        dx = norm_back(line[where, :].astype(F32), sums[0:1, :], spare[where, :], input_grad[where, :], 0)
        input_grad[where, :] = dx
        return carry

    lax.fori_loop(0, rows // strip, back1, 0)
    share = grad_up.shape[0]
    vector_copies, bias_copies = [], []
    for step in range(1, count):
        peer = lax.rem(spot.dp + step, count)
        vector_copies.append(remote(
            vectors.at[:, block_of(peer, share)], vector_in.at[spot.dp], v_send.at[step], v_recv.at[step], peer,
            spot.tensor,
        ))
        bias_copies.append(remote(biases, bias_in.at[spot.dp], b_send.at[step], b_recv.at[step], peer, spot.tensor))
    for copy in vector_copies + bias_copies:
        copy.start()
    vector_in[spot.dp] = vectors[:, block_of(spot.dp, share)]
    bias_in[spot.dp] = biases[...]
    up.settle()
    qkv.serve(1)
    out.produce(1)
    for copy in vector_copies + bias_copies:
        copy.wait_recv()
    total, bias_total = vector_in[0], bias_in[0]
    for index in range(1, count):
        total = total + vector_in[index]
        bias_total = bias_total + bias_in[index]
    part_sum[...] = total
    bias_sums[...] = bias_total
    part_copies = [
        remote(part_sum, part_in.at[spot.tensor], t_send.at[slot], t_recv.at[slot], spot.dp, peer)
        for slot, peer in enumerate((spot.x_peer, spot.core_peer, spot.far_peer))
    ]
    for copy in part_copies:
        copy.start()
    part_in[spot.tensor] = part_sum[...]
    qkv.serve(2)
    out.produce(2)
    for copy in part_copies:
        copy.wait_recv()
    vector_sums[...] = part_in[0] + part_in[1] + part_in[2] + part_in[3]
    qkv.serve(3)
    out.produce(3)
    out.serve(0)
    out.serve(1)
    out.serve(2)
    for copy in vector_copies + bias_copies + part_copies:
        copy.wait_send()
    qkv.settle()
    out.serve(3)
    out.settle()
    for copy in list(shared["y_busy"].values()) + list(shared["z_busy"].values()):
        copy.wait_send()


def backward_call(heads, count, prefix, sums, tokens, cotangent, weights, saved):
    rows, features = tokens.shape
    length = rows * 4
    share = features // count
    wqkv, wo, w1, w2 = weights
    width, hidden, triple = wo.shape[0], w1.shape[1], wqkv.shape[1]
    outer, inner = split_of(count)
    shape = jax.ShapeDtypeStruct
    hbm = pl.BlockSpec(memory_space=pl.ANY)
    vmem = pl.BlockSpec(memory_space=pltpu.VMEM)
    dma = pltpu.SemaphoreType.DMA
    regular = pltpu.SemaphoreType.REGULAR
    wide = (length, features)
    return pl.pallas_call(
        functools.partial(backward_kernel, heads, count),
        out_shape=[
            shape((rows, features), BF16),
            shape((rows, features), F32),
            shape((share, hidden), F32),
            shape((share, hidden), F32),
            shape((share, width), F32),
            shape((share, triple), F32),
            shape((8, share), F32),
            shape((8, 512), F32),
            shape((outer - 1, share, hidden), BF16),
            shape((outer - 1, share, hidden), BF16),
            shape((outer - 1, share, width), BF16),
            shape((outer - 1, share, triple), BF16),
        ],
        in_specs=[pl.BlockSpec(memory_space=pltpu.SMEM), vmem] + [hbm] * 10 + [vmem] + [hbm] * 4,
        out_specs=[hbm, vmem] + [hbm] * 4 + [vmem] * 2 + [hbm] * 4,
        scratch_shapes=[
            pltpu.VMEM((hidden, features), BF16),
            pltpu.VMEM(wide, BF16),
            pltpu.VMEM(wide, BF16),
            pltpu.VMEM(wide, BF16),
            pltpu.VMEM(wide, BF16),
            pltpu.VMEM(wide, BF16),
            pltpu.VMEM(wide, BF16),
            pltpu.VMEM((share, hidden), BF16),
            pltpu.VMEM((2, rows, features), BF16),
            pltpu.VMEM((2, rows, features), BF16),
            pltpu.VMEM((rows, features), BF16),
            pltpu.VMEM((rows, features), BF16),
            pltpu.VMEM((outer, share, hidden), BF16),
            pltpu.VMEM((outer, share, hidden), BF16),
            pltpu.VMEM((outer, share, hidden), BF16),
            pltpu.VMEM((4, outer - 1, share, 128), BF16),
            pltpu.VMEM((4, share, 128), F32),
            pltpu.VMEM((rows, features), F32),
            pltpu.VMEM((rows, features), BF16),
            pltpu.VMEM((length, width // heads), F32),
            pltpu.VMEM((length, width // heads), F32),
            pltpu.VMEM((8, features), F32),
            pltpu.VMEM((8, 512), F32),
            pltpu.VMEM((count, 8, share), F32),
            pltpu.VMEM((count, 8, 512), F32),
            pltpu.VMEM((8, share), F32),
            pltpu.VMEM((4, 8, share), F32),
            dma((outer,)),
            dma((outer,)),
            dma((outer,)),
            dma((4, outer)),
            dma((3,)),
            dma((3,)),
            dma((3,)),
            dma((3,)),
            dma((count,)),
            dma((count,)),
            dma((count,)),
            dma((count,)),
            dma((3,)),
            dma((3,)),
            dma((8,)),
            dma((8,)),
            dma((1,)),
            regular,
            regular,
            regular,
        ],
        compiler_params=pltpu.CompilerParams(
            collective_id=1, has_side_effects=True, vmem_limit_bytes=VMEM_BYTES
        ),
    )(prefix, sums, tokens, cotangent, wqkv, wo, w1, w2, *saved)


def pack_small(biases, vectors):
    devices = lax.axis_size("dp")
    parts = jnp.concatenate(biases, axis=0)
    lane = lax.broadcasted_iota(jnp.int32, (parts.shape[0], parts.shape[1] * devices), 1)
    wide = jnp.where(lane // parts.shape[1] == lax.axis_index("dp"), jnp.tile(parts, (1, devices)), 0)
    halves = jnp.pad(jnp.stack(vectors), ((0, 2), (0, 0)))
    return jnp.concatenate([wide, halves[:, :128], halves[:, 128:]], axis=0).astype(F32)


def layer_norm(rows, gain, shift):
    center = rows - jnp.mean(rows, axis=-1, keepdims=True)
    spread = jnp.mean(center * center, axis=-1, keepdims=True)
    return center * lax.rsqrt(spread + 1e-05) * gain + shift


def gelu_exact(values):
    return jax.nn.gelu(values, approximate=False)


def head_major(matrix, heads):
    return matrix.reshape(matrix.shape[0], heads, -1).transpose(1, 0, 2)


def row_major(stacked):
    return stacked.transpose(1, 0, 2).reshape(stacked.shape[1], -1)


def masked_scores(q_block, keys, start, prefix_len):
    scores = jnp.einsum("hqd,hkd->hqk", q_block, keys, preferred_element_type=jnp.float32)
    rows = start + lax.broadcasted_iota(jnp.int32, scores.shape[1:], 0)
    cols = lax.broadcasted_iota(jnp.int32, scores.shape[1:], 1)
    seen = (cols <= rows) | (cols < prefix_len)
    return jnp.where(seen[None], scores, -1e30)


def to_blocks(stacked, count):
    heads, length = (stacked.shape[0], stacked.shape[1])
    return stacked.reshape((heads, count, length // count) + stacked.shape[2:]).swapaxes(0, 1)


def from_blocks(blocked):
    count, heads, block = (blocked.shape[0], blocked.shape[1], blocked.shape[2])
    return blocked.swapaxes(0, 1).reshape((heads, count * block) + blocked.shape[3:])


def contract_rows(left, right):
    return jnp.einsum("ld,le->de", left, right, preferred_element_type=jnp.float32)


def times_transpose(left, right):
    return jnp.einsum("le,de->ld", left, right, preferred_element_type=jnp.float32)


def plain(
    tokens,
    prefix,
    query_weight,
    key_weight,
    value_weight,
    out_weight,
    query_bias,
    value_bias,
    up_weight,
    down_weight,
    up_bias,
    norm1_gain,
    norm1_bias,
    norm2_gain,
    norm2_bias,
    out_bias,
    down_bias,
    cotangent,
):
    f32 = jnp.float32
    bf16 = jnp.bfloat16
    devices = lax.axis_size("dp")
    small = (query_bias, value_bias, up_bias, norm1_gain, norm1_bias, norm2_gain, norm2_bias, out_bias, down_bias)
    packed = jnp.concatenate([part.reshape(-1) for part in small])
    packed = lax.all_gather(packed, "dp", axis=0, tiled=False)
    pieces = []
    offset = 0
    for part in small:
        piece = packed[:, offset : offset + part.size].reshape((devices,) + part.shape)
        offset += part.size
        pieces.append(jnp.moveaxis(piece, 0, -2).reshape(part.shape[:-1] + (-1,)))
    bq, bv, b1, g1, n1, g2, n2, bo, b2 = pieces
    wq, wk, wv, wo = (
        lax.all_gather(query_weight, "dp", axis=0, tiled=True),
        lax.all_gather(key_weight, "dp", axis=0, tiled=True),
        lax.all_gather(value_weight, "dp", axis=0, tiled=True),
        lax.all_gather(out_weight, "dp", axis=1, tiled=True),
    )
    w1, w2 = (
        lax.all_gather(up_weight, "dp", axis=0, tiled=True),
        lax.all_gather(down_weight, "dp", axis=1, tiled=True),
    )
    g1f, n1f, g2f, n2f = (g1.astype(f32), n1.astype(f32), g2.astype(f32), n2.astype(f32))
    bof, b2f = (bo.astype(f32), b2.astype(f32))
    heads = bq.shape[0]
    head_size = bq.shape[1]
    scale = head_size ** (-0.5)
    prefix_len = prefix[0]
    xf = tokens.astype(f32)
    h1 = layer_norm(xf, g1f, n1f).astype(bf16)
    rows1 = lax.all_gather(h1, "tensor", axis=0, tiled=True)
    length = rows1.shape[0]
    block = min(512, length)
    count = length // block
    query = (
        (jnp.dot(rows1, wq, preferred_element_type=f32) + bq.astype(f32).reshape(-1)) * scale
    ).astype(bf16)
    keyed = jnp.dot(rows1, wk, preferred_element_type=f32).astype(bf16)
    valued = (jnp.dot(rows1, wv, preferred_element_type=f32) + bv.astype(f32).reshape(-1)).astype(
        bf16
    )
    q_heads = head_major(query, heads)
    k_heads = head_major(keyed, heads)
    v_heads = head_major(valued, heads)
    q_blocks = to_blocks(q_heads, count)
    starts = jnp.arange(count, dtype=jnp.int32) * block

    def forward_block(item):
        q_block, start = item
        scores = masked_scores(q_block, k_heads, start, prefix_len)
        top = jnp.max(scores, axis=-1, keepdims=True)
        expd = jnp.exp(scores - top)
        total = jnp.sum(expd, axis=-1, keepdims=True)
        probs = (expd / total).astype(bf16)
        outv = jnp.einsum("hqk,hkd->hqd", probs, v_heads, preferred_element_type=f32)
        return (outv.astype(bf16), (top + jnp.log(total))[..., 0])

    o_blocks, lse_blocks = lax.map(forward_block, (q_blocks, starts))
    mixed = row_major(from_blocks(o_blocks))
    attn_part = jnp.dot(mixed, wo, preferred_element_type=f32)
    attn_total = lax.psum_scatter(attn_part.astype(bf16), "tensor", scatter_dimension=0, tiled=True).astype(f32)
    second = xf + attn_total + bof
    h2 = layer_norm(second, g2f, n2f).astype(bf16)
    rows2 = lax.all_gather(h2, "tensor", axis=0, tiled=True)
    hidden = jnp.dot(rows2, w1, preferred_element_type=f32) + b1.astype(f32).reshape(-1)
    gated = gelu_exact(hidden).astype(bf16)
    mlp_part = jnp.dot(gated, w2, preferred_element_type=f32)
    mlp_total = lax.psum_scatter(
        mlp_part.astype(jnp.bfloat16), "tensor", scatter_dimension=0, tiled=True
    ).astype(jnp.float32)
    layer_out = (second + mlp_total + b2f).astype(bf16)
    d_out = cotangent.astype(f32)
    g_b2 = jnp.sum(d_out, axis=0)
    d_rows = lax.all_gather(cotangent, "tensor", axis=0, tiled=True)
    d_gated = times_transpose(d_rows, w2)
    d_hidden = jax.vjp(gelu_exact, hidden)[1](d_gated)[0]
    g_b1 = jnp.sum(d_hidden, axis=0).reshape(b1.shape)
    d_hidden_low = d_hidden.astype(bf16)
    d_h2_part = times_transpose(d_hidden_low, w1)
    g_w2 = contract_rows(gated, d_rows)
    g_w1 = contract_rows(rows2, d_hidden_low)
    d_h2 = lax.psum_scatter(d_h2_part.astype(bf16), "tensor", scatter_dimension=0, tiled=True).astype(f32)
    norm2_back = jax.vjp(layer_norm, second, g2f, n2f)[1]
    d_second_ln, g_g2, g_n2 = norm2_back(d_h2)
    d_second = d_out + d_second_ln
    g_bo = jnp.sum(d_second, axis=0)
    d_second_low = d_second.astype(bf16)
    back_rows = lax.all_gather(d_second_low, "tensor", axis=0, tiled=True)
    g_wo = contract_rows(mixed, back_rows)
    d_mixed = times_transpose(back_rows, wo).astype(bf16)
    do_blocks = to_blocks(head_major(d_mixed, heads), count)

    def backward_block(carry, item):
        d_keys, d_vals = carry
        q_block, do_block, lse_block, start = item
        scores = masked_scores(q_block, k_heads, start, prefix_len)
        probs = jnp.exp(scores - lse_block[..., None])
        d_probs = jnp.einsum("hqd,hkd->hqk", do_block, v_heads, preferred_element_type=f32)
        d_vals = d_vals + jnp.einsum(
            "hqk,hqd->hkd", probs.astype(bf16), do_block, preferred_element_type=f32
        )
        inner = jnp.sum(probs * d_probs, axis=-1, keepdims=True)
        d_scores = (probs * (d_probs - inner)).astype(bf16)
        d_query = jnp.einsum("hqk,hkd->hqd", d_scores, k_heads, preferred_element_type=f32)
        d_keys = d_keys + jnp.einsum("hqk,hqd->hkd", d_scores, q_block, preferred_element_type=f32)
        return ((d_keys, d_vals), d_query)

    empty = jnp.zeros(k_heads.shape, f32)
    (d_keys, d_vals), dq_blocks = lax.scan(
        backward_block, (empty, empty), (q_blocks, do_blocks, lse_blocks, starts)
    )
    d_query = row_major(from_blocks(dq_blocks)) * scale
    d_keys = row_major(d_keys)
    d_vals = row_major(d_vals)
    g_bq = jnp.sum(d_query, axis=0).reshape(bq.shape)
    g_bv = jnp.sum(d_vals, axis=0).reshape(bv.shape)
    dq_low, dk_low, dv_low = (d_query.astype(bf16), d_keys.astype(bf16), d_vals.astype(bf16))
    g_wq = contract_rows(rows1, dq_low)
    g_wk = contract_rows(rows1, dk_low)
    g_wv = contract_rows(rows1, dv_low)
    d_h1_part = (
        times_transpose(dq_low, wq) + times_transpose(dk_low, wk) + times_transpose(dv_low, wv)
    )
    d_h1 = lax.psum_scatter(d_h1_part.astype(bf16), "tensor", scatter_dimension=0, tiled=True).astype(f32)
    norm1_back = jax.vjp(layer_norm, xf, g1f, n1f)[1]
    d_input_ln, g_g1, g_n1 = norm1_back(d_h1)
    input_grad = d_second + d_input_ln
    def scatter(part, dim):
        return lax.psum_scatter(part.astype(bf16), "dp", scatter_dimension=dim, tiled=True).astype(f32)

    s_w2, s_w1, s_wo = scatter(g_w2, 1), scatter(g_w1, 0), scatter(g_wo, 1)
    s_wq, s_wk, s_wv = scatter(g_wq, 0), scatter(g_wk, 0), scatter(g_wv, 0)

    def by_device(part):
        return jnp.moveaxis(part.reshape(part.shape[:-1] + (devices, -1)), -2, 0).reshape(devices, -1)

    rows = [by_device(part) for part in (g_bq, g_bv, g_b1, g_g1, g_n1, g_g2, g_n2, g_bo, g_b2)]
    total = lax.psum_scatter(jnp.concatenate(rows, axis=1), "dp", scatter_dimension=0, tiled=True)[0]
    offset = 0
    outs = []
    for part in (query_bias, value_bias, up_bias):
        outs.append(total[offset : offset + part.size].reshape(part.shape))
        offset += part.size
    s_bq, s_bv, s_b1 = outs
    vectors = lax.psum_scatter(
        total[offset:].reshape(6, lax.axis_size("tensor"), -1), "tensor", scatter_dimension=1, tiled=True
    ).reshape(6, -1)
    s_g1, s_n1, s_g2, s_n2, s_bo, s_b2 = (vectors[index] for index in range(6))
    return (
        layer_out,
        input_grad,
        s_wq,
        s_wk,
        s_wv,
        s_wo,
        s_bq,
        s_bv,
        s_w1,
        s_w2,
        s_b1,
        s_g1,
        s_n1,
        s_g2,
        s_n2,
        s_bo,
        s_b2,
    )


def fast(
    tokens,
    prefix,
    query_weight,
    key_weight,
    value_weight,
    out_weight,
    query_bias,
    value_bias,
    up_weight,
    down_weight,
    up_bias,
    norm1_gain,
    norm1_bias,
    norm2_gain,
    norm2_bias,
    out_bias,
    down_bias,
    cotangent,
):
    devices = lax.axis_size("dp")
    me = lax.axis_index("dp")
    heads = query_bias.shape[0]
    small = pack_small(
        (query_bias, value_bias, up_bias), (norm1_gain, norm1_bias, norm2_gain, norm2_bias, out_bias, down_bias)
    )
    results = forward_call(
        heads, devices, prefix, tokens, cotangent, small,
        jnp.concatenate([query_weight, key_weight, value_weight], axis=1), out_weight, up_weight, down_weight,
    )
    layer_out, input_grad, g_w2, g_w1, g_wo, g_qkv, vectors, biases, *_ = backward_call(
        heads, devices, prefix, results[-1], tokens, cotangent, results[:4], results[4:-1]
    )
    g_wq, g_wk, g_wv = jnp.split(g_qkv, 3, axis=1)
    vectors = vectors.reshape(8, lax.axis_size("tensor"), -1)
    vectors = lax.dynamic_index_in_dim(vectors, lax.axis_index("tensor"), axis=1, keepdims=False)

    def own(flat, part):
        whole = flat.reshape(part.shape[0], -1)
        return lax.dynamic_slice_in_dim(whole, me * part.shape[1], part.shape[1], axis=1)

    width = out_weight.shape[0]
    up_size = up_bias.size * devices
    g_b1 = own(biases[: up_size // 512].reshape(-1), up_bias)
    g_bq = own(biases[4, :width], query_bias)
    g_bv = own(biases[5, :width], value_bias)
    return (
        layer_out, input_grad, g_wq, g_wk, g_wv, g_wo.T, g_bq, g_bv, g_w1, g_w2.T, g_b1,
        vectors[0], vectors[1], vectors[2], vectors[3], vectors[4], vectors[5],
    )


def local(*args):
    tokens, query_weight, up_weight = args[0], args[2], args[8]
    devices = lax.axis_size("dp")
    features = tokens.shape[1]
    share = features // devices
    fits = (
        lax.axis_size("tensor") == 4
        and devices == 8
        and share % 128 == 0
        and tokens.shape[0] == 256
        and query_weight.shape[1] == 512
        and args[6].shape[0] == 4
        and features == 2048
        and up_weight.shape[1] == 2048
    )
    return fast(*args) if fits else plain(*args)


def solution(mesh):
    in_specs = (
        P(("dp", "tensor"), None),
        P("dp"),
        P("dp", "tensor"),
        P("dp", "tensor"),
        P("dp", "tensor"),
        P("tensor", "dp"),
        P("tensor", "dp"),
        P("tensor", "dp"),
        P("dp", "tensor"),
        P("tensor", "dp"),
        P("tensor", "dp"),
        P("dp"),
        P("dp"),
        P("dp"),
        P("dp"),
        P("dp"),
        P("dp"),
        P(("dp", "tensor"), None),
    )
    out_specs = (
        P(("dp", "tensor"), None),
        P(("dp", "tensor"), None),
        P("dp", "tensor"),
        P("dp", "tensor"),
        P("dp", "tensor"),
        P("tensor", "dp"),
        P("tensor", "dp"),
        P("tensor", "dp"),
        P("dp", "tensor"),
        P("tensor", "dp"),
        P("tensor", "dp"),
        P(("dp", "tensor")),
        P(("dp", "tensor")),
        P(("dp", "tensor")),
        P(("dp", "tensor")),
        P(("dp", "tensor")),
        P(("dp", "tensor")),
    )
    return jax.shard_map(local, mesh=mesh, in_specs=in_specs, out_specs=out_specs, check_vma=False)
```
